128 devices in a mesh: rows: 32 (over z, y, x_hi), feat: 4 (over x_lo, core).
Axes of the slice: x: 4 (x_hi: 2, x_lo: 2; x = x_hi * 2 + x_lo), y: 4, z: 4, core: 2. Of those that a mesh axis runs over, the one named last changes fastest.
Arguments:
- slab: bfloat16 [98304, 4096], P('rows', 'feat'), may hold values from -12 to 12
- basis: float32 [4096, 256], P('feat'), may hold values from -1 to 1
- cluster_ids: int32 [98304, 1], P('rows'), may hold values from 0 to 63; in each aligned block of 3072 rows (0 to 3071, 3072 to 6143, ...) at most 128 rows name the same one
- kept: int32 [1], replicated, may hold values from 128 to 256
Outputs:
- packed: bfloat16 [64, 4096, 256], P('rows', None, 'feat')
The draws below stay inside these ranges and needn't reach their ends.
Inputs may be any that keep to these rules, and one draw needn't show every extreme that they name: `cluster_ids`: within the rows of one device (aligned blocks of 3072 rows), no cluster is named by more than 128 rows, a bound that some block reaches.
All inputs are finite; a program needn't handle non-finite values.
Results may differ from the reference program's by a relative error of at most 0.0065.
Values may be sent and summed in bfloat16 or wider, within the bound.
A program may use at most 64 MiB of HBM per device.

```python
import math
import jax
import jax.numpy as jnp
import numpy as np
from jax import lax

D = 4096
K = 256
ITERS = 2
CAP = 128
CLUSTERS = 64
R_DEV = 3072
NROWS = 98304
N_ROWS = 32


def draw_slab(key, part):
    base_key = jax.random.fold_in(key, 11)
    scale_key = jax.random.fold_in(key, 12)
    values = jax.random.truncated_normal(base_key, -4.0, 4.0, (NROWS, D), jnp.float32)
    scales = jnp.exp(jax.random.uniform(scale_key, (D,), jnp.float32, 0.0, math.log(3.0)))
    return (values * scales[None, :]).astype(jnp.bfloat16)


def draw_basis(key, part):
    base_key = jax.random.fold_in(key, 21)
    values = jax.random.truncated_normal(base_key, -4.0, 4.0, (D, K), jnp.float32)
    return values / math.sqrt(D)


def deal_out(rng, own, number, rows, number_of, top, most, slope):
    sequence = jax.random.permutation(rng, number_of)
    crowded, ordinary = load_shares(number_of, rows * top, most, slope, True), load_shares(number_of, rows * top, most, slope, False)
    places = jnp.arange(number_of)

    def named(tallies, rotation):
        used = int((tallies > 0).sum())
        fixed = max(1, used // 4)
        shifted = fixed + (places - fixed + rotation * (used - fixed)) % max(1, number_of - fixed)
        return jnp.zeros((number_of,), jnp.int32).at[sequence[jnp.where(places < fixed, places, shifted)]].set(jnp.asarray(tallies, jnp.int32))

    tallies = jnp.where(number % 4 == 0, named(crowded, number // 4), named(ordinary, number - number // 4 - 1))
    mixed = jax.random.permutation(jax.random.fold_in(own, 3), number_of)
    giver, taker = mixed[0:number_of // 2 * 2:2], mixed[1:number_of // 2 * 2:2]
    slack = jnp.minimum(tallies[giver] - 1, most - tallies[taker]) // 2
    slack = jnp.where((giver == sequence[0]) | (taker == sequence[0]) | (tallies[taker] == 0), 0, jnp.maximum(slack, 0))
    shifted = jax.random.randint(jax.random.fold_in(own, 4), (number_of // 2,), 0, 1 << 20) % (slack + 1)
    tallies = tallies.at[giver].add(-shifted).at[taker].add(shifted)
    items = jnp.searchsorted(jnp.cumsum(tallies), jnp.arange(rows * top), side="right").astype(jnp.int32)
    table = items.reshape(top, rows).T
    table = table[jax.random.permutation(jax.random.fold_in(own, 1), rows)]
    rotation = jax.random.randint(jax.random.fold_in(own, 2), (rows, 1), 0, top)
    return jnp.take_along_axis(table, (jnp.arange(top)[None, :] + rotation) % top, axis=1)


def load_shares(count, total, limit, skew, full):
    weights = [(1 << 20) // math.isqrt(grade ** skew) + 1 for grade in range(1, count + 1)]
    largest = limit if full else min(limit, max(-(-total // count), total * weights[0] // sum(weights)))
    least = 1 if total - largest >= count - 1 else 0
    holding, surplus = [largest] + [least] * (count - 1), total - largest - least * (count - 1)
    while surplus > 0:
        candidates = [i for i in range(1, count) if holding[i] < largest] or [i for i in range(1, count) if holding[i] < limit]
        whole, remaining = sum([weights[i] for i in candidates]), surplus
        for i in candidates:
            more = min(limit - holding[i], max(1, remaining * weights[i] // whole), surplus)
            holding[i] = holding[i] + more
            surplus = surplus - more
    return np.array(holding)


def setup_inputs(seed: int = 0) -> dict:
    keys = jax.random.split(jax.random.key(seed), 5)
    slab = draw_slab(jax.random.fold_in(keys[4], 71), 0)
    basis = draw_basis(jax.random.fold_in(keys[4], 71), 0)
    cluster_ids_keys = jax.random.split(jax.random.fold_in(keys[2], 1), NROWS // R_DEV)
    cluster_ids_turns = jax.random.permutation(jax.random.fold_in(keys[2], 3), NROWS // R_DEV)
    cluster_ids = jax.vmap(lambda own, number: deal_out(jax.random.fold_in(keys[2], 2), own, number, R_DEV, CLUSTERS, 1, CAP, 2))(cluster_ids_keys, cluster_ids_turns).reshape((NROWS, 1))
    kept = jax.random.randint(keys[3], (1,), K // 2, K + 1).astype(jnp.int32)
    return {"slab": slab, "basis": basis, "cluster_ids": cluster_ids, "kept": kept}


def orthonormal(matrix):
    gram = jnp.dot(matrix.T, matrix, precision=lax.Precision.HIGHEST)
    lower = jnp.linalg.cholesky(gram)
    eye = jnp.eye(gram.shape[0], dtype=matrix.dtype)
    inverse = lax.linalg.triangular_solve(lower, eye, left_side=True, lower=True)
    return jnp.dot(matrix, inverse.T, precision=lax.Precision.HIGHEST)

def reference(slab, basis, cluster_ids, kept):
    current = basis
    for step in range(ITERS):
        basis_b = current.astype(jnp.bfloat16)
        scores = jnp.dot(slab.astype(jnp.float32), basis_b.astype(jnp.float32), preferred_element_type=jnp.float32).astype(jnp.bfloat16)
        product = lax.dot_general(slab.astype(jnp.float32), scores.astype(jnp.float32), (((0,), (0,)), ((), ())), preferred_element_type=jnp.float32)
        current = orthonormal(product)
    columns = jnp.arange(K, dtype=jnp.int32)
    masked = jnp.where(columns[None, :] < kept[0], current.astype(jnp.bfloat16), jnp.zeros((), jnp.bfloat16))
    projected = jnp.dot(slab.astype(jnp.float32), masked.astype(jnp.float32), preferred_element_type=jnp.float32).astype(jnp.bfloat16)
    ids = cluster_ids[:, 0].reshape(N_ROWS, R_DEV)
    onehot = (ids[:, :, None] == jnp.arange(CLUSTERS, dtype=jnp.int32)[None, None, :]).astype(jnp.int32)
    running = jnp.cumsum(onehot, axis=1)
    slot = jnp.sum(onehot * running, axis=2) - 1
    source = jnp.arange(N_ROWS, dtype=jnp.int32)[:, None]
    flat = ((ids * N_ROWS + source) * CAP + slot).reshape(-1).astype(jnp.int32)
    packed = jnp.zeros((CLUSTERS * N_ROWS * CAP, K), jnp.bfloat16).at[flat].set(projected)
    return packed.reshape(CLUSTERS, N_ROWS * CAP, K)
```

```python
import functools

import jax
import jax.numpy as jnp
from jax import lax
from jax.experimental import pallas as pl
from jax.experimental.pallas import tpu as pltpu
from jax.sharding import Mesh
from jax.sharding import PartitionSpec as P

ITERS = 2
CAP = 128
NC = 4
TOL = 2e-3
STEPS = 12
F32 = jnp.float32
BF16 = jnp.bfloat16
MESH = pl.DeviceIdType.MESH
VMEM = pl.BlockSpec(memory_space=pltpu.VMEM)
ANY = pl.BlockSpec(memory_space=pl.ANY)
FEAT = ("xl", "core")


def nn(a, b, precision=None):
    return lax.dot_general(
        a, b, (((1,), (0,)), ((), ())), precision=precision, preferred_element_type=F32
    )


def nt(a, b, precision=None):
    return lax.dot_general(
        a, b, (((1,), (1,)), ((), ())), precision=precision, preferred_element_type=F32
    )


def tn(a, b):
    return lax.dot_general(a, b, (((0,), (0,)), ((), ())), preferred_element_type=F32)


def greet(targets):
    barrier = pltpu.get_barrier_semaphore()
    for target in targets:
        pl.semaphore_signal(barrier, inc=1, device_id=target, device_id_type=MESH)
    return barrier


def greet_rows(barrier, me, count):
    @pl.loop(1, count)
    def _(d):
        peer = lax.rem(me + d, count)
        pl.semaphore_signal(barrier, inc=1, device_id={"rows": peer}, device_id_type=MESH)


def remote(src, dst, send, recv, target):
    return pltpu.make_async_remote_copy(
        src_ref=src, dst_ref=dst, send_sem=send, recv_sem=recv, device_id=target, device_id_type=MESH
    )


def slab_loads(slab, held, sems, core, chunk):
    half = NC * chunk

    def load(own, i):
        h = core if own else 1 - core
        start = pl.multiple_of(h * half + i * chunk, chunk)
        return pltpu.make_async_copy(slab.at[pl.ds(start, chunk)], held.at[h, i], sems.at[int(own), i])

    for i in range(NC):
        load(False, i).start()
        load(True, i).start()
    return load


def covariance_kernel(rows, slab, q, z_out, gram_out, held, away, home, part, mine, theirs, y, z,
                      z_send, z_recv, z_full, g_part, g_near, g_mine, g_far, g_all,
                      load_sem, near_sem, far_sem, y_sem, rs_sem, ag_sem, g_sem):
    me, core, xl = lax.axis_index("rows"), lax.axis_index("core"), lax.axis_index("xl")
    near, far = {"core": 1 - core}, {"xl": 1 - xl}
    chunk = slab.shape[0] // (2 * NC)
    width = q.shape[1]
    barrier = greet((near, far))
    greet_rows(barrier, me, rows)
    load = slab_loads(slab, held, load_sem, core, chunk)

    def to_near(i):
        return remote(away.at[i], home.at[i], near_sem.at[0, i], near_sem.at[1, i], near)

    def to_far(i):
        return remote(mine.at[i], theirs.at[i], far_sem.at[0, i], far_sem.at[1, i], far)

    def share(i):
        return remote(y.at[core, i], y.at[core, i], y_sem.at[0, i], y_sem.at[1, i], near)

    def shared(i):
        return remote(y.at[1 - core, i], y.at[1 - core, i], y_sem.at[0, i], y_sem.at[1, i], near)

    def chip_sum(i):
        to_near(i).wait_recv()
        mine[i] = (part[i] + home[i].astype(F32)).astype(BF16)
        to_far(i).start()

    for i in range(NC):
        load(False, i).wait()
        away[i] = nn(held[1 - core, i], q[...]).astype(BF16)
        if i == 0:
            pl.semaphore_wait(barrier, rows + 1)
        to_near(i).start()
        load(True, i).wait()
        part[i] = nn(held[core, i], q[...])
        if i > 0:
            chip_sum(i - 1)
    chip_sum(NC - 1)

    def add(h, i, first=False):
        term = tn(y[h, i], held[h, i])
        z[...] = term if first else z[...] + term

    for i in range(NC):
        to_far(i).wait_recv()
        y[core, i] = (mine[i].astype(F32) + theirs[i].astype(F32)).astype(BF16)
        share(i).start()
        add(core, i, i == 0)
        if i > 0:
            shared(i - 1).wait_recv()
            add(1 - core, i - 1)
    shared(NC - 1).wait_recv()
    add(1 - core, NC - 1)

    deep, wide = z_send.shape[1:]
    group = rows // 2
    for p in range(rows):
        f, k = divmod(p, group)
        z_send[p] = z[k * deep:(k + 1) * deep, f * wide:(f + 1) * wide].astype(BF16)

    def scatter(d):
        peer = lax.rem(me + d, rows)
        return remote(z_send.at[peer], z_recv.at[d - 1], rs_sem.at[0, d - 1], rs_sem.at[1, d - 1],
                      {"rows": peer})

    def gather(d):
        peer = lax.rem(me + d, rows)
        return remote(z_full.at[me], z_full.at[me], ag_sem.at[0, d - 1], ag_sem.at[1, d - 1],
                      {"rows": peer})

    def gathered(d):
        peer = lax.rem(me - d + rows, rows)
        return remote(z_full.at[peer], z_full.at[peer], ag_sem.at[0, d - 1], ag_sem.at[1, d - 1],
                      {"rows": peer})

    @pl.loop(1, rows)
    def _(d):
        scatter(d).start()

    def total(d, acc):
        scatter(d).wait_recv()
        return acc + z_recv[d - 1].astype(F32)

    z_full[me] = lax.fori_loop(1, rows, total, z_send[me].astype(F32)).astype(BF16)

    @pl.loop(1, rows)
    def _(d):
        gather(d).start()

    @pl.loop(1, rows)
    def _(d):
        gathered(d).wait_recv()

    half = width // 2
    first = z_full[0:group].reshape(width, wide)
    second = z_full[group:rows].reshape(width, wide)
    g_part[...] = (nt(first, first) + nt(second, second)).reshape(2, half, width)
    out_near = remote(g_part.at[1 - core], g_near, g_sem.at[0, 0], g_sem.at[1, 0], near)
    out_far = remote(g_mine, g_far, g_sem.at[0, 1], g_sem.at[1, 1], far)
    out_back = remote(g_all.at[core], g_all.at[core], g_sem.at[0, 2], g_sem.at[1, 2], near)
    in_back = remote(g_all.at[1 - core], g_all.at[1 - core], g_sem.at[0, 2], g_sem.at[1, 2], near)
    out_near.start()
    z_out[...] = z_full[...]
    out_near.wait_recv()
    g_mine[...] = g_part[core] + g_near[...]
    out_far.start()
    out_far.wait_recv()
    g_all[core] = g_mine[...] + g_far[...]
    out_back.start()
    in_back.wait_recv()
    gram_out[...] = g_all[...].reshape(width, width)
    for i in range(NC):
        to_near(i).wait_send()
        to_far(i).wait_send()
        share(i).wait_send()

    @pl.loop(1, rows)
    def _(d):
        scatter(d).wait_send()
        gather(d).wait_send()

    out_near.wait_send()
    out_far.wait_send()
    out_back.wait_send()


def covariance(slab, q, rows, ident):
    length, feats = slab.shape
    width = q.shape[1]
    chunk = length // (2 * NC)
    piece = (2 * width // rows, feats // 2)
    half = (width // 2, width)
    dma = pltpu.SemaphoreType.DMA
    return pl.pallas_call(
        functools.partial(covariance_kernel, rows),
        out_shape=(
            jax.ShapeDtypeStruct((rows, *piece), BF16),
            jax.ShapeDtypeStruct((width, width), F32),
        ),
        in_specs=[ANY, VMEM],
        out_specs=(VMEM, VMEM),
        scratch_shapes=[
            pltpu.VMEM((2, NC, chunk, feats), BF16),
            pltpu.VMEM((NC, chunk, width), BF16),
            pltpu.VMEM((NC, chunk, width), BF16),
            pltpu.VMEM((NC, chunk, width), F32),
            pltpu.VMEM((NC, chunk, width), BF16),
            pltpu.VMEM((NC, chunk, width), BF16),
            pltpu.VMEM((2, NC, chunk, width), BF16),
            pltpu.VMEM((width, feats), F32),
            pltpu.VMEM((rows, *piece), BF16),
            pltpu.VMEM((rows - 1, *piece), BF16),
            pltpu.VMEM((rows, *piece), BF16),
            pltpu.VMEM((2, *half), F32),
            pltpu.VMEM(half, F32),
            pltpu.VMEM(half, F32),
            pltpu.VMEM(half, F32),
            pltpu.VMEM((2, *half), F32),
            dma((2, NC)),
            dma((2, NC)),
            dma((2, NC)),
            dma((2, NC)),
            dma((2, rows - 1)),
            dma((2, rows - 1)),
            dma((2, 3)),
        ],
        compiler_params=pltpu.CompilerParams(
            collective_id=ident, has_side_effects=True, vmem_limit_bytes=48 << 20
        ),
        name="covariance",
    )(slab, q)


def basis_kernel(last, kept, gram, z, q_out, x, e, a, state):
    n = gram.shape[0]
    row = lax.broadcasted_iota(jnp.int32, (n, n), 0)
    col = lax.broadcasted_iota(jnp.int32, (n, n), 1)
    lower = jnp.where(row > col, F32(1), jnp.where(row == col, F32(0.5), F32(0)))
    eye = jnp.where(row == col, F32(1), F32(0))
    high = lax.Precision.HIGHEST

    g = gram[...]
    diag = g * eye
    across = lax.rsqrt(jnp.sum(diag, axis=0, keepdims=True))
    down = lax.rsqrt(jnp.sum(diag, axis=1, keepdims=True))
    e[...] = g * across * down - eye
    x[...] = eye * across
    state[0] = 0
    state[1] = 0

    @pl.loop(0, STEPS)
    def _(step):
        @pl.when(state[0] == 0)
        def _():
            now = e[...]
            err = jnp.sum(now * now)
            x[...] = x[...] - nn(now * lower, x[...], high)
            done = err < TOL * TOL
            state[0] = done.astype(jnp.int32)

            @pl.when(jnp.logical_not(done))
            def _():
                e[...] = nt(nn(x[...], gram[...], high), x[...], high) - eye

    @pl.when(state[0] == 0)
    def _():
        a[...] = gram[...]
        x[...] = eye

        @pl.loop(0, n)
        def _(j):
            pick_row = row == j
            pick_col = col == j
            now = a[...]
            inv = x[...]
            a_row = jnp.sum(jnp.where(pick_row, now, 0.0), axis=0, keepdims=True)
            a_col = jnp.sum(jnp.where(pick_col, now, 0.0), axis=1, keepdims=True)
            x_row = jnp.sum(jnp.where(pick_row, inv, 0.0), axis=0, keepdims=True)
            pivot = jnp.sum(jnp.where(pick_row & pick_col, now, 0.0))
            root = jnp.sqrt(jnp.full((1, n), pivot))
            scaled = x_row / root
            factor = jnp.where(row[:, :1] > j, a_col / root[:, :1], 0.0)
            x[...] = jnp.where(pick_row, scaled, inv - factor * scaled)
            a[...] = now - factor * (a_row / root)

    inverse = x[...]
    top = inverse.astype(BF16)
    rest = (inverse - top.astype(F32)).astype(BF16)
    rows = z.shape[0]
    wide = z.shape[2]
    for f in range(2):
        block = z[f * (rows // 2):(f + 1) * (rows // 2)].reshape(n, wide)
        qt = nn(top, block) + nn(rest, block)
        if last:
            index = lax.broadcasted_iota(jnp.int32, (n, wide), 0)
            qt = jnp.where(index < kept[0], qt, 0.0)
        q_out[f * wide:(f + 1) * wide, :] = qt.T.astype(BF16)


def new_basis(kept, gram, z, last):
    n = gram.shape[0]
    return pl.pallas_call(
        functools.partial(basis_kernel, last),
        out_shape=jax.ShapeDtypeStruct((2 * z.shape[2], n), BF16),
        in_specs=[pl.BlockSpec(memory_space=pltpu.SMEM), VMEM, VMEM],
        out_specs=VMEM,
        scratch_shapes=[
            pltpu.VMEM((n, n), F32),
            pltpu.VMEM((n, n), F32),
            pltpu.VMEM((n, n), F32),
            pltpu.SMEM((2,), jnp.int32),
        ],
        name="new_basis",
    )(kept, gram, z)


def project_kernel(slab, q, p_out, held, away, home, part, keep, send, recv, p,
                   load_sem, near_sem, far_sem, p_sem):
    core, xl = lax.axis_index("core"), lax.axis_index("xl")
    near, far = {"core": 1 - core}, {"xl": 1 - xl}
    chunk = slab.shape[0] // (2 * NC)
    width = q.shape[1]
    half = width // 2
    barrier = greet((near, far))
    load = slab_loads(slab, held, load_sem, core, chunk)

    def to_near(i):
        return remote(away.at[i], home.at[i], near_sem.at[0, i], near_sem.at[1, i], near)

    def to_far(i):
        return remote(send.at[i], recv.at[i], far_sem.at[0, i], far_sem.at[1, i], far)

    def share(i):
        return remote(p.at[core, i], p.at[core, i], p_sem.at[0, i], p_sem.at[1, i], near)

    def shared(i):
        return remote(p.at[1 - core, i], p.at[1 - core, i], p_sem.at[0, i], p_sem.at[1, i], near)

    def chip_sum(i):
        to_near(i).wait_recv()
        both = part[i] + home[i].astype(F32)
        low, high = both[:, :half], both[:, half:]
        keep[i] = jnp.where(xl == 0, low, high)
        send[i] = jnp.where(xl == 0, high, low).astype(BF16)
        to_far(i).start()

    for i in range(NC):
        load(False, i).wait()
        away[i] = nn(held[1 - core, i], q[...]).astype(BF16)
        if i == 0:
            pl.semaphore_wait(barrier, 2)
        to_near(i).start()
        load(True, i).wait()
        part[i] = nn(held[core, i], q[...])
        if i > 0:
            chip_sum(i - 1)
    chip_sum(NC - 1)
    for i in range(NC):
        to_far(i).wait_recv()
        p[core, i] = (keep[i] + recv[i].astype(F32)).astype(BF16)
        share(i).start()
    for i in range(NC):
        shared(i).wait_recv()
    p_out[...] = p[...].reshape(p_out.shape)
    for i in range(NC):
        to_near(i).wait_send()
        to_far(i).wait_send()
        share(i).wait_send()


def project(slab, q, ident):
    length, feats = slab.shape
    width = q.shape[1]
    chunk = length // (2 * NC)
    half = width // 2
    dma = pltpu.SemaphoreType.DMA
    return pl.pallas_call(
        project_kernel,
        out_shape=jax.ShapeDtypeStruct((length, half), BF16),
        in_specs=[ANY, VMEM],
        out_specs=VMEM,
        scratch_shapes=[
            pltpu.VMEM((2, NC, chunk, feats), BF16),
            pltpu.VMEM((NC, chunk, width), BF16),
            pltpu.VMEM((NC, chunk, width), BF16),
            pltpu.VMEM((NC, chunk, width), F32),
            pltpu.VMEM((NC, chunk, half), F32),
            pltpu.VMEM((NC, chunk, half), BF16),
            pltpu.VMEM((NC, chunk, half), BF16),
            pltpu.VMEM((2, NC, chunk, half), BF16),
            dma((2, NC)),
            dma((2, NC)),
            dma((2, NC)),
            dma((2, NC)),
        ],
        compiler_params=pltpu.CompilerParams(
            collective_id=ident, has_side_effects=True, vmem_limit_bytes=40 << 20
        ),
        name="project",
    )(slab, q)


def place_kernel(clusters, ids, place):
    blocks = ids.shape[0]
    lane = lax.broadcasted_iota(jnp.int32, (CAP, CAP), 1)
    sub = lax.broadcasted_iota(jnp.int32, (CAP, CAP), 0)
    before = jnp.where(sub < lane, F32(1), F32(0)).astype(BF16)
    names = lax.broadcasted_iota(jnp.int32, (clusters, CAP), 0)
    seen = jnp.zeros((clusters, 1), F32)
    for b in range(blocks):
        block = ids[b:b + 1, :]
        hot = jnp.where(names == block, F32(1), F32(0))
        earlier = nn(hot.astype(BF16), before) + seen
        slot = jnp.sum(hot * earlier, axis=0, keepdims=True).astype(jnp.int32)
        pair = lax.div(block, 2)
        odd = block - 2 * pair
        place[b:b + 1, :] = odd * (clusters // 2 * CAP) + pair * CAP + slot
        seen = seen + jnp.sum(hot, axis=1, keepdims=True)


def places(cluster_ids, clusters):
    ids = cluster_ids.reshape(-1, CAP)
    return pl.pallas_call(
        functools.partial(place_kernel, clusters),
        out_shape=jax.ShapeDtypeStruct(ids.shape, jnp.int32),
        in_specs=[VMEM],
        out_specs=VMEM,
        name="places",
    )(ids).reshape(-1)


def pack_kernel(place, side, p, out, doubled, spread):
    rows = out.shape[0]
    length, lanes = p.shape
    cols = lanes // 2
    unroll = 16
    low = lax.broadcasted_iota(jnp.int32, (length, lanes), 1) < cols
    wide = p[...].astype(F32)
    turned = pltpu.roll(wide, cols, 1)
    doubled[...] = jnp.where(low == (side[0] == 0), wide, turned)
    spread[...] = jnp.zeros_like(spread)

    @pl.loop(0, length // unroll)
    def _(step):
        for u in range(unroll):
            i = step * unroll + u
            spread[pl.ds(place[i], 1), :] = doubled[pl.ds(i, 1), :]

    even = lax.broadcasted_iota(jnp.int32, (CAP, lanes), 1) < cols

    @pl.loop(0, rows)
    def _(r):
        start = pl.multiple_of(r * CAP, CAP)
        first = spread[pl.ds(start, CAP), :]
        second = spread[pl.ds(pl.multiple_of(rows * CAP + start, CAP), CAP), :]
        out[r] = jnp.where(even, first, second).T.astype(BF16)


def packed_rows(place, side, p, rows):
    length, lanes = p.shape
    smem = pl.BlockSpec(memory_space=pltpu.SMEM)
    return pl.pallas_call(
        pack_kernel,
        out_shape=jax.ShapeDtypeStruct((rows, lanes, CAP), BF16),
        in_specs=[smem, smem, VMEM],
        out_specs=VMEM,
        scratch_shapes=[pltpu.VMEM((length, lanes), F32), pltpu.VMEM((2 * rows * CAP, lanes), F32)],
        compiler_params=pltpu.CompilerParams(vmem_limit_bytes=32 << 20),
        name="packed_rows",
    )(place, side, p)


def exchange_kernel(rows, buf, out, arrived, sem):
    me = lax.axis_index("rows")
    barrier = pltpu.get_barrier_semaphore()
    greet_rows(barrier, me, rows)
    pl.semaphore_wait(barrier, rows - 1)

    def send(d):
        peer = lax.rem(me + d, rows)
        return remote(buf.at[peer], arrived.at[me], sem.at[0, d - 1], sem.at[1, d - 1], {"rows": peer})

    def came(d):
        peer = lax.rem(me - d + rows, rows)
        return remote(buf.at[peer], arrived.at[peer], sem.at[0, d - 1], sem.at[1, d - 1], {"rows": peer})

    @pl.loop(1, rows)
    def _(d):
        send(d).start()

    arrived[me] = buf[me]

    @pl.loop(1, rows)
    def _(d):
        came(d).wait_recv()

    cols = out.shape[1]
    for r in range(rows):
        for h in range(2):
            out[h, :, r * CAP:(r + 1) * CAP] = arrived[r, h * cols:(h + 1) * cols, :]

    @pl.loop(1, rows)
    def _(d):
        send(d).wait_send()


def exchange(buf, ident):
    rows, lanes, _ = buf.shape
    return pl.pallas_call(
        functools.partial(exchange_kernel, rows),
        out_shape=jax.ShapeDtypeStruct((2, lanes // 2, rows * CAP), BF16),
        in_specs=[VMEM],
        out_specs=VMEM,
        scratch_shapes=[pltpu.VMEM(buf.shape, BF16), pltpu.SemaphoreType.DMA((2, rows - 1))],
        compiler_params=pltpu.CompilerParams(collective_id=ident, has_side_effects=True),
        name="exchange",
    )(buf)


def shards(rows, slab, basis, cluster_ids, kept):
    place = places(cluster_ids, 2 * rows)
    side = jnp.broadcast_to(lax.axis_index("core"), (1,)).astype(jnp.int32)
    q = basis.astype(BF16)
    for step in range(ITERS):
        z, gram = covariance(slab, q, rows, step)
        q = new_basis(kept, gram, z, step == ITERS - 1)
    p = project(slab, q, ITERS)
    buf = packed_rows(place, side, p, rows)
    return jnp.swapaxes(exchange(buf, ITERS + 1), 1, 2)


def solution(mesh):
    rows = mesh.shape["rows"]
    torus = Mesh(mesh.devices.reshape(rows, 2, 2), ("rows", "xl", "core"))
    placed = (P("rows", FEAT), P(FEAT, None), P("rows", None), P())
    return jax.shard_map(
        functools.partial(shards, rows), mesh=torus, in_specs=placed,
        out_specs=P("rows", None, FEAT), check_vma=False,
    )
```

```python
import functools

import jax
import jax.numpy as jnp
from jax import lax
from jax.experimental import pallas as pl
from jax.experimental.pallas import tpu as pltpu
from jax.sharding import Mesh
from jax.sharding import PartitionSpec as P

ITERS = 2
CAP = 128
NC = 6
NP = 4
NS = 2
TOL = 2e-3
COARSE = 1.0
STEPS = 14
F32 = jnp.float32
BF16 = jnp.bfloat16
MESH = pl.DeviceIdType.MESH
VMEM = pl.BlockSpec(memory_space=pltpu.VMEM)
SMEM = pl.BlockSpec(memory_space=pltpu.SMEM)
FEAT = ("xl", "core")


def nn(a, b):
    return lax.dot_general(a, b, (((1,), (0,)), ((), ())), preferred_element_type=F32)


def nt(a, b):
    return lax.dot_general(a, b, (((1,), (1,)), ((), ())), preferred_element_type=F32)


def tn(a, b):
    return lax.dot_general(a, b, (((0,), (0,)), ((), ())), preferred_element_type=F32)


def greet(targets):
    barrier = pltpu.get_barrier_semaphore()
    for target in targets:
        pl.semaphore_signal(barrier, inc=1, device_id=target, device_id_type=MESH)
    return barrier


def grid_of(rows):
    return (4, 4, 2) if rows == 32 else (2, rows // 4, 2)


def shifted(me, rows, shift):
    nz, ny, nx = grid_of(rows)
    z, y, x = me // (ny * nx), (me // nx) % ny, me % nx
    dz, dy, dx = shift
    return ((z + dz) % nz) * (ny * nx) + ((y + dy) % ny) * nx + (x + dx) % nx


def axis_peers(me, rows):
    nz, ny, nx = grid_of(rows)
    shifts = [(d, 0, 0) for d in range(1, nz)] + [(0, d, 0) for d in range(1, ny)]
    shifts += [(0, 0, d) for d in range(1, nx)]
    return [{"rows": shifted(me, rows, shift)} for shift in shifts]


def each_peer(me, rows, body):
    nz, ny, nx = grid_of(rows)
    fz, fy, fx = nz // 2, ny // 2, nx // 2

    def step(i):
        dz = (fz + i // (ny * nx)) % nz
        dy = (fy + (i // nx) % ny) % ny
        dx = (fx + i % nx) % nx
        there = shifted(me, rows, (dz, dy, dx))
        back = shifted(me, rows, (nz - dz, ny - dy, nx - dx))
        body(i, there, back)

    own = ((nz - fz) % nz) * ny * nx + ((ny - fy) % ny) * nx + (nx - fx) % nx
    pl.loop(0, own)(step)
    if own + 1 < rows:
        pl.loop(own + 1, rows)(step)


def remote(src, dst, send, recv, target):
    return pltpu.make_async_remote_copy(
        src_ref=src, dst_ref=dst, send_sem=send, recv_sem=recv, device_id=target, device_id_type=MESH
    )


def find_places(clusters, ids, place):
    blocks = ids.shape[0]
    lane = lax.broadcasted_iota(jnp.int32, (CAP, CAP), 1)
    sub = lax.broadcasted_iota(jnp.int32, (CAP, CAP), 0)
    before = jnp.where(sub < lane, F32(1), F32(0)).astype(BF16)
    names = lax.broadcasted_iota(jnp.int32, (clusters, CAP), 0)
    seen = jnp.zeros((clusters, 1), F32)
    for b in range(blocks):
        block = ids[b:b + 1, :]
        hot = jnp.where(names == block, F32(1), F32(0))
        earlier = nn(hot.astype(BF16), before) + seen
        slot = jnp.sum(hot * earlier, axis=0, keepdims=True).astype(jnp.int32)
        pair = block // 2
        odd = block - 2 * pair
        place[b:b + 1, :] = odd * (clusters // 2 * CAP) + pair * CAP + slot
        seen = seen + jnp.sum(hot, axis=1, keepdims=True)


def covariance_kernel(rows, first, *refs):
    if first:
        slab, q, ids, z_out, gram_out, place, *refs = refs
    else:
        slab, q, z_out, gram_out, *refs = refs
    (qb, total, away, home, part, mine, theirs, y, z, z_send, z_recv, z_full, g_part, g_near, g_mine, g_far, g_all,
     near_sem, far_sem, y_sem, rs_sem, ag_sem, g_sem, round_a, round_b) = refs
    me, core, xl = lax.axis_index("rows"), lax.axis_index("core"), lax.axis_index("xl")
    near, far = {"core": 1 - core}, {"xl": 1 - xl}
    chunk = slab.shape[0] // (2 * NC)
    half_rows = NC * chunk
    width = q.shape[1]
    peers = axis_peers(me, rows)
    barrier = greet([near, far] + peers)
    qb[...] = q[...].astype(BF16)

    def held(h, i):
        return slab[pl.ds(pl.multiple_of(h * half_rows + i * chunk, chunk), chunk), :]

    def to_near(i):
        return remote(away.at[i], home.at[i], near_sem.at[0, i], near_sem.at[1, i], near)

    def to_far(i):
        return remote(mine.at[i], theirs.at[i], far_sem.at[0, i], far_sem.at[1, i], far)

    def share(i):
        return remote(y.at[core, i], y.at[core, i], y_sem.at[0, i], y_sem.at[1, i], near)

    def shared(i):
        return remote(y.at[1 - core, i], y.at[1 - core, i], y_sem.at[0, i], y_sem.at[1, i], near)

    def chip_sum(i):
        to_near(i).wait_recv()
        mine[i] = (part[i] + home[i].astype(F32)).astype(BF16)
        to_far(i).start()

    def pass_on(sem):
        for peer in peers:
            pl.semaphore_signal(sem, inc=1, device_id=peer, device_id_type=MESH)

    for i in range(NC):
        away[i] = nn(held(1 - core, i), qb[...]).astype(BF16)
        if i == 0:
            pl.semaphore_wait(barrier, len(peers) + 2)
        to_near(i).start()
        part[i] = nn(held(core, i), qb[...])
        if i > 0:
            chip_sum(i - 1)
        if i == 1:
            pass_on(round_a)
    chip_sum(NC - 1)
    pl.semaphore_wait(round_a, len(peers))
    pass_on(round_b)
    if first:
        find_places(2 * rows, ids, place)
    pl.semaphore_wait(round_b, len(peers))

    def add(h, i, start=False):
        term = tn(y[h, i], held(h, i))
        z[...] = term if start else z[...] + term

    for i in range(NC):
        to_far(i).wait_recv()
        y[core, i] = (mine[i].astype(F32) + theirs[i].astype(F32)).astype(BF16)
        share(i).start()
        add(core, i, i == 0)
        if i > 0:
            shared(i - 1).wait_recv()
            add(1 - core, i - 1)
    shared(NC - 1).wait_recv()
    add(1 - core, NC - 1)

    deep, wide = z_send.shape[2:]
    group = rows // 2
    for s in range(NS):
        for p in range(rows):
            f, k = divmod(p, group)
            left = (f * NS + s) * wide
            z_send[s, p] = z[k * deep:(k + 1) * deep, left:left + wide].astype(BF16)

    def scatter(s, slot, there):
        return remote(z_send.at[s, there], z_recv.at[s, slot], rs_sem.at[0, s, slot], rs_sem.at[1, s, slot],
                      {"rows": there})

    def gather(s, slot, owner, there):
        return remote(z_full.at[s, owner], z_full.at[s, owner], ag_sem.at[0, s, slot], ag_sem.at[1, s, slot],
                      {"rows": there})

    for s in range(NS):
        each_peer(me, rows, lambda i, there, back: scatter(s, i, there).start())
    for s in range(NS):
        total[...] = z_send[s, me].astype(F32)

        def more(i, there, back):
            scatter(s, i, there).wait_recv()
            total[...] = total[...] + z_recv[s, i].astype(F32)

        each_peer(me, rows, more)
        z_full[s, me] = total[...].astype(BF16)
        each_peer(me, rows, lambda i, there, back: gather(s, i, me, there).start())

    half = width // 2
    for s in range(NS):
        each_peer(me, rows, lambda i, there, back: gather(s, i, back, there).wait_recv())
        for f in range(2):
            block = z_full[s, f * group:(f + 1) * group].reshape(width, wide)
            term = nt(block, block).reshape(2, half, width)
            g_part[...] = term if s + f == 0 else g_part[...] + term
    out_near = remote(g_part.at[1 - core], g_near, g_sem.at[0, 0], g_sem.at[1, 0], near)
    out_far = remote(g_mine, g_far, g_sem.at[0, 1], g_sem.at[1, 1], far)
    out_back = remote(g_all.at[core], g_all.at[core], g_sem.at[0, 2], g_sem.at[1, 2], near)
    in_back = remote(g_all.at[1 - core], g_all.at[1 - core], g_sem.at[0, 2], g_sem.at[1, 2], near)
    out_near.start()
    z_out[...] = z_full[...]
    out_near.wait_recv()
    g_mine[...] = g_part[core] + g_near[...]
    out_far.start()
    out_far.wait_recv()
    g_all[core] = g_mine[...] + g_far[...]
    out_back.start()
    in_back.wait_recv()
    gram_out[...] = g_all[...].reshape(width, width)
    for i in range(NC):
        to_near(i).wait_send()
        to_far(i).wait_send()
        share(i).wait_send()
    for s in range(NS):
        def sent(i, there, back):
            scatter(s, i, there).wait_send()
            gather(s, i, me, there).wait_send()

        each_peer(me, rows, sent)
    out_near.wait_send()
    out_far.wait_send()
    out_back.wait_send()


def covariance(slab, q, rows, ident, ids=None):
    length, feats = slab.shape
    width = q.shape[1]
    chunk = length // (2 * NC)
    piece = (2 * width // rows, feats // (2 * NS))
    half = (width // 2, width)
    dma = pltpu.SemaphoreType.DMA
    first = ids is not None
    out = [jax.ShapeDtypeStruct((NS, rows, *piece), BF16), jax.ShapeDtypeStruct((width, width), F32)]
    args = [slab, q]
    if first:
        out.append(jax.ShapeDtypeStruct(ids.shape, jnp.int32))
        args.append(ids)
    return pl.pallas_call(
        functools.partial(covariance_kernel, rows, first),
        out_shape=out,
        in_specs=[VMEM] * len(args),
        out_specs=[VMEM] * len(out),
        scratch_shapes=[
            pltpu.VMEM(q.shape, BF16),
            pltpu.VMEM(piece, F32),
            pltpu.VMEM((NC, chunk, width), BF16),
            pltpu.VMEM((NC, chunk, width), BF16),
            pltpu.VMEM((NC, chunk, width), F32),
            pltpu.VMEM((NC, chunk, width), BF16),
            pltpu.VMEM((NC, chunk, width), BF16),
            pltpu.VMEM((2, NC, chunk, width), BF16),
            pltpu.VMEM((width, feats), F32),
            pltpu.VMEM((NS, rows, *piece), BF16),
            pltpu.VMEM((NS, rows, *piece), BF16),
            pltpu.VMEM((NS, rows, *piece), BF16),
            pltpu.VMEM((2, *half), F32),
            pltpu.VMEM(half, F32),
            pltpu.VMEM(half, F32),
            pltpu.VMEM(half, F32),
            pltpu.VMEM((2, *half), F32),
            dma((2, NC)),
            dma((2, NC)),
            dma((2, NC)),
            dma((2, NS, rows)),
            dma((2, NS, rows)),
            dma((2, 3)),
            pltpu.SemaphoreType.REGULAR,
            pltpu.SemaphoreType.REGULAR,
        ],
        compiler_params=pltpu.CompilerParams(
            collective_id=ident, has_side_effects=True, vmem_limit_bytes=32 << 20
        ),
        name="covariance",
    )(*args)


def split(a):
    top = a.astype(BF16)
    return top, (a - top.astype(F32)).astype(BF16)


def fine(dot, a, b):
    (a0, a1), (b0, b1) = split(a), split(b)
    return dot(a0, b0) + (dot(a0, b1) + dot(a1, b0))


def basis_kernel(last, kept, gram, z, q_out, unit, x, e, a, state):
    n = gram.shape[0]
    row = lax.broadcasted_iota(jnp.int32, (n, n), 0)
    col = lax.broadcasted_iota(jnp.int32, (n, n), 1)
    lower = jnp.where(row > col, F32(1), jnp.where(row == col, F32(0.5), F32(0)))
    eye = jnp.where(row == col, F32(1), F32(0))

    g = gram[...]
    diag = g * eye
    across = lax.rsqrt(jnp.sum(diag, axis=0, keepdims=True))
    down = lax.rsqrt(jnp.sum(diag, axis=1, keepdims=True))
    scaled = g * across * down
    unit[...] = scaled
    begin = scaled - eye
    e[...] = begin
    x[...] = eye
    state[0] = 0

    @pl.loop(0, STEPS)
    def _(step):
        @pl.when(state[0] == 0)
        def _():
            now = e[...]
            size = jnp.sum(now * now)
            better = x[...] - nn((now * lower).astype(BF16), x[...].astype(BF16))
            x[...] = better
            done = size < TOL * TOL
            state[0] = done.astype(jnp.int32)

            @pl.when(size > COARSE * COARSE)
            def _():
                near = better.astype(BF16)
                e[...] = nt(nn(near, unit[...].astype(BF16)).astype(BF16), near) - eye

            @pl.when(jnp.logical_not(done) & jnp.logical_not(size > COARSE * COARSE))
            def _():
                e[...] = fine(nt, fine(nn, better, unit[...]), better) - eye

    @pl.when(state[0] == 0)
    def _():
        a[...] = unit[...]
        x[...] = eye

        @pl.loop(0, n)
        def _(j):
            pick_row = row == j
            pick_col = col == j
            now = a[...]
            inv = x[...]
            a_row = jnp.sum(jnp.where(pick_row, now, 0.0), axis=0, keepdims=True)
            a_col = jnp.sum(jnp.where(pick_col, now, 0.0), axis=1, keepdims=True)
            x_row = jnp.sum(jnp.where(pick_row, inv, 0.0), axis=0, keepdims=True)
            pivot = jnp.sum(jnp.where(pick_row & pick_col, now, 0.0))
            root = jnp.sqrt(jnp.full((1, n), pivot))
            line = x_row / root
            factor = jnp.where(row[:, :1] > j, a_col / root[:, :1], 0.0)
            x[...] = jnp.where(pick_row, line, inv - factor * line)
            a[...] = now - factor * (a_row / root)

    top, rest = split(x[...] * across)
    ns, rows, _, wide = z.shape
    group = rows // 2
    for f in range(2):
        for s in range(ns):
            block = z[s, f * group:(f + 1) * group].reshape(n, wide)
            qt = nn(top, block) + nn(rest, block)
            if last:
                index = lax.broadcasted_iota(jnp.int32, (n, wide), 0)
                qt = jnp.where(index < kept[0], qt, 0.0)
            left = (f * ns + s) * wide
            q_out[left:left + wide, :] = qt.T.astype(BF16)


def new_basis(kept, gram, z, last):
    n = gram.shape[0]
    return pl.pallas_call(
        functools.partial(basis_kernel, last),
        out_shape=jax.ShapeDtypeStruct((2 * z.shape[0] * z.shape[3], n), BF16),
        in_specs=[SMEM, VMEM, VMEM],
        out_specs=VMEM,
        scratch_shapes=[pltpu.VMEM((n, n), F32)] * 4 + [pltpu.SMEM((2,), jnp.int32)],
        compiler_params=pltpu.CompilerParams(vmem_limit_bytes=24 << 20),
        name="new_basis",
    )(kept, gram, z)


def project_kernel(slab, q, p_out, away, home, part, keep, send, recv, p,
                   near_sem, far_sem, p_sem):
    core, xl = lax.axis_index("core"), lax.axis_index("xl")
    near, far = {"core": 1 - core}, {"xl": 1 - xl}
    chunk = slab.shape[0] // (2 * NP)
    width = q.shape[1]
    half = width // 2
    barrier = greet((near, far))

    def held(h, i):
        return slab[pl.ds(pl.multiple_of(h * NP * chunk + i * chunk, chunk), chunk), :]

    def to_near(i):
        return remote(away.at[i], home.at[i], near_sem.at[0, i], near_sem.at[1, i], near)

    def to_far(i):
        return remote(send.at[i], recv.at[i], far_sem.at[0, i], far_sem.at[1, i], far)

    def share(i):
        return remote(p.at[core, i], p.at[core, i], p_sem.at[0, i], p_sem.at[1, i], near)

    def shared(i):
        return remote(p.at[1 - core, i], p.at[1 - core, i], p_sem.at[0, i], p_sem.at[1, i], near)

    def chip_sum(i):
        to_near(i).wait_recv()
        both = part[i] + home[i].astype(F32)
        low, high = both[:, :half], both[:, half:]
        keep[i] = jnp.where(xl == 0, low, high)
        send[i] = jnp.where(xl == 0, high, low).astype(BF16)
        to_far(i).start()

    for i in range(NP):
        away[i] = nn(held(1 - core, i), q[...]).astype(BF16)
        if i == 0:
            pl.semaphore_wait(barrier, 2)
        to_near(i).start()
        part[i] = nn(held(core, i), q[...])
        if i > 0:
            chip_sum(i - 1)
    chip_sum(NP - 1)
    for i in range(NP):
        to_far(i).wait_recv()
        p[core, i] = (keep[i] + recv[i].astype(F32)).astype(BF16)
        share(i).start()
    for i in range(NP):
        shared(i).wait_recv()
    p_out[...] = p[...].reshape(p_out.shape)
    for i in range(NP):
        to_near(i).wait_send()
        to_far(i).wait_send()
        share(i).wait_send()


def project(slab, q, ident):
    length = slab.shape[0]
    width = q.shape[1]
    chunk = length // (2 * NP)
    half = width // 2
    dma = pltpu.SemaphoreType.DMA
    return pl.pallas_call(
        project_kernel,
        out_shape=jax.ShapeDtypeStruct((length, half), BF16),
        in_specs=[VMEM, VMEM],
        out_specs=VMEM,
        scratch_shapes=[
            pltpu.VMEM((NP, chunk, width), BF16),
            pltpu.VMEM((NP, chunk, width), BF16),
            pltpu.VMEM((NP, chunk, width), F32),
            pltpu.VMEM((NP, chunk, half), F32),
            pltpu.VMEM((NP, chunk, half), BF16),
            pltpu.VMEM((NP, chunk, half), BF16),
            pltpu.VMEM((2, NP, chunk, half), BF16),
            dma((2, NP)),
            dma((2, NP)),
            dma((2, NP)),
        ],
        compiler_params=pltpu.CompilerParams(
            collective_id=ident, has_side_effects=True, vmem_limit_bytes=24 << 20
        ),
        name="project",
    )(slab, q)


def pack_kernel(place, side, p, out, doubled, spread):
    rows = out.shape[0]
    length, lanes = p.shape
    cols = lanes // 2
    unroll = 16
    low = lax.broadcasted_iota(jnp.int32, (length, lanes), 1) < cols
    wide = p[...].astype(F32)
    turned = pltpu.roll(wide, cols, 1)
    doubled[...] = jnp.where(low == (side[0] == 0), wide, turned)
    spread[...] = jnp.zeros_like(spread)

    @pl.loop(0, length // unroll)
    def _(step):
        for u in range(unroll):
            i = step * unroll + u
            spread[pl.ds(place[i], 1), :] = doubled[pl.ds(i, 1), :]

    even = lax.broadcasted_iota(jnp.int32, (CAP, lanes), 1) < cols

    @pl.loop(0, rows)
    def _(r):
        start = pl.multiple_of(r * CAP, CAP)
        first = spread[pl.ds(start, CAP), :]
        second = spread[pl.ds(pl.multiple_of(rows * CAP + start, CAP), CAP), :]
        out[r] = jnp.where(even, first, second).T.astype(BF16)


def packed_rows(place, side, p, rows):
    length, lanes = p.shape
    return pl.pallas_call(
        pack_kernel,
        out_shape=jax.ShapeDtypeStruct((rows, lanes, CAP), BF16),
        in_specs=[SMEM, SMEM, VMEM],
        out_specs=VMEM,
        scratch_shapes=[pltpu.VMEM((length, lanes), F32), pltpu.VMEM((2 * rows * CAP, lanes), F32)],
        compiler_params=pltpu.CompilerParams(vmem_limit_bytes=32 << 20),
        name="packed_rows",
    )(place, side, p)


def exchange_kernel(rows, buf, out, arrived, sem):
    me = lax.axis_index("rows")
    barrier = pltpu.get_barrier_semaphore()

    def hello(i, there, back):
        pl.semaphore_signal(barrier, inc=1, device_id={"rows": there}, device_id_type=MESH)

    each_peer(me, rows, hello)
    pl.semaphore_wait(barrier, rows - 1)

    def send(i, there, at):
        return remote(buf.at[there], arrived.at[at], sem.at[0, i], sem.at[1, i], {"rows": there})

    each_peer(me, rows, lambda i, there, back: send(i, there, me).start())
    arrived[me] = buf[me]
    each_peer(me, rows, lambda i, there, back: send(i, there, back).wait_recv())
    out[...] = arrived[...]
    each_peer(me, rows, lambda i, there, back: send(i, there, me).wait_send())


def exchange(buf, ident):
    rows = buf.shape[0]
    return pl.pallas_call(
        functools.partial(exchange_kernel, rows),
        out_shape=jax.ShapeDtypeStruct(buf.shape, BF16),
        in_specs=[VMEM],
        out_specs=VMEM,
        scratch_shapes=[pltpu.VMEM(buf.shape, BF16), pltpu.SemaphoreType.DMA((2, rows))],
        compiler_params=pltpu.CompilerParams(
            collective_id=ident, has_side_effects=True, vmem_limit_bytes=16 << 20
        ),
        name="exchange",
    )(buf)


def arrange_kernel(arrived, out):
    cols = out.shape[1]
    for r in range(arrived.shape[0]):
        for h in range(2):
            out[h, :, r * CAP:(r + 1) * CAP] = arrived[r, h * cols:(h + 1) * cols, :]


def arrange(arrived):
    rows, lanes, _ = arrived.shape
    return pl.pallas_call(
        arrange_kernel,
        out_shape=jax.ShapeDtypeStruct((2, lanes // 2, rows * CAP), BF16),
        in_specs=[VMEM],
        out_specs=VMEM,
        compiler_params=pltpu.CompilerParams(vmem_limit_bytes=16 << 20),
        name="arrange",
    )(arrived)


def shards(rows, slab, basis, cluster_ids, kept):
    side = jnp.broadcast_to(lax.axis_index("core"), (1,)).astype(jnp.int32)
    z, gram, place = covariance(slab, basis, rows, 0, cluster_ids.reshape(-1, CAP))
    for step in range(1, ITERS):
        q = new_basis(kept, gram, z, False)
        z, gram = covariance(slab, q, rows, step)
    q = new_basis(kept, gram, z, True)
    p = project(slab, q, ITERS)
    buf = packed_rows(place.reshape(-1), side, p, rows)
    return jnp.swapaxes(arrange(exchange(buf, ITERS + 1)), 1, 2)


def solution(mesh):
    rows = mesh.shape["rows"]
    torus = Mesh(mesh.devices.reshape(rows, 2, 2), ("rows", "xl", "core"))
    placed = (P("rows", FEAT), P(FEAT, None), P("rows", None), P())
    return jax.shard_map(
        functools.partial(shards, rows), mesh=torus, in_specs=placed,
        out_specs=P("rows", None, FEAT), check_vma=False,
    )
```

```python
import functools

import jax
import jax.numpy as jnp
from jax import lax
from jax.experimental import pallas as pl
from jax.experimental.pallas import tpu as pltpu
from jax.sharding import Mesh
from jax.sharding import PartitionSpec as P

ITERS = 2
CAP = 128
SHARES = (1, 2, 2, 2, 2, 2, 1)
NP = 4
NS = 2
TOL = 2e-3
COARSE = 1.0
STEPS = 14
F32 = jnp.float32
BF16 = jnp.bfloat16
MESH = pl.DeviceIdType.MESH
VMEM = pl.BlockSpec(memory_space=pltpu.VMEM)
SMEM = pl.BlockSpec(memory_space=pltpu.SMEM)
HBM = pl.BlockSpec(memory_space=pltpu.HBM)
FEAT = ("xl", "core")


def nn(a, b):
    return lax.dot_general(a, b, (((1,), (0,)), ((), ())), preferred_element_type=F32)


def nt(a, b):
    return lax.dot_general(a, b, (((1,), (1,)), ((), ())), preferred_element_type=F32)


def tn(a, b):
    return lax.dot_general(a, b, (((0,), (0,)), ((), ())), preferred_element_type=F32)


def greet(targets):
    barrier = pltpu.get_barrier_semaphore()
    for target in targets:
        pl.semaphore_signal(barrier, inc=1, device_id=target, device_id_type=MESH)
    return barrier


def grid_of(rows):
    return (4, 4, 2) if rows == 32 else (2, rows // 4, 2)


def terms(me, rows):
    nz, ny, nx = grid_of(rows)
    z, y, x = me // (ny * nx), (me // nx) % ny, me % nx
    along_z = [((z + d) % nz) * (ny * nx) for d in range(nz)]
    along_y = [((y + d) % ny) * nx for d in range(ny)]
    return along_z, along_y, [(x + d) % nx for d in range(nx)]


def axis_peers(me, rows):
    az, ay, ax = terms(me, rows)
    return ([{"rows": a + ay[0] + ax[0]} for a in az[1:]] + [{"rows": az[0] + a + ax[0]} for a in ay[1:]]
            + [{"rows": az[0] + ay[0] + a} for a in ax[1:]])


def peers_of(me, rows):
    lists = terms(me, rows)

    def order(n):
        return sorted(range(n), key=lambda d: -min(d, n - d))

    found = []
    for dz in order(len(lists[0])):
        for dy in order(len(lists[1])):
            for dx in order(len(lists[2])):
                if dz or dy or dx:
                    there = lists[0][dz] + lists[1][dy] + lists[2][dx]
                    back = lists[0][-dz] + lists[1][-dy] + lists[2][-dx]
                    found.append((len(found), there, back))
    return found


def chunks_of(half):
    unit = half // sum(SHARES)
    found, start = [], 0
    for share in SHARES:
        found.append((start, share * unit))
        start += share * unit
    return found


def remote(src, dst, send, recv, target):
    return pltpu.make_async_remote_copy(
        src_ref=src, dst_ref=dst, send_sem=send, recv_sem=recv, device_id=target, device_id_type=MESH
    )


def find_places(clusters, ids, place):
    blocks = ids.shape[0]
    lane = lax.broadcasted_iota(jnp.int32, (CAP, CAP), 1)
    sub = lax.broadcasted_iota(jnp.int32, (CAP, CAP), 0)
    before = jnp.where(sub < lane, F32(1), F32(0)).astype(BF16)
    names = lax.broadcasted_iota(jnp.int32, (clusters, CAP), 0)
    seen = jnp.zeros((clusters, 1), F32)
    for b in range(blocks):
        block = ids[b:b + 1, :]
        hot = jnp.where(names == block, F32(1), F32(0))
        earlier = nn(hot.astype(BF16), before) + seen
        slot = jnp.sum(hot * earlier, axis=0, keepdims=True).astype(jnp.int32)
        pair = block // 2
        odd = block - 2 * pair
        place[b:b + 1, :] = odd * (clusters // 2 * CAP) + pair * CAP + slot
        seen = seen + jnp.sum(hot, axis=1, keepdims=True)


def covariance_kernel(rows, first, *refs):
    if first:
        source, basis, names, z_out, gram_out, place, q, ids, *refs = refs
    else:
        source, q, z_out, gram_out, *refs = refs
    (slab, load_sem, qb, away, home, part, mine, theirs, y, z, z_send, z_recv, z_full, g_part, g_near, g_mine, g_far, g_all,
     near_sem, far_sem, y_sem, rs_sem, ag_sem, g_sem, round_a, round_b) = refs
    me, core, xl = lax.axis_index("rows"), lax.axis_index("core"), lax.axis_index("xl")
    near, far = {"core": 1 - core}, {"xl": 1 - xl}
    half_rows = slab.shape[0] // 2
    width = q.shape[1]
    chunks = chunks_of(half_rows)
    count = len(chunks)
    beside = axis_peers(me, rows)
    barrier = greet([near, far] + beside)

    def rows_at(h, i):
        start, size = chunks[i]
        return pl.ds(pl.multiple_of(h * half_rows + start, 8), size)

    def load(own, i):
        at = rows_at(core if own else 1 - core, i)
        return pltpu.make_async_copy(source.at[at], slab.at[at], load_sem.at[own, i])

    for i in range(count):
        load(0, i).start()
        load(1, i).start()
    if first:
        begin = pltpu.make_async_copy(basis, q, load_sem.at[0, count])
        naming = pltpu.make_async_copy(names, ids, load_sem.at[1, count])
        begin.start()
        naming.start()
        begin.wait()

    def held(own, i):
        return slab[rows_at(core if own else 1 - core, i), :]

    def scores(own, i):
        load(own, i).wait()
        return nn(held(own, i), qb[...])

    def at(ref, i):
        start, size = chunks[i]
        return ref.at[pl.ds(start, size)]

    def to_near(i):
        return remote(at(away, i), at(home, i), near_sem.at[0, i], near_sem.at[1, i], near)

    def to_far(i):
        return remote(at(mine, i), at(theirs, i), far_sem.at[0, i], far_sem.at[1, i], far)

    def y_at(own, i):
        return at(y.at[core if own else 1 - core], i)

    def share(i):
        return remote(y_at(1, i), y_at(1, i), y_sem.at[0, i], y_sem.at[1, i], near)

    def shared(i):
        return remote(y_at(0, i), y_at(0, i), y_sem.at[0, i], y_sem.at[1, i], near)

    def chip_sum(i):
        to_near(i).wait_recv()
        at(mine, i)[...] = (at(part, i)[...] + at(home, i)[...].astype(F32)).astype(BF16)
        to_far(i).start()

    def pass_on(sem):
        for peer in beside:
            pl.semaphore_signal(sem, inc=1, device_id=peer, device_id_type=MESH)

    qb[...] = q[...].astype(BF16)
    for i in range(count):
        at(away, i)[...] = scores(0, i).astype(BF16)
        if i == 0:
            at(part, i)[...] = scores(1, i)
            continue
        if i == 1:
            pl.semaphore_wait(barrier, len(beside) + 2)
            to_near(0).start()
        to_near(i).start()
        at(part, i)[...] = scores(1, i)
        chip_sum(i - 1)
        if i == 2:
            pass_on(round_a)
    chip_sum(count - 1)
    pl.semaphore_wait(round_a, len(beside))
    pass_on(round_b)
    if first:
        naming.wait()
        find_places(2 * rows, ids, place)
    pl.semaphore_wait(round_b, len(beside))

    def add(own, i, start=False):
        term = tn(y_at(own, i)[...], held(own, i))
        z[...] = term if start else z[...] + term

    for i in range(count):
        to_far(i).wait_recv()
        y_at(1, i)[...] = (at(mine, i)[...].astype(F32) + at(theirs, i)[...].astype(F32)).astype(BF16)
        share(i).start()
        add(1, i, i == 0)
        if i > 0:
            shared(i - 1).wait_recv()
            add(0, i - 1)
    shared(count - 1).wait_recv()
    add(0, count - 1)

    deep, wide = z_send.shape[2:]
    group = rows // 2
    peers = peers_of(me, rows)

    def scatter(s, slot, there):
        return remote(z_send.at[s, there], z_recv.at[s, slot], rs_sem.at[0, s, slot], rs_sem.at[1, s, slot],
                      {"rows": there})

    def gather(s, slot, owner, there):
        return remote(z_full.at[s, owner], z_full.at[s, owner], ag_sem.at[0, s, slot], ag_sem.at[1, s, slot],
                      {"rows": there})

    for s in range(NS):
        for p in range(rows):
            f, k = divmod(p, group)
            left = (f * NS + s) * wide
            z_send[s, p] = z[k * deep:(k + 1) * deep, left:left + wide].astype(BF16)
        for slot, there, _ in peers:
            scatter(s, slot, there).start()
    for s in range(NS):
        total = z_send[s, me].astype(F32)
        for slot, there, _ in reversed(peers):
            scatter(s, slot, there).wait_recv()
            total = total + z_recv[s, slot].astype(F32)
        z_full[s, me] = total.astype(BF16)
        for slot, there, _ in peers:
            gather(s, slot, me, there).start()

    low = width // 2
    part_rows = low // 2
    for s in range(NS):
        for slot, there, back in reversed(peers):
            gather(s, slot, back, there).wait_recv()
        for f in range(2):
            block = z_full[s, f * group:(f + 1) * group].reshape(width, wide)
            terms_of = (nt(block[:low], block[:low]), nt(block[low:], block[:low]), nt(block[low:], block[low:]))
            for b, term in enumerate(terms_of):
                for h in range(2):
                    line = term[h * part_rows:(h + 1) * part_rows]
                    g_part[h, b] = line if s + f == 0 else g_part[h, b] + line
    out_near = remote(g_part.at[1 - core], g_near, g_sem.at[0, 0], g_sem.at[1, 0], near)
    out_far = remote(g_mine, g_far, g_sem.at[0, 1], g_sem.at[1, 1], far)
    out_back = remote(g_all.at[core], g_all.at[core], g_sem.at[0, 2], g_sem.at[1, 2], near)
    in_back = remote(g_all.at[1 - core], g_all.at[1 - core], g_sem.at[0, 2], g_sem.at[1, 2], near)
    out_near.start()
    z_out[...] = z_full[...]
    out_near.wait_recv()
    g_mine[...] = g_part[core] + g_near[...]
    out_far.start()
    for i in range(count):
        to_near(i).wait_send()
        to_far(i).wait_send()
        share(i).wait_send()
    for s in range(NS):
        for slot, there, _ in peers:
            scatter(s, slot, there).wait_send()
            gather(s, slot, me, there).wait_send()
    out_far.wait_recv()
    g_all[core] = g_mine[...] + g_far[...]
    out_back.start()
    in_back.wait_recv()
    for h in range(2):
        for b in range(3):
            gram_out[b, h * part_rows:(h + 1) * part_rows, :] = g_all[h, b]
    out_near.wait_send()
    out_far.wait_send()
    out_back.wait_send()


def covariance(slab, q, rows, ident, ids=None):
    length, feats = slab.shape
    width = q.shape[1]
    half = length // 2
    count = len(SHARES)
    piece = (2 * width // rows, feats // (2 * NS))
    low = width // 2
    parts = (3, low // 2, low)
    dma = pltpu.SemaphoreType.DMA
    first = ids is not None
    out = [jax.ShapeDtypeStruct((NS, rows, *piece), BF16), jax.ShapeDtypeStruct((3, low, low), F32)]
    args, extra, specs = [slab, q], [], [HBM, VMEM]
    if first:
        out.append(jax.ShapeDtypeStruct(ids.shape, jnp.int32))
        args.append(ids)
        extra = [pltpu.VMEM(q.shape, F32), pltpu.VMEM(ids.shape, jnp.int32)]
        specs = [HBM] * 3
    return pl.pallas_call(
        functools.partial(covariance_kernel, rows, first),
        out_shape=out,
        in_specs=specs,
        out_specs=[VMEM] * len(out),
        scratch_shapes=extra + [
            pltpu.VMEM(slab.shape, BF16),
            dma((2, count + 1)),
            pltpu.VMEM(q.shape, BF16),
            pltpu.VMEM((half, width), BF16),
            pltpu.VMEM((half, width), BF16),
            pltpu.VMEM((half, width), F32),
            pltpu.VMEM((half, width), BF16),
            pltpu.VMEM((half, width), BF16),
            pltpu.VMEM((2, half, width), BF16),
            pltpu.VMEM((width, feats), F32),
            pltpu.VMEM((NS, rows, *piece), BF16),
            pltpu.VMEM((NS, rows, *piece), BF16),
            pltpu.VMEM((NS, rows, *piece), BF16),
            pltpu.VMEM((2, *parts), F32),
            pltpu.VMEM(parts, F32),
            pltpu.VMEM(parts, F32),
            pltpu.VMEM(parts, F32),
            pltpu.VMEM((2, *parts), F32),
            dma((2, count)),
            dma((2, count)),
            dma((2, count)),
            dma((2, NS, rows)),
            dma((2, NS, rows)),
            dma((2, 3)),
            pltpu.SemaphoreType.REGULAR,
            pltpu.SemaphoreType.REGULAR,
        ],
        compiler_params=pltpu.CompilerParams(
            collective_id=ident, has_side_effects=True, vmem_limit_bytes=(53 if first else 52) << 20
        ),
        name="covariance",
    )(*args)


def split(a):
    top = a.astype(BF16)
    return top, (a - top.astype(F32)).astype(BF16)


def fine(dot, a, b):
    (a0, a1), (b0, b1) = split(a), split(b)
    return dot(a0, b0) + (dot(a0, b1) + dot(a1, b0))


def basis_kernel(last, kept, gram, z, q_out, unit, x, e, a, state):
    low = gram.shape[1]
    n = 2 * low
    row = lax.broadcasted_iota(jnp.int32, (n, n), 0)
    col = lax.broadcasted_iota(jnp.int32, (n, n), 1)
    lower = jnp.where(row > col, F32(1), jnp.where(row == col, F32(0.5), F32(0)))
    eye = jnp.where(row == col, F32(1), F32(0))

    x[:low, :low] = gram[0]
    x[low:, :low] = gram[1]
    x[low:, low:] = gram[2]
    x[:low, low:] = gram[1].T
    g = x[...]
    diag = g * eye
    across = lax.rsqrt(jnp.sum(diag, axis=0, keepdims=True))
    down = lax.rsqrt(jnp.sum(diag, axis=1, keepdims=True))
    scaled = g * across * down
    unit[...] = scaled
    begin = scaled - eye
    e[...] = begin
    x[...] = eye
    state[0] = 0

    @pl.loop(0, STEPS)
    def _(step):
        @pl.when(state[0] == 0)
        def _():
            now = e[...]
            size = jnp.sum(now * now)
            better = x[...] - nn((now * lower).astype(BF16), x[...].astype(BF16))
            x[...] = better
            done = size < TOL * TOL
            state[0] = done.astype(jnp.int32)

            @pl.when(size > COARSE * COARSE)
            def _():
                near = better.astype(BF16)
                e[...] = nt(nn(near, unit[...].astype(BF16)).astype(BF16), near) - eye

            @pl.when(jnp.logical_not(done) & jnp.logical_not(size > COARSE * COARSE))
            def _():
                e[...] = fine(nt, fine(nn, better, unit[...]), better) - eye

    @pl.when(state[0] == 0)
    def _():
        a[...] = unit[...]
        x[...] = eye

        @pl.loop(0, n)
        def _(j):
            pick_row = row == j
            pick_col = col == j
            now = a[...]
            inv = x[...]
            a_row = jnp.sum(jnp.where(pick_row, now, 0.0), axis=0, keepdims=True)
            a_col = jnp.sum(jnp.where(pick_col, now, 0.0), axis=1, keepdims=True)
            x_row = jnp.sum(jnp.where(pick_row, inv, 0.0), axis=0, keepdims=True)
            pivot = jnp.sum(jnp.where(pick_row & pick_col, now, 0.0))
            root = jnp.sqrt(jnp.full((1, n), pivot))
            line = x_row / root
            factor = jnp.where(row[:, :1] > j, a_col / root[:, :1], 0.0)
            x[...] = jnp.where(pick_row, line, inv - factor * line)
            a[...] = now - factor * (a_row / root)

    top, rest = split(x[...] * across)
    ns, rows, _, wide = z.shape
    group = rows // 2
    for f in range(2):
        for s in range(ns):
            block = z[s, f * group:(f + 1) * group].reshape(n, wide)
            qt = nn(top, block) + nn(rest, block)
            if last:
                index = lax.broadcasted_iota(jnp.int32, (n, wide), 0)
                qt = jnp.where(index < kept[0], qt, 0.0)
            left = (f * ns + s) * wide
            q_out[left:left + wide, :] = qt.T.astype(BF16)


def new_basis(kept, gram, z, last):
    n = 2 * gram.shape[1]
    return pl.pallas_call(
        functools.partial(basis_kernel, last),
        out_shape=jax.ShapeDtypeStruct((2 * z.shape[0] * z.shape[3], n), BF16),
        in_specs=[SMEM, VMEM, VMEM],
        out_specs=VMEM,
        scratch_shapes=[pltpu.VMEM((n, n), F32)] * 4 + [pltpu.SMEM((2,), jnp.int32)],
        compiler_params=pltpu.CompilerParams(vmem_limit_bytes=24 << 20),
        name="new_basis",
    )(kept, gram, z)


def project_kernel(source, q, p_out, slab, away, home, part, keep, send, recv, p,
                   load_sem, near_sem, far_sem, p_sem):
    core, xl = lax.axis_index("core"), lax.axis_index("xl")
    near, far = {"core": 1 - core}, {"xl": 1 - xl}
    chunk = source.shape[0] // (2 * NP)
    width = q.shape[1]
    half = width // 2
    barrier = greet((near, far))

    def load(own, i):
        h = core if own else 1 - core
        at = pl.ds(pl.multiple_of(h * NP * chunk + i * chunk, chunk), chunk)
        return pltpu.make_async_copy(source.at[at], slab.at[at], load_sem.at[own, i])

    for i in range(NP):
        load(0, i).start()
        load(1, i).start()

    def scores(own, i):
        load(own, i).wait()
        h = core if own else 1 - core
        return nn(slab[pl.ds(pl.multiple_of(h * NP * chunk + i * chunk, chunk), chunk), :], q[...])

    def to_near(i):
        return remote(away.at[i], home.at[i], near_sem.at[0, i], near_sem.at[1, i], near)

    def to_far(i):
        return remote(send.at[i], recv.at[i], far_sem.at[0, i], far_sem.at[1, i], far)

    def share(i):
        return remote(p.at[core, i], p.at[core, i], p_sem.at[0, i], p_sem.at[1, i], near)

    def shared(i):
        return remote(p.at[1 - core, i], p.at[1 - core, i], p_sem.at[0, i], p_sem.at[1, i], near)

    def chip_sum(i):
        to_near(i).wait_recv()
        both = part[i] + home[i].astype(F32)
        low, high = both[:, :half], both[:, half:]
        keep[i] = jnp.where(xl == 0, low, high)
        send[i] = jnp.where(xl == 0, high, low).astype(BF16)
        to_far(i).start()

    for i in range(NP):
        away[i] = scores(0, i).astype(BF16)
        if i == 0:
            pl.semaphore_wait(barrier, 2)
        to_near(i).start()
        part[i] = scores(1, i)
        if i > 0:
            chip_sum(i - 1)
    chip_sum(NP - 1)
    for i in range(NP):
        to_far(i).wait_recv()
        p[core, i] = (keep[i] + recv[i].astype(F32)).astype(BF16)
        share(i).start()
    for i in range(NP):
        shared(i).wait_recv()
    p_out[...] = p[...].reshape(p_out.shape)
    for i in range(NP):
        to_near(i).wait_send()
        to_far(i).wait_send()
        share(i).wait_send()


def project(slab, q, ident):
    length = slab.shape[0]
    width = q.shape[1]
    chunk = length // (2 * NP)
    half = width // 2
    dma = pltpu.SemaphoreType.DMA
    return pl.pallas_call(
        project_kernel,
        out_shape=jax.ShapeDtypeStruct((length, half), BF16),
        in_specs=[HBM, VMEM],
        out_specs=VMEM,
        scratch_shapes=[
            pltpu.VMEM(slab.shape, BF16),
            pltpu.VMEM((NP, chunk, width), BF16),
            pltpu.VMEM((NP, chunk, width), BF16),
            pltpu.VMEM((NP, chunk, width), F32),
            pltpu.VMEM((NP, chunk, half), F32),
            pltpu.VMEM((NP, chunk, half), BF16),
            pltpu.VMEM((NP, chunk, half), BF16),
            pltpu.VMEM((2, NP, chunk, half), BF16),
            dma((2, NP)),
            dma((2, NP)),
            dma((2, NP)),
            dma((2, NP)),
        ],
        compiler_params=pltpu.CompilerParams(
            collective_id=ident, has_side_effects=True, vmem_limit_bytes=52 << 20
        ),
        name="project",
    )(slab, q)


def pack_kernel(place, side, p, spread, doubled):
    length, lanes = p.shape
    cols = lanes // 2
    unroll = 16
    low = lax.broadcasted_iota(jnp.int32, (length, lanes), 1) < cols
    wide = p[...].astype(F32)
    turned = pltpu.roll(wide, cols, 1)
    doubled[...] = jnp.where(low == (side[0] == 0), wide, turned)
    spread[...] = jnp.zeros_like(spread)

    @pl.loop(0, length // unroll)
    def _(step):
        for u in range(unroll):
            i = step * unroll + u
            spread[pl.ds(place[i], 1), :] = doubled[pl.ds(i, 1), :]


def spread_rows(place, side, p, rows):
    length, lanes = p.shape
    return pl.pallas_call(
        pack_kernel,
        out_shape=jax.ShapeDtypeStruct((2 * rows * CAP, lanes), F32),
        in_specs=[SMEM, SMEM, VMEM],
        out_specs=VMEM,
        scratch_shapes=[pltpu.VMEM((length, lanes), F32)],
        compiler_params=pltpu.CompilerParams(vmem_limit_bytes=16 << 20),
        name="spread_rows",
    )(place, side, p)


def exchange_kernel(rows, spread, out, buf, arrived, sem):
    me = lax.axis_index("rows")
    lanes = spread.shape[1]
    peers = peers_of(me, rows)
    barrier = greet([{"rows": there} for _, there, _ in peers])
    even = lax.broadcasted_iota(jnp.int32, (CAP, lanes), 1) < lanes // 2

    def block(r):
        start = pl.multiple_of(r * CAP, CAP)
        low = spread[pl.ds(start, CAP), :]
        high = spread[pl.ds(pl.multiple_of(start + rows * CAP, CAP), CAP), :]
        return jnp.where(even, low, high).T.astype(BF16)

    def send(slot, there, at):
        return remote(buf.at[slot], arrived.at[at], sem.at[0, slot], sem.at[1, slot], {"rows": there})

    ahead = min(12, rows - 1)
    for slot, there, _ in peers[:ahead]:
        buf[slot] = block(there)
    pl.semaphore_wait(barrier, rows - 1)
    for slot, there, _ in peers:
        if slot >= ahead:
            buf[slot] = block(there)
        send(slot, there, me).start()
    out[me] = block(me)
    for slot, there, back in reversed(peers):
        send(slot, there, back).wait_recv()
        out[back] = arrived[back]
    for slot, there, _ in peers:
        send(slot, there, me).wait_send()


def exchange(spread, rows, ident):
    lanes = spread.shape[1]
    whole = (rows, lanes, CAP)
    return pl.pallas_call(
        functools.partial(exchange_kernel, rows),
        out_shape=jax.ShapeDtypeStruct(whole, BF16),
        in_specs=[VMEM],
        out_specs=VMEM,
        scratch_shapes=[
            pltpu.VMEM((rows - 1, lanes, CAP), BF16),
            pltpu.VMEM(whole, BF16),
            pltpu.SemaphoreType.DMA((2, rows - 1)),
        ],
        compiler_params=pltpu.CompilerParams(
            collective_id=ident, has_side_effects=True, vmem_limit_bytes=16 << 20
        ),
        name="exchange",
    )(spread)


def arrange_kernel(arrived, out):
    cols = out.shape[1]
    for r in range(arrived.shape[0]):
        for h in range(2):
            out[h, :, r * CAP:(r + 1) * CAP] = arrived[r, h * cols:(h + 1) * cols, :]


def arrange(arrived):
    rows, lanes, _ = arrived.shape
    return pl.pallas_call(
        arrange_kernel,
        out_shape=jax.ShapeDtypeStruct((2, lanes // 2, rows * CAP), BF16),
        in_specs=[VMEM],
        out_specs=VMEM,
        compiler_params=pltpu.CompilerParams(vmem_limit_bytes=16 << 20),
        name="arrange",
    )(arrived)


def shards(rows, slab, basis, cluster_ids, kept):
    side = jnp.broadcast_to(lax.axis_index("core"), (1,)).astype(jnp.int32)
    z, gram, place = covariance(slab, basis, rows, 0, cluster_ids.reshape(-1, CAP))
    for step in range(1, ITERS):
        q = new_basis(kept, gram, z, False)
        z, gram = covariance(slab, q, rows, step)
    q = new_basis(kept, gram, z, True)
    p = project(slab, q, ITERS)
    spread = spread_rows(place.reshape(-1), side, p, rows)
    return jnp.swapaxes(arrange(exchange(spread, rows, ITERS + 1)), 1, 2)


def solution(mesh):
    rows = mesh.shape["rows"]
    torus = Mesh(mesh.devices.reshape(rows, 2, 2), ("rows", "xl", "core"))
    placed = (P("rows", FEAT), P(FEAT, None), P("rows", None), P())
    return jax.shard_map(
        functools.partial(shards, rows), mesh=torus, in_specs=placed,
        out_specs=P("rows", None, FEAT), check_vma=False,
    )
```

```python
import functools

import jax
import jax.numpy as jnp
from jax import lax
from jax.experimental import pallas as pl
from jax.experimental.pallas import tpu as pltpu
from jax.sharding import Mesh
from jax.sharding import PartitionSpec as P

ITERS = 2
CAP = 128
SHARES = (1, 2, 2, 2, 2, 2, 1)
NS = 1
GRANT = 44
TOL = 2e-3
COARSE = 1.0
STEPS = 14
F32 = jnp.float32
BF16 = jnp.bfloat16
MESH = pl.DeviceIdType.MESH
VMEM = pl.BlockSpec(memory_space=pltpu.VMEM)
SMEM = pl.BlockSpec(memory_space=pltpu.SMEM)
HBM = pl.BlockSpec(memory_space=pltpu.HBM)
FEAT = ("xl", "core")


def nn(a, b):
    return lax.dot_general(a, b, (((1,), (0,)), ((), ())), preferred_element_type=F32)


def nt(a, b):
    return lax.dot_general(a, b, (((1,), (1,)), ((), ())), preferred_element_type=F32)


def tn(a, b):
    return lax.dot_general(a, b, (((0,), (0,)), ((), ())), preferred_element_type=F32)


def greet(targets):
    barrier = pltpu.get_barrier_semaphore()
    for target in targets:
        pl.semaphore_signal(barrier, inc=1, device_id=target, device_id_type=MESH)
    return barrier


def grid_of(rows):
    return (4, 4, 2) if rows == 32 else (2, rows // 4, 2)


def terms(me, rows):
    nz, ny, nx = grid_of(rows)
    z, y, x = me // (ny * nx), (me // nx) % ny, me % nx
    along_z = [((z + d) % nz) * (ny * nx) for d in range(nz)]
    along_y = [((y + d) % ny) * nx for d in range(ny)]
    return along_z, along_y, [(x + d) % nx for d in range(nx)]


def axis_peers(me, rows):
    az, ay, ax = terms(me, rows)
    return ([{"rows": a + ay[0] + ax[0]} for a in az[1:]] + [{"rows": az[0] + a + ax[0]} for a in ay[1:]]
            + [{"rows": az[0] + ay[0] + a} for a in ax[1:]])


def peers_of(me, rows):
    lists = terms(me, rows)

    def order(n):
        return sorted(range(n), key=lambda d: -min(d, n - d))

    found = []
    for dz in order(len(lists[0])):
        for dy in order(len(lists[1])):
            for dx in order(len(lists[2])):
                if dz or dy or dx:
                    there = lists[0][dz] + lists[1][dy] + lists[2][dx]
                    back = lists[0][-dz] + lists[1][-dy] + lists[2][-dx]
                    found.append((len(found), there, back))
    return found


def chunks_of(half):
    unit = half // sum(SHARES)
    found, start = [], 0
    for share in SHARES:
        found.append((start, share * unit))
        start += share * unit
    return found


def remote(src, dst, send, recv, target):
    return pltpu.make_async_remote_copy(
        src_ref=src, dst_ref=dst, send_sem=send, recv_sem=recv, device_id=target, device_id_type=MESH
    )


def find_places(clusters, ids, place):
    blocks = ids.shape[0]
    lane = lax.broadcasted_iota(jnp.int32, (CAP, CAP), 1)
    sub = lax.broadcasted_iota(jnp.int32, (CAP, CAP), 0)
    before = jnp.where(sub < lane, F32(1), F32(0)).astype(BF16)
    names = lax.broadcasted_iota(jnp.int32, (clusters, CAP), 0)
    seen = jnp.zeros((clusters, 1), F32)
    for b in range(blocks):
        block = ids[b:b + 1, :]
        hot = jnp.where(names == block, F32(1), F32(0))
        earlier = nn(hot.astype(BF16), before) + seen
        slot = jnp.sum(hot * earlier, axis=0, keepdims=True).astype(jnp.int32)
        pair = block // 2
        odd = block - 2 * pair
        place[b:b + 1, :] = odd * (clusters // 2 * CAP) + pair * CAP + slot
        seen = seen + jnp.sum(hot, axis=1, keepdims=True)


def covariance_kernel(rows, first, *refs):
    if first:
        source, basis, names, z_out, gram_out, place, slab, q, ids, load_sem, *refs = refs
    else:
        slab, q, z_out, gram_out, *refs = refs
    (qb, away, home, part, mine, theirs, y, z, z_send, z_recv, z_full, g_part, g_near, g_mine, g_far, g_all,
     near_sem, far_sem, y_sem, rs_sem, ag_sem, g_sem, round_a, round_b) = refs
    me, core, xl = lax.axis_index("rows"), lax.axis_index("core"), lax.axis_index("xl")
    near, far = {"core": 1 - core}, {"xl": 1 - xl}
    half_rows = slab.shape[0] // 2
    width = q.shape[1]
    chunks = chunks_of(half_rows)
    count = len(chunks)
    beside = axis_peers(me, rows)
    barrier = greet([near, far] + beside)

    def rows_at(h, i):
        start, size = chunks[i]
        return pl.ds(pl.multiple_of(h * half_rows + start, 8), size)

    def load(own, i):
        at = rows_at(core if own else 1 - core, i)
        return pltpu.make_async_copy(source.at[at], slab.at[at], load_sem.at[own, i])

    if first:
        for i in range(count):
            load(0, i).start()
            load(1, i).start()
        begin = pltpu.make_async_copy(basis, q, load_sem.at[0, count])
        naming = pltpu.make_async_copy(names, ids, load_sem.at[1, count])
        begin.start()
        naming.start()
        begin.wait()

    def held(own, i):
        return slab[rows_at(core if own else 1 - core, i), :]

    def scores(own, i):
        if first:
            load(own, i).wait()
        return nn(held(own, i), qb[...])

    def at(ref, i):
        start, size = chunks[i]
        return ref.at[pl.ds(start, size)]

    def to_near(i):
        return remote(at(away, i), at(home, i), near_sem.at[0, i], near_sem.at[1, i], near)

    def to_far(i):
        return remote(at(mine, i), at(theirs, i), far_sem.at[0, i], far_sem.at[1, i], far)

    def y_at(own, i):
        return at(y.at[core if own else 1 - core], i)

    def share(i):
        return remote(y_at(1, i), y_at(1, i), y_sem.at[0, i], y_sem.at[1, i], near)

    def shared(i):
        return remote(y_at(0, i), y_at(0, i), y_sem.at[0, i], y_sem.at[1, i], near)

    def chip_sum(i):
        to_near(i).wait_recv()
        at(mine, i)[...] = (at(part, i)[...] + at(home, i)[...].astype(F32)).astype(BF16)
        to_far(i).start()

    def pass_on(sem):
        for peer in beside:
            pl.semaphore_signal(sem, inc=1, device_id=peer, device_id_type=MESH)

    qb[...] = q[...].astype(BF16)
    for i in range(count):
        at(away, i)[...] = scores(0, i).astype(BF16)
        if i == 0:
            at(part, i)[...] = scores(1, i)
            continue
        if i == 1:
            pl.semaphore_wait(barrier, len(beside) + 2)
            to_near(0).start()
        to_near(i).start()
        at(part, i)[...] = scores(1, i)
        chip_sum(i - 1)
        if i == 2:
            pass_on(round_a)
    chip_sum(count - 1)
    pl.semaphore_wait(round_a, len(beside))
    pass_on(round_b)
    if first:
        naming.wait()
        find_places(2 * rows, ids, place)
    pl.semaphore_wait(round_b, len(beside))

    def add(own, i, start=False):
        term = tn(y_at(own, i)[...], held(own, i))
        z[...] = term if start else z[...] + term

    for i in range(count):
        to_far(i).wait_recv()
        y_at(1, i)[...] = (at(mine, i)[...].astype(F32) + at(theirs, i)[...].astype(F32)).astype(BF16)
        share(i).start()
        add(1, i, i == 0)
        if i > 0:
            shared(i - 1).wait_recv()
            add(0, i - 1)
    shared(count - 1).wait_recv()
    add(0, count - 1)

    deep, wide = z_send.shape[2:]
    group = rows // 2
    peers = peers_of(me, rows)

    def scatter(s, slot, there):
        return remote(z_send.at[s, there], z_recv.at[s, slot], rs_sem.at[0, s, slot], rs_sem.at[1, s, slot],
                      {"rows": there})

    def gather(s, slot, owner, there):
        return remote(z_full.at[s, owner], z_full.at[s, owner], ag_sem.at[0, s, slot], ag_sem.at[1, s, slot],
                      {"rows": there})

    for s in range(NS):
        for p in range(rows):
            f, k = divmod(p, group)
            left = (f * NS + s) * wide
            z_send[s, p] = z[k * deep:(k + 1) * deep, left:left + wide].astype(BF16)
        for slot, there, _ in peers:
            scatter(s, slot, there).start()
    for s in range(NS):
        total = z_send[s, me].astype(F32)
        for slot, there, _ in reversed(peers):
            scatter(s, slot, there).wait_recv()
            total = total + z_recv[s, slot].astype(F32)
        z_full[s, me] = total.astype(BF16)
        for slot, there, _ in peers:
            gather(s, slot, me, there).start()

    low = width // 2
    part_rows = low // 2
    for s in range(NS):
        for slot, there, back in reversed(peers):
            gather(s, slot, back, there).wait_recv()
        for f in range(2):
            block = z_full[s, f * group:(f + 1) * group].reshape(width, wide)
            terms_of = (nt(block[:low], block[:low]), nt(block[low:], block[:low]), nt(block[low:], block[low:]))
            for b, term in enumerate(terms_of):
                for h in range(2):
                    line = term[h * part_rows:(h + 1) * part_rows]
                    g_part[h, b] = line if s + f == 0 else g_part[h, b] + line
    out_near = remote(g_part.at[1 - core], g_near, g_sem.at[0, 0], g_sem.at[1, 0], near)
    out_far = remote(g_mine, g_far, g_sem.at[0, 1], g_sem.at[1, 1], far)
    out_back = remote(g_all.at[core], g_all.at[core], g_sem.at[0, 2], g_sem.at[1, 2], near)
    in_back = remote(g_all.at[1 - core], g_all.at[1 - core], g_sem.at[0, 2], g_sem.at[1, 2], near)
    out_near.start()
    z_out[...] = z_full[...]
    out_near.wait_recv()
    g_mine[...] = g_part[core] + g_near[...]
    out_far.start()
    for i in range(count):
        to_near(i).wait_send()
        to_far(i).wait_send()
        share(i).wait_send()
    for s in range(NS):
        for slot, there, _ in peers:
            scatter(s, slot, there).wait_send()
            gather(s, slot, me, there).wait_send()
    out_far.wait_recv()
    g_all[core] = g_mine[...] + g_far[...]
    out_back.start()
    in_back.wait_recv()
    for h in range(2):
        for b in range(3):
            gram_out[b, h * part_rows:(h + 1) * part_rows, :] = g_all[h, b]
    out_near.wait_send()
    out_far.wait_send()
    out_back.wait_send()


def covariance(slab, q, rows, ident, ids=None):
    length, feats = slab.shape
    width = q.shape[1]
    half = length // 2
    count = len(SHARES)
    piece = (2 * width // rows, feats // (2 * NS))
    low = width // 2
    parts = (3, low // 2, low)
    dma = pltpu.SemaphoreType.DMA
    first = ids is not None
    out = [jax.ShapeDtypeStruct((NS, rows, *piece), BF16), jax.ShapeDtypeStruct((3, low, low), F32)]
    args, extra, specs = [slab, q], [], [VMEM, VMEM]
    if first:
        out += [jax.ShapeDtypeStruct(ids.shape, jnp.int32), jax.ShapeDtypeStruct(slab.shape, BF16)]
        args.append(ids)
        extra = [pltpu.VMEM(q.shape, F32), pltpu.VMEM(ids.shape, jnp.int32), dma((2, count + 1))]
        specs = [HBM] * 3
    return pl.pallas_call(
        functools.partial(covariance_kernel, rows, first),
        out_shape=out,
        in_specs=specs,
        out_specs=[VMEM] * len(out),
        scratch_shapes=extra + [
            pltpu.VMEM(q.shape, BF16),
            pltpu.VMEM((half, width), BF16),
            pltpu.VMEM((half, width), BF16),
            pltpu.VMEM((half, width), F32),
            pltpu.VMEM((half, width), BF16),
            pltpu.VMEM((half, width), BF16),
            pltpu.VMEM((2, half, width), BF16),
            pltpu.VMEM((width, feats), F32),
            pltpu.VMEM((NS, rows, *piece), BF16),
            pltpu.VMEM((NS, rows, *piece), BF16),
            pltpu.VMEM((NS, rows, *piece), BF16),
            pltpu.VMEM((2, *parts), F32),
            pltpu.VMEM(parts, F32),
            pltpu.VMEM(parts, F32),
            pltpu.VMEM(parts, F32),
            pltpu.VMEM((2, *parts), F32),
            dma((2, count)),
            dma((2, count)),
            dma((2, count)),
            dma((2, NS, rows)),
            dma((2, NS, rows)),
            dma((2, 3)),
            pltpu.SemaphoreType.REGULAR,
            pltpu.SemaphoreType.REGULAR,
        ],
        compiler_params=pltpu.CompilerParams(
            collective_id=ident, has_side_effects=True, vmem_limit_bytes=(GRANT if first else 32) << 20
        ),
        name="covariance",
    )(*args)


def split(a):
    top = a.astype(BF16)
    return top, (a - top.astype(F32)).astype(BF16)


def fine(dot, a, b):
    (a0, a1), (b0, b1) = split(a), split(b)
    return dot(a0, b0) + (dot(a0, b1) + dot(a1, b0))


def basis_kernel(last, kept, gram, z, q_out, unit, x, e, a, state):
    low = gram.shape[1]
    n = 2 * low
    row = lax.broadcasted_iota(jnp.int32, (n, n), 0)
    col = lax.broadcasted_iota(jnp.int32, (n, n), 1)
    lower = jnp.where(row > col, F32(1), jnp.where(row == col, F32(0.5), F32(0)))
    eye = jnp.where(row == col, F32(1), F32(0))

    x[:low, :low] = gram[0]
    x[low:, :low] = gram[1]
    x[low:, low:] = gram[2]
    x[:low, low:] = gram[1].T
    g = x[...]
    diag = g * eye
    across = lax.rsqrt(jnp.sum(diag, axis=0, keepdims=True))
    down = lax.rsqrt(jnp.sum(diag, axis=1, keepdims=True))
    scaled = g * across * down
    unit[...] = scaled
    begin = scaled - eye
    e[...] = begin
    x[...] = eye
    state[0] = 0

    @pl.loop(0, STEPS)
    def _(step):
        @pl.when(state[0] == 0)
        def _():
            now = e[...]
            size = jnp.sum(now * now)
            better = x[...] - nn((now * lower).astype(BF16), x[...].astype(BF16))
            x[...] = better
            done = size < TOL * TOL
            state[0] = done.astype(jnp.int32)

            @pl.when(size > COARSE * COARSE)
            def _():
                near = better.astype(BF16)
                e[...] = nt(nn(near, unit[...].astype(BF16)).astype(BF16), near) - eye

            @pl.when(jnp.logical_not(done) & jnp.logical_not(size > COARSE * COARSE))
            def _():
                e[...] = fine(nt, fine(nn, better, unit[...]), better) - eye

    @pl.when(state[0] == 0)
    def _():
        a[...] = unit[...]
        x[...] = eye

        @pl.loop(0, n)
        def _(j):
            pick_row = row == j
            pick_col = col == j
            now = a[...]
            inv = x[...]
            a_row = jnp.sum(jnp.where(pick_row, now, 0.0), axis=0, keepdims=True)
            a_col = jnp.sum(jnp.where(pick_col, now, 0.0), axis=1, keepdims=True)
            x_row = jnp.sum(jnp.where(pick_row, inv, 0.0), axis=0, keepdims=True)
            pivot = jnp.sum(jnp.where(pick_row & pick_col, now, 0.0))
            root = jnp.sqrt(jnp.full((1, n), pivot))
            line = x_row / root
            factor = jnp.where(row[:, :1] > j, a_col / root[:, :1], 0.0)
            x[...] = jnp.where(pick_row, line, inv - factor * line)
            a[...] = now - factor * (a_row / root)

    top, rest = split(x[...] * across)
    ns, rows, _, wide = z.shape
    group = rows // 2
    for f in range(2):
        for s in range(ns):
            block = z[s, f * group:(f + 1) * group].reshape(n, wide)
            qt = nn(top, block) + nn(rest, block)
            if last:
                index = lax.broadcasted_iota(jnp.int32, (n, wide), 0)
                qt = jnp.where(index < kept[0], qt, 0.0)
            left = (f * ns + s) * wide
            q_out[left:left + wide, :] = qt.T.astype(BF16)


def new_basis(kept, gram, z, last):
    n = 2 * gram.shape[1]
    return pl.pallas_call(
        functools.partial(basis_kernel, last),
        out_shape=jax.ShapeDtypeStruct((2 * z.shape[0] * z.shape[3], n), BF16),
        in_specs=[SMEM, VMEM, VMEM],
        out_specs=VMEM,
        scratch_shapes=[pltpu.VMEM((n, n), F32)] * 4 + [pltpu.SMEM((2,), jnp.int32)],
        compiler_params=pltpu.CompilerParams(vmem_limit_bytes=24 << 20),
        name="new_basis",
    )(kept, gram, z)


def project_kernel(slab, q, p_out, away, home, keep, send, recv, p, near_sem, far_sem, p_sem):
    core, xl = lax.axis_index("core"), lax.axis_index("xl")
    near, far = {"core": 1 - core}, {"xl": 1 - xl}
    half_rows = slab.shape[0] // 2
    half = q.shape[1] // 2
    chunks = chunks_of(half_rows)
    count = len(chunks)
    barrier = greet((near, far))

    def scores(own, i):
        start, size = chunks[i]
        h = core if own else 1 - core
        return nn(slab[pl.ds(pl.multiple_of(h * half_rows + start, 8), size), :], q[...])

    def at(ref, i):
        start, size = chunks[i]
        return ref.at[pl.ds(start, size)]

    def p_at(own, i):
        return at(p.at[core if own else 1 - core], i)

    def to_near(i):
        return remote(at(away, i), at(home, i), near_sem.at[0, i], near_sem.at[1, i], near)

    def to_far(i):
        return remote(at(send, i), at(recv, i), far_sem.at[0, i], far_sem.at[1, i], far)

    def share(i):
        return remote(p_at(1, i), p_at(1, i), p_sem.at[0, i], p_sem.at[1, i], near)

    def shared(i):
        return remote(p_at(0, i), p_at(0, i), p_sem.at[0, i], p_sem.at[1, i], near)

    def chip_sum(i, part):
        to_near(i).wait_recv()
        both = part + at(home, i)[...].astype(F32)
        low, high = both[:, :half], both[:, half:]
        at(send, i)[...] = jnp.where(xl == 0, high, low).astype(BF16)
        to_far(i).start()
        at(keep, i)[...] = jnp.where(xl == 0, low, high)

    for i in range(2):
        at(away, i)[...] = scores(0, i).astype(BF16)
    own = [scores(1, 0)]
    pl.semaphore_wait(barrier, 2)
    to_near(0).start()
    to_near(1).start()
    for i in range(count):
        if i + 2 < count:
            at(away, i + 2)[...] = scores(0, i + 2).astype(BF16)
            to_near(i + 2).start()
        if i + 1 < count:
            own.append(scores(1, i + 1))
        chip_sum(i, own[i])
    for i in range(count):
        to_far(i).wait_recv()
        p_at(1, i)[...] = (at(keep, i)[...] + at(recv, i)[...].astype(F32)).astype(BF16)
        share(i).start()
    for i in range(count):
        to_near(i).wait_send()
        to_far(i).wait_send()
    for i in range(count):
        shared(i).wait_recv()
    p_out[...] = p[...].reshape(p_out.shape)
    for i in range(count):
        share(i).wait_send()


def project(slab, q, ident):
    length = slab.shape[0]
    width = q.shape[1]
    half = width // 2
    dma = pltpu.SemaphoreType.DMA((2, len(SHARES)))
    return pl.pallas_call(
        project_kernel,
        out_shape=jax.ShapeDtypeStruct((length, half), BF16),
        in_specs=[VMEM, VMEM],
        out_specs=VMEM,
        scratch_shapes=[
            pltpu.VMEM((length // 2, width), BF16),
            pltpu.VMEM((length // 2, width), BF16),
            pltpu.VMEM((length // 2, half), F32),
            pltpu.VMEM((length // 2, half), BF16),
            pltpu.VMEM((length // 2, half), BF16),
            pltpu.VMEM((2, length // 2, half), BF16),
            dma,
            dma,
            dma,
        ],
        compiler_params=pltpu.CompilerParams(
            collective_id=ident, has_side_effects=True, vmem_limit_bytes=24 << 20
        ),
        name="project",
    )(slab, q)


def pack_kernel(place, side, p, spread, doubled):
    length, lanes = p.shape
    cols = lanes // 2
    unroll = 16
    low = lax.broadcasted_iota(jnp.int32, (length, lanes), 1) < cols
    wide = p[...].astype(F32)
    turned = pltpu.roll(wide, cols, 1)
    doubled[...] = jnp.where(low == (side[0] == 0), wide, turned)
    spread[...] = jnp.zeros_like(spread)

    @pl.loop(0, length // unroll)
    def _(step):
        for u in range(unroll):
            i = step * unroll + u
            spread[pl.ds(place[i], 1), :] = doubled[pl.ds(i, 1), :]


def spread_rows(place, side, p, rows):
    length, lanes = p.shape
    return pl.pallas_call(
        pack_kernel,
        out_shape=jax.ShapeDtypeStruct((2 * rows * CAP, lanes), F32),
        in_specs=[SMEM, SMEM, VMEM],
        out_specs=VMEM,
        scratch_shapes=[pltpu.VMEM((length, lanes), F32)],
        compiler_params=pltpu.CompilerParams(vmem_limit_bytes=16 << 20),
        name="spread_rows",
    )(place, side, p)


def exchange_kernel(rows, spread, out, buf, arrived, sem):
    me = lax.axis_index("rows")
    lanes = spread.shape[1]
    peers = peers_of(me, rows)
    barrier = greet([{"rows": there} for _, there, _ in peers])
    even = lax.broadcasted_iota(jnp.int32, (CAP, lanes), 1) < lanes // 2

    def block(r):
        start = pl.multiple_of(r * CAP, CAP)
        low = spread[pl.ds(start, CAP), :]
        high = spread[pl.ds(pl.multiple_of(start + rows * CAP, CAP), CAP), :]
        return jnp.where(even, low, high).T.astype(BF16)

    def send(slot, there, at):
        return remote(buf.at[slot], arrived.at[at], sem.at[0, slot], sem.at[1, slot], {"rows": there})

    ahead = min(12, rows - 1)
    for slot, there, _ in peers[:ahead]:
        buf[slot] = block(there)
    pl.semaphore_wait(barrier, rows - 1)
    for slot, there, _ in peers:
        if slot >= ahead:
            buf[slot] = block(there)
        send(slot, there, me).start()
    out[me] = block(me)
    for slot, there, back in reversed(peers):
        send(slot, there, back).wait_recv()
        out[back] = arrived[back]
    for slot, there, _ in peers:
        send(slot, there, me).wait_send()


def exchange(spread, rows, ident):
    lanes = spread.shape[1]
    whole = (rows, lanes, CAP)
    return pl.pallas_call(
        functools.partial(exchange_kernel, rows),
        out_shape=jax.ShapeDtypeStruct(whole, BF16),
        in_specs=[VMEM],
        out_specs=VMEM,
        scratch_shapes=[
            pltpu.VMEM((rows - 1, lanes, CAP), BF16),
            pltpu.VMEM(whole, BF16),
            pltpu.SemaphoreType.DMA((2, rows - 1)),
        ],
        compiler_params=pltpu.CompilerParams(
            collective_id=ident, has_side_effects=True, vmem_limit_bytes=16 << 20
        ),
        name="exchange",
    )(spread)


def arrange_kernel(arrived, out):
    cols = out.shape[1]
    for r in range(arrived.shape[0]):
        for h in range(2):
            out[h, :, r * CAP:(r + 1) * CAP] = arrived[r, h * cols:(h + 1) * cols, :]


def arrange(arrived):
    rows, lanes, _ = arrived.shape
    return pl.pallas_call(
        arrange_kernel,
        out_shape=jax.ShapeDtypeStruct((2, lanes // 2, rows * CAP), BF16),
        in_specs=[VMEM],
        out_specs=VMEM,
        compiler_params=pltpu.CompilerParams(vmem_limit_bytes=16 << 20),
        name="arrange",
    )(arrived)


def shards(rows, slab, basis, cluster_ids, kept):
    side = jnp.broadcast_to(lax.axis_index("core"), (1,)).astype(jnp.int32)
    z, gram, place, slab = covariance(slab, basis, rows, 0, cluster_ids.reshape(-1, CAP))
    for step in range(1, ITERS):
        q = new_basis(kept, gram, z, False)
        z, gram = covariance(slab, q, rows, step)
    q = new_basis(kept, gram, z, True)
    p = project(slab, q, ITERS)
    spread = spread_rows(place.reshape(-1), side, p, rows)
    return jnp.swapaxes(arrange(exchange(spread, rows, ITERS + 1)), 1, 2)


def solution(mesh):
    rows = mesh.shape["rows"]
    torus = Mesh(mesh.devices.reshape(rows, 2, 2), ("rows", "xl", "core"))
    placed = (P("rows", FEAT), P(FEAT, None), P("rows", None), P())
    return jax.shard_map(
        functools.partial(shards, rows), mesh=torus, in_specs=placed,
        out_specs=P("rows", None, FEAT), check_vma=False,
    )
```

```python
import functools

import jax
import jax.numpy as jnp
from jax import lax
from jax.experimental import pallas as pl
from jax.experimental.pallas import tpu as pltpu
from jax.sharding import Mesh
from jax.sharding import PartitionSpec as P

ITERS = 2
CAP = 128
SHARES = (1, 2, 2, 2, 2, 2, 1)
NS = 1
GRANT = 44
TOL = 2e-3
COARSE = 1.0
STEPS = 14
F32 = jnp.float32
BF16 = jnp.bfloat16
MESH = pl.DeviceIdType.MESH
VMEM = pl.BlockSpec(memory_space=pltpu.VMEM)
SMEM = pl.BlockSpec(memory_space=pltpu.SMEM)
HBM = pl.BlockSpec(memory_space=pltpu.HBM)
FEAT = ("xl", "core")


def nn(a, b):
    return lax.dot_general(a, b, (((1,), (0,)), ((), ())), preferred_element_type=F32)


def nt(a, b):
    return lax.dot_general(a, b, (((1,), (1,)), ((), ())), preferred_element_type=F32)


def tn(a, b):
    return lax.dot_general(a, b, (((0,), (0,)), ((), ())), preferred_element_type=F32)


def greet(targets):
    barrier = pltpu.get_barrier_semaphore()
    for target in targets:
        pl.semaphore_signal(barrier, inc=1, device_id=target, device_id_type=MESH)
    return barrier


def grid_of(rows):
    return (4, 4, 2) if rows == 32 else (2, rows // 4, 2)


def terms(me, rows):
    nz, ny, nx = grid_of(rows)
    z, y, x = me // (ny * nx), (me // nx) % ny, me % nx
    along_z = [((z + d) % nz) * (ny * nx) for d in range(nz)]
    along_y = [((y + d) % ny) * nx for d in range(ny)]
    return along_z, along_y, [(x + d) % nx for d in range(nx)]


def axis_peers(me, rows):
    az, ay, ax = terms(me, rows)
    return ([{"rows": a + ay[0] + ax[0]} for a in az[1:]] + [{"rows": az[0] + a + ax[0]} for a in ay[1:]]
            + [{"rows": az[0] + ay[0] + a} for a in ax[1:]])


def peers_of(me, rows):
    lists = terms(me, rows)

    def order(n):
        return sorted(range(n), key=lambda d: -min(d, n - d))

    found = []
    for dz in order(len(lists[0])):
        for dy in order(len(lists[1])):
            for dx in order(len(lists[2])):
                if dz or dy or dx:
                    there = lists[0][dz] + lists[1][dy] + lists[2][dx]
                    back = lists[0][-dz] + lists[1][-dy] + lists[2][-dx]
                    found.append((len(found), there, back))
    return found


def chunks_of(half):
    unit = half // sum(SHARES)
    found, start = [], 0
    for share in SHARES:
        found.append((start, share * unit))
        start += share * unit
    return found


def remote(src, dst, send, recv, target):
    return pltpu.make_async_remote_copy(
        src_ref=src, dst_ref=dst, send_sem=send, recv_sem=recv, device_id=target, device_id_type=MESH
    )


def find_places(clusters, ids, place):
    blocks = ids.shape[0]
    lane = lax.broadcasted_iota(jnp.int32, (CAP, CAP), 1)
    sub = lax.broadcasted_iota(jnp.int32, (CAP, CAP), 0)
    before = jnp.where(sub < lane, F32(1), F32(0)).astype(BF16)
    names = lax.broadcasted_iota(jnp.int32, (clusters, CAP), 0)
    seen = jnp.zeros((clusters, 1), F32)
    for b in range(blocks):
        block = ids[b:b + 1, :]
        hot = jnp.where(names == block, F32(1), F32(0))
        earlier = nn(hot.astype(BF16), before) + seen
        slot = jnp.sum(hot * earlier, axis=0, keepdims=True).astype(jnp.int32)
        pair = block // 2
        odd = block - 2 * pair
        place[b:b + 1, :] = odd * (clusters // 2 * CAP) + pair * CAP + slot
        seen = seen + jnp.sum(hot, axis=1, keepdims=True)


def covariance_kernel(rows, kind, *refs):
    first, joint = kind == "first", kind == "joint"
    if first:
        source, basis, names, z_out, place, slab, q, ids, load_sem, *refs = refs
    elif joint:
        slab, z_in, z_out, gram_out, gram_in, size_out, unit, *refs = refs
    else:
        slab, q, z_out, gram_out, *refs = refs
    (qb, away, home, part, mine, theirs, y, z, z_send, z_recv, z_full, g_part, g_near, g_mine, g_far, g_all,
     near_sem, far_sem, y_sem, rs_sem, ag_sem, g_sem, round_a, round_b) = refs
    me, core, xl = lax.axis_index("rows"), lax.axis_index("core"), lax.axis_index("xl")
    near, far = {"core": 1 - core}, {"xl": 1 - xl}
    half_rows = slab.shape[0] // 2
    width = qb.shape[1]
    chunks = chunks_of(half_rows)
    count = len(chunks)
    deep, wide = z_send.shape[2:]
    group = rows // 2
    low = width // 2
    part_rows = low // 2
    beside = axis_peers(me, rows)
    barrier = greet([near, far] + beside)

    def rows_at(h, i):
        start, size = chunks[i]
        return pl.ds(pl.multiple_of(h * half_rows + start, 8), size)

    def load(own, i):
        at = rows_at(core if own else 1 - core, i)
        return pltpu.make_async_copy(source.at[at], slab.at[at], load_sem.at[own, i])

    if first:
        for i in range(count):
            load(0, i).start()
            load(1, i).start()
        begin = pltpu.make_async_copy(basis, q, load_sem.at[0, count])
        naming = pltpu.make_async_copy(names, ids, load_sem.at[1, count])
        begin.start()
        naming.start()
        begin.wait()

    def held(own, i):
        return slab[rows_at(core if own else 1 - core, i), :]

    def scores(own, i):
        if first:
            load(own, i).wait()
        return nn(held(own, i), qb[...])

    def at(ref, i):
        start, size = chunks[i]
        return ref.at[pl.ds(start, size)]

    def to_near(i):
        return remote(at(away, i), at(home, i), near_sem.at[0, i], near_sem.at[1, i], near)

    def to_far(i):
        return remote(at(mine, i), at(theirs, i), far_sem.at[0, i], far_sem.at[1, i], far)

    def y_at(own, i):
        return at(y.at[core if own else 1 - core], i)

    def share(i):
        return remote(y_at(1, i), y_at(1, i), y_sem.at[0, i], y_sem.at[1, i], near)

    def shared(i):
        return remote(y_at(0, i), y_at(0, i), y_sem.at[0, i], y_sem.at[1, i], near)

    def chip_sum(i):
        to_near(i).wait_recv()
        at(mine, i)[...] = (at(part, i)[...] + at(home, i)[...].astype(F32)).astype(BF16)
        to_far(i).start()

    def pass_on(sem):
        for peer in beside:
            pl.semaphore_signal(sem, inc=1, device_id=peer, device_id_type=MESH)

    def gram_terms(e, pieces, s):
        for f in range(2):
            block = pieces[s, f * group:(f + 1) * group].reshape(width, wide)
            terms_of = (nt(block[:low], block[:low]), nt(block[low:], block[:low]), nt(block[low:], block[low:]))
            for b, term in enumerate(terms_of):
                for h in range(2):
                    line = term[h * part_rows:(h + 1) * part_rows]
                    g_part[e, h, b] = line if s + f == 0 else g_part[e, h, b] + line

    def gram_copy(e, i, src, dst, target):
        return remote(src, dst, g_sem.at[0, e, i], g_sem.at[1, e, i], target)

    def gram_near(e):
        return gram_copy(e, 0, g_part.at[e, 1 - core], g_near.at[e], near)

    def gram_far(e):
        return gram_copy(e, 1, g_mine.at[e], g_far.at[e], far)

    def gram_back(e, c):
        return gram_copy(e, 2, g_all.at[e, c], g_all.at[e, c], near)

    def gram_to_far(e):
        gram_near(e).wait_recv()
        g_mine[e] = g_part[e, core] + g_near[e]
        gram_far(e).start()

    def gram_finish(e, out):
        gram_far(e).wait_recv()
        g_all[e, core] = g_mine[e] + g_far[e]
        gram_back(e, core).start()
        gram_back(e, 1 - core).wait_recv()
        for h in range(2):
            for b in range(3):
                out[b, h * part_rows:(h + 1) * part_rows, :] = g_all[e, h, b]
        gram_near(e).wait_send()
        gram_far(e).wait_send()
        gram_back(e, core).wait_send()

    if joint:
        for s in range(NS):
            gram_terms(1, z_in, s)
            for f in range(2):
                left = (f * NS + s) * wide
                qb[left:left + wide, :] = z_in[s, f * group:(f + 1) * group].reshape(width, wide).T
    else:
        qb[...] = q[...].astype(BF16)
    for i in range(count):
        at(away, i)[...] = scores(0, i).astype(BF16)
        if i == 0:
            at(part, i)[...] = scores(1, i)
            continue
        if i == 1:
            pl.semaphore_wait(barrier, len(beside) + 2)
            if joint:
                gram_near(1).start()
            to_near(0).start()
        to_near(i).start()
        at(part, i)[...] = scores(1, i)
        if joint and i == 1:
            gram_to_far(1)
        chip_sum(i - 1)
        if i == 2:
            pass_on(round_a)
    chip_sum(count - 1)
    pl.semaphore_wait(round_a, len(beside))
    pass_on(round_b)
    if first:
        naming.wait()
        find_places(2 * rows, ids, place)
    pl.semaphore_wait(round_b, len(beside))
    if joint:
        gram_finish(1, gram_in)
        inverse, last_size = steps_for(gram_in, unit)
        top, rest = split(inverse)
        size_out[...] = jnp.full(size_out.shape, last_size)

    def add(own, i, start=False):
        term = tn(y_at(own, i)[...], held(own, i))
        z[...] = term if start else z[...] + term

    for i in range(count):
        to_far(i).wait_recv()
        both = (at(mine, i)[...].astype(F32) + at(theirs, i)[...].astype(F32)).astype(BF16)
        y_at(1, i)[...] = (nt(both, top) + nt(both, rest)).astype(BF16) if joint else both
        share(i).start()
        add(1, i, i == 0)
        if i > 0:
            shared(i - 1).wait_recv()
            add(0, i - 1)
    shared(count - 1).wait_recv()
    add(0, count - 1)

    peers = peers_of(me, rows)

    def scatter(s, slot, there):
        return remote(z_send.at[s, there], z_recv.at[s, slot], rs_sem.at[0, s, slot], rs_sem.at[1, s, slot],
                      {"rows": there})

    def gather(s, slot, owner, there):
        return remote(z_full.at[s, owner], z_full.at[s, owner], ag_sem.at[0, s, slot], ag_sem.at[1, s, slot],
                      {"rows": there})

    for s in range(NS):
        for p in range(rows):
            f, k = divmod(p, group)
            left = (f * NS + s) * wide
            z_send[s, p] = z[k * deep:(k + 1) * deep, left:left + wide].astype(BF16)
        for slot, there, _ in peers:
            scatter(s, slot, there).start()
    for s in range(NS):
        total = z_send[s, me].astype(F32)
        for slot, there, _ in reversed(peers):
            scatter(s, slot, there).wait_recv()
            total = total + z_recv[s, slot].astype(F32)
        z_full[s, me] = total.astype(BF16)
        for slot, there, _ in peers:
            gather(s, slot, me, there).start()

    for s in range(NS):
        for slot, there, back in reversed(peers):
            gather(s, slot, back, there).wait_recv()
        if not first:
            gram_terms(0, z_full, s)
    if not first:
        gram_near(0).start()
    z_out[...] = z_full[...]
    if not first:
        gram_to_far(0)
    for i in range(count):
        to_near(i).wait_send()
        to_far(i).wait_send()
        share(i).wait_send()
    for s in range(NS):
        for slot, there, _ in peers:
            scatter(s, slot, there).wait_send()
            gather(s, slot, me, there).wait_send()
    if not first:
        gram_finish(0, gram_out)


def covariance(slab, q, rows, ident, ids=None):
    joint = q.ndim == 4
    length, feats = slab.shape
    width = q.shape[1] * q.shape[2] // 2 if joint else q.shape[1]
    half = length // 2
    count = len(SHARES)
    piece = (2 * width // rows, feats // (2 * NS))
    low = width // 2
    parts = (3, low // 2, low)
    dma = pltpu.SemaphoreType.DMA
    first = ids is not None
    lower = jax.ShapeDtypeStruct((3, low, low), F32)
    out = [jax.ShapeDtypeStruct((NS, rows, *piece), BF16)] + [lower] * (not first)
    args, extra, specs = [slab, q], [], [VMEM, VMEM]
    if first:
        out += [jax.ShapeDtypeStruct(ids.shape, jnp.int32), jax.ShapeDtypeStruct(slab.shape, BF16)]
        args.append(ids)
        extra = [pltpu.VMEM(q.shape, F32), pltpu.VMEM(ids.shape, jnp.int32), dma((2, count + 1))]
        specs = [HBM] * 3
    if joint:
        out += [lower, jax.ShapeDtypeStruct((8, 128), F32)]
        extra = [pltpu.VMEM((width, width), F32)]
    kind = "first" if first else "joint" if joint else "plain"
    grams = 1 + joint
    return pl.pallas_call(
        functools.partial(covariance_kernel, rows, kind),
        out_shape=out,
        in_specs=specs,
        out_specs=[VMEM] * len(out),
        scratch_shapes=extra + [
            pltpu.VMEM((feats, width), BF16),
            pltpu.VMEM((half, width), BF16),
            pltpu.VMEM((half, width), BF16),
            pltpu.VMEM((half, width), F32),
            pltpu.VMEM((half, width), BF16),
            pltpu.VMEM((half, width), BF16),
            pltpu.VMEM((2, half, width), BF16),
            pltpu.VMEM((width, feats), F32),
            pltpu.VMEM((NS, rows, *piece), BF16),
            pltpu.VMEM((NS, rows, *piece), BF16),
            pltpu.VMEM((NS, rows, *piece), BF16),
            pltpu.VMEM((grams, 2, *parts), F32),
            pltpu.VMEM((grams, *parts), F32),
            pltpu.VMEM((grams, *parts), F32),
            pltpu.VMEM((grams, *parts), F32),
            pltpu.VMEM((grams, 2, *parts), F32),
            dma((2, count)),
            dma((2, count)),
            dma((2, count)),
            dma((2, NS, rows)),
            dma((2, NS, rows)),
            dma((2, grams, 3)),
            pltpu.SemaphoreType.REGULAR,
            pltpu.SemaphoreType.REGULAR,
        ],
        compiler_params=pltpu.CompilerParams(
            collective_id=ident, has_side_effects=True, vmem_limit_bytes=(GRANT if first else 32) << 20
        ),
        name="covariance",
    )(*args)


def split(a):
    top = a.astype(BF16)
    return top, (a - top.astype(F32)).astype(BF16)


def fine(dot, a, b):
    (a0, a1), (b0, b1) = split(a), split(b)
    return dot(a0, b0) + (dot(a0, b1) + dot(a1, b0))


def masks(n):
    row = lax.broadcasted_iota(jnp.int32, (n, n), 0)
    col = lax.broadcasted_iota(jnp.int32, (n, n), 1)
    eye = jnp.where(row == col, F32(1), F32(0))
    return row, col, eye, jnp.where(row > col, F32(1), F32(0.5) * eye)


def whole_gram(gram, out):
    low = gram.shape[1]
    out[:low, :low] = gram[0]
    out[low:, :low] = gram[1]
    out[low:, low:] = gram[2]
    out[:low, low:] = gram[1].T
    return out[...]


def unit_diagonal(g, eye):
    diag = g * eye
    across = lax.rsqrt(jnp.sum(diag, axis=0, keepdims=True))
    down = lax.rsqrt(jnp.sum(diag, axis=1, keepdims=True))
    return g * across * down, across


def coarse_residual(x, unit, eye):
    near = x.astype(BF16)
    return nt(nn(near, unit.astype(BF16)).astype(BF16), near) - eye


def fine_residual(x, unit, eye):
    return fine(nt, fine(nn, x, unit), x) - eye


def improved(x, e, lower):
    return x - nn((e * lower).astype(BF16), x.astype(BF16))


def steps_for(gram, unit):
    n = unit.shape[0]
    _, _, eye, lower = masks(n)
    scaled, across = unit_diagonal(whole_gram(gram, unit), eye)
    unit[...] = scaled
    x = eye - (scaled - eye) * lower
    for step in range(5):
        e = (coarse_residual if step < 2 else fine_residual)(x, unit[...], eye)
        x = improved(x, e, lower)
    return x * across, jnp.sum(e * e)


def basis_kernel(last, kept, gram, z, q_out, unit, x, e, a, state):
    n = unit.shape[0]
    row, col, eye, lower = masks(n)
    scaled, across = unit_diagonal(whole_gram(gram, x), eye)
    unit[...] = scaled
    begin = scaled - eye
    e[...] = begin
    x[...] = eye
    state[0] = 0

    @pl.loop(0, STEPS)
    def _(step):
        @pl.when(state[0] == 0)
        def _():
            now = e[...]
            size = jnp.sum(now * now)
            better = improved(x[...], now, lower)
            x[...] = better
            done = size < TOL * TOL
            state[0] = done.astype(jnp.int32)

            @pl.when(size > COARSE * COARSE)
            def _():
                e[...] = coarse_residual(better, unit[...], eye)

            @pl.when(jnp.logical_not(done) & jnp.logical_not(size > COARSE * COARSE))
            def _():
                e[...] = fine_residual(better, unit[...], eye)

    @pl.when(state[0] == 0)
    def _():
        a[...] = unit[...]
        x[...] = eye

        @pl.loop(0, n)
        def _(j):
            pick_row = row == j
            pick_col = col == j
            now = a[...]
            inv = x[...]
            a_row = jnp.sum(jnp.where(pick_row, now, 0.0), axis=0, keepdims=True)
            a_col = jnp.sum(jnp.where(pick_col, now, 0.0), axis=1, keepdims=True)
            x_row = jnp.sum(jnp.where(pick_row, inv, 0.0), axis=0, keepdims=True)
            pivot = jnp.sum(jnp.where(pick_row & pick_col, now, 0.0))
            root = jnp.sqrt(jnp.full((1, n), pivot))
            line = x_row / root
            factor = jnp.where(row[:, :1] > j, a_col / root[:, :1], 0.0)
            x[...] = jnp.where(pick_row, line, inv - factor * line)
            a[...] = now - factor * (a_row / root)

    top, rest = split(x[...] * across)
    ns, rows, _, wide = z.shape
    group = rows // 2
    for f in range(2):
        for s in range(ns):
            block = z[s, f * group:(f + 1) * group].reshape(n, wide)
            qt = nn(top, block) + nn(rest, block)
            if last:
                index = lax.broadcasted_iota(jnp.int32, (n, wide), 0)
                qt = jnp.where(index < kept[0], qt, 0.0)
            left = (f * ns + s) * wide
            q_out[left:left + wide, :] = qt.T.astype(BF16)


def new_basis(kept, gram, z, last):
    n = 2 * gram.shape[1]
    return pl.pallas_call(
        functools.partial(basis_kernel, last),
        out_shape=jax.ShapeDtypeStruct((2 * z.shape[0] * z.shape[3], n), BF16),
        in_specs=[SMEM, VMEM, VMEM],
        out_specs=VMEM,
        scratch_shapes=[pltpu.VMEM((n, n), F32)] * 4 + [pltpu.SMEM((2,), jnp.int32)],
        compiler_params=pltpu.CompilerParams(vmem_limit_bytes=24 << 20),
        name="new_basis",
    )(kept, gram, z)


def project_kernel(source, q, p_out, slab, away, home, keep, send, recv, p, near_sem, far_sem, p_sem, load_sem):
    core, xl = lax.axis_index("core"), lax.axis_index("xl")
    near, far = {"core": 1 - core}, {"xl": 1 - xl}
    half_rows = slab.shape[0] // 2
    half = q.shape[1] // 2
    chunks = chunks_of(half_rows)
    count = len(chunks)
    barrier = greet((near, far))

    def rows_at(own, i):
        start, size = chunks[i]
        h = core if own else 1 - core
        return pl.ds(pl.multiple_of(h * half_rows + start, 8), size)

    def load(own, i):
        at = rows_at(own, i)
        return pltpu.make_async_copy(source.at[at], slab.at[at], load_sem.at[own, i])

    for i in range(count):
        load(0, i).start()
        load(1, i).start()

    def scores(own, i):
        load(own, i).wait()
        return nn(slab[rows_at(own, i), :], q[...])

    def at(ref, i):
        start, size = chunks[i]
        return ref.at[pl.ds(start, size)]

    def p_at(own, i):
        return at(p.at[core if own else 1 - core], i)

    def to_near(i):
        return remote(at(away, i), at(home, i), near_sem.at[0, i], near_sem.at[1, i], near)

    def to_far(i):
        return remote(at(send, i), at(recv, i), far_sem.at[0, i], far_sem.at[1, i], far)

    def share(i):
        return remote(p_at(1, i), p_at(1, i), p_sem.at[0, i], p_sem.at[1, i], near)

    def shared(i):
        return remote(p_at(0, i), p_at(0, i), p_sem.at[0, i], p_sem.at[1, i], near)

    def chip_sum(i, part):
        to_near(i).wait_recv()
        both = part + at(home, i)[...].astype(F32)
        low, high = both[:, :half], both[:, half:]
        at(send, i)[...] = jnp.where(xl == 0, high, low).astype(BF16)
        to_far(i).start()
        at(keep, i)[...] = jnp.where(xl == 0, low, high)

    for i in range(2):
        at(away, i)[...] = scores(0, i).astype(BF16)
    own = [scores(1, 0)]
    pl.semaphore_wait(barrier, 2)
    to_near(0).start()
    to_near(1).start()
    for i in range(count):
        if i + 2 < count:
            at(away, i + 2)[...] = scores(0, i + 2).astype(BF16)
            to_near(i + 2).start()
        if i + 1 < count:
            own.append(scores(1, i + 1))
        chip_sum(i, own[i])
    for i in range(count):
        to_far(i).wait_recv()
        p_at(1, i)[...] = (at(keep, i)[...] + at(recv, i)[...].astype(F32)).astype(BF16)
        share(i).start()
    for i in range(count):
        to_near(i).wait_send()
        to_far(i).wait_send()
    for i in range(count):
        shared(i).wait_recv()
    p_out[...] = p[...].reshape(p_out.shape)
    for i in range(count):
        share(i).wait_send()


def project(slab, q, ident):
    length = slab.shape[0]
    width = q.shape[1]
    half = width // 2
    dma = pltpu.SemaphoreType.DMA((2, len(SHARES)))
    return pl.pallas_call(
        project_kernel,
        out_shape=jax.ShapeDtypeStruct((length, half), BF16),
        in_specs=[HBM, VMEM],
        out_specs=VMEM,
        scratch_shapes=[
            pltpu.VMEM(slab.shape, BF16),
            pltpu.VMEM((length // 2, width), BF16),
            pltpu.VMEM((length // 2, width), BF16),
            pltpu.VMEM((length // 2, half), F32),
            pltpu.VMEM((length // 2, half), BF16),
            pltpu.VMEM((length // 2, half), BF16),
            pltpu.VMEM((2, length // 2, half), BF16),
            dma,
            dma,
            dma,
            dma,
        ],
        compiler_params=pltpu.CompilerParams(
            collective_id=ident, has_side_effects=True, vmem_limit_bytes=32 << 20
        ),
        name="project",
    )(slab, q)


def pack_kernel(place, side, p, spread, doubled):
    length, lanes = p.shape
    cols = lanes // 2
    unroll = 16
    low = lax.broadcasted_iota(jnp.int32, (length, lanes), 1) < cols
    wide = p[...].astype(F32)
    turned = pltpu.roll(wide, cols, 1)
    doubled[...] = jnp.where(low == (side[0] == 0), wide, turned)
    spread[...] = jnp.zeros_like(spread)

    @pl.loop(0, length // unroll)
    def _(step):
        for u in range(unroll):
            i = step * unroll + u
            spread[pl.ds(place[i], 1), :] = doubled[pl.ds(i, 1), :]


def spread_rows(place, side, p, rows):
    length, lanes = p.shape
    return pl.pallas_call(
        pack_kernel,
        out_shape=jax.ShapeDtypeStruct((2 * rows * CAP, lanes), F32),
        in_specs=[SMEM, SMEM, VMEM],
        out_specs=VMEM,
        scratch_shapes=[pltpu.VMEM((length, lanes), F32)],
        compiler_params=pltpu.CompilerParams(vmem_limit_bytes=16 << 20),
        name="spread_rows",
    )(place, side, p)


def exchange_kernel(rows, spread, out, buf, arrived, sem):
    me = lax.axis_index("rows")
    lanes = spread.shape[1]
    peers = peers_of(me, rows)
    barrier = greet([{"rows": there} for _, there, _ in peers])
    even = lax.broadcasted_iota(jnp.int32, (CAP, lanes), 1) < lanes // 2

    def block(r):
        start = pl.multiple_of(r * CAP, CAP)
        low = spread[pl.ds(start, CAP), :]
        high = spread[pl.ds(pl.multiple_of(start + rows * CAP, CAP), CAP), :]
        return jnp.where(even, low, high).T.astype(BF16)

    def send(slot, there, at):
        return remote(buf.at[slot], arrived.at[at], sem.at[0, slot], sem.at[1, slot], {"rows": there})

    ahead = min(12, rows - 1)
    for slot, there, _ in peers[:ahead]:
        buf[slot] = block(there)
    pl.semaphore_wait(barrier, rows - 1)
    for slot, there, _ in peers:
        if slot >= ahead:
            buf[slot] = block(there)
        send(slot, there, me).start()
    out[me] = block(me)
    for slot, there, back in reversed(peers):
        send(slot, there, back).wait_recv()
        out[back] = arrived[back]
    for slot, there, _ in peers:
        send(slot, there, me).wait_send()


def exchange(spread, rows, ident):
    lanes = spread.shape[1]
    whole = (rows, lanes, CAP)
    return pl.pallas_call(
        functools.partial(exchange_kernel, rows),
        out_shape=jax.ShapeDtypeStruct(whole, BF16),
        in_specs=[VMEM],
        out_specs=VMEM,
        scratch_shapes=[
            pltpu.VMEM((rows - 1, lanes, CAP), BF16),
            pltpu.VMEM(whole, BF16),
            pltpu.SemaphoreType.DMA((2, rows - 1)),
        ],
        compiler_params=pltpu.CompilerParams(
            collective_id=ident, has_side_effects=True, vmem_limit_bytes=16 << 20
        ),
        name="exchange",
    )(spread)


def arrange_kernel(arrived, out):
    cols = out.shape[1]
    for r in range(arrived.shape[0]):
        for h in range(2):
            out[h, :, r * CAP:(r + 1) * CAP] = arrived[r, h * cols:(h + 1) * cols, :]


def arrange(arrived):
    rows, lanes, _ = arrived.shape
    return pl.pallas_call(
        arrange_kernel,
        out_shape=jax.ShapeDtypeStruct((2, lanes // 2, rows * CAP), BF16),
        in_specs=[VMEM],
        out_specs=VMEM,
        compiler_params=pltpu.CompilerParams(vmem_limit_bytes=16 << 20),
        name="arrange",
    )(arrived)


def shards(rows, slab, basis, cluster_ids, kept):
    side = jnp.broadcast_to(lax.axis_index("core"), (1,)).astype(jnp.int32)
    z, place, near_slab = covariance(slab, basis, rows, 0, cluster_ids.reshape(-1, CAP))
    for step in range(1, ITERS):
        after, gram, before, size = covariance(near_slab, z, rows, step)

        def again(before, z, after, gram):
            return tuple(covariance(slab, new_basis(kept, before, z, False), rows, ITERS + 1 + step))

        def kept_on(before, z, after, gram):
            return after, gram

        z, gram = lax.cond(size[0, 0] < TOL * TOL, kept_on, again, before, z, after, gram)
    q = new_basis(kept, gram, z, True)
    p = project(slab, q, ITERS)
    spread = spread_rows(place.reshape(-1), side, p, rows)
    return jnp.swapaxes(arrange(exchange(spread, rows, ITERS + 1)), 1, 2)


def solution(mesh):
    rows = mesh.shape["rows"]
    torus = Mesh(mesh.devices.reshape(rows, 2, 2), ("rows", "xl", "core"))
    placed = (P("rows", FEAT), P(FEAT, None), P("rows", None), P())
    return jax.shard_map(
        functools.partial(shards, rows), mesh=torus, in_specs=placed,
        out_specs=P("rows", None, FEAT), check_vma=False,
    )
```

```python
import functools

import jax
import jax.numpy as jnp
from jax import lax
from jax.experimental import pallas as pl
from jax.experimental.pallas import tpu as pltpu
from jax.sharding import Mesh
from jax.sharding import PartitionSpec as P

ITERS = 2
CAP = 128
SHARES = (1, 2, 2, 2, 2, 2, 1)
NS = 1
GRANT = 44
TOL = 2e-3
COARSE = 1.0
STEPS = 14
F32 = jnp.float32
BF16 = jnp.bfloat16
MESH = pl.DeviceIdType.MESH
VMEM = pl.BlockSpec(memory_space=pltpu.VMEM)
SMEM = pl.BlockSpec(memory_space=pltpu.SMEM)
HBM = pl.BlockSpec(memory_space=pltpu.HBM)
FEAT = ("xl", "core")


def nn(a, b):
    return lax.dot_general(a, b, (((1,), (0,)), ((), ())), preferred_element_type=F32)


def nt(a, b):
    return lax.dot_general(a, b, (((1,), (1,)), ((), ())), preferred_element_type=F32)


def tn(a, b):
    return lax.dot_general(a, b, (((0,), (0,)), ((), ())), preferred_element_type=F32)


def greet(targets):
    barrier = pltpu.get_barrier_semaphore()
    for target in targets:
        pl.semaphore_signal(barrier, inc=1, device_id=target, device_id_type=MESH)
    return barrier


def grid_of(rows):
    return (4, 4, 2) if rows == 32 else (2, rows // 4, 2)


def terms(me, rows):
    nz, ny, nx = grid_of(rows)
    z, y, x = me // (ny * nx), (me // nx) % ny, me % nx
    along_z = [((z + d) % nz) * (ny * nx) for d in range(nz)]
    along_y = [((y + d) % ny) * nx for d in range(ny)]
    return along_z, along_y, [(x + d) % nx for d in range(nx)]


def axis_peers(me, rows):
    az, ay, ax = terms(me, rows)
    return ([{"rows": a + ay[0] + ax[0]} for a in az[1:]] + [{"rows": az[0] + a + ax[0]} for a in ay[1:]]
            + [{"rows": az[0] + ay[0] + a} for a in ax[1:]])


def peers_of(me, rows):
    lists = terms(me, rows)

    def order(n):
        return sorted(range(n), key=lambda d: -min(d, n - d))

    found = []
    for dx in order(len(lists[2])):
        for dz in order(len(lists[0])):
            for dy in order(len(lists[1])):
                if dz or dy or dx:
                    there = lists[0][dz] + lists[1][dy] + lists[2][dx]
                    back = lists[0][-dz] + lists[1][-dy] + lists[2][-dx]
                    found.append((len(found), there, back))
    return found


def chunks_of(half):
    unit = half // sum(SHARES)
    found, start = [], 0
    for share in SHARES:
        found.append((start, share * unit))
        start += share * unit
    return found


def remote(src, dst, send, recv, target):
    return pltpu.make_async_remote_copy(
        src_ref=src, dst_ref=dst, send_sem=send, recv_sem=recv, device_id=target, device_id_type=MESH
    )


def find_places(clusters, ids, place):
    blocks = ids.shape[0]
    lane = lax.broadcasted_iota(jnp.int32, (CAP, CAP), 1)
    sub = lax.broadcasted_iota(jnp.int32, (CAP, CAP), 0)
    before = jnp.where(sub < lane, F32(1), F32(0)).astype(BF16)
    names = lax.broadcasted_iota(jnp.int32, (clusters, CAP), 0)
    seen = jnp.zeros((clusters, 1), F32)
    for b in range(blocks):
        block = ids[b:b + 1, :]
        hot = jnp.where(names == block, F32(1), F32(0))
        earlier = nn(hot.astype(BF16), before) + seen
        slot = jnp.sum(hot * earlier, axis=0, keepdims=True).astype(jnp.int32)
        pair = block // 2
        odd = block - 2 * pair
        place[b:b + 1, :] = odd * (clusters // 2 * CAP) + pair * CAP + slot
        seen = seen + jnp.sum(hot, axis=1, keepdims=True)


def covariance_kernel(rows, kind, *refs):
    first, joint = kind == "first", kind == "joint"
    if first:
        source, basis, z_out, slab, q, load_sem, *refs = refs
    elif joint:
        slab, z_in, z_out, gram_out, gram_in, size_out, unit, *refs = refs
    else:
        slab, q, z_out, gram_out, *refs = refs
    (qb, away, home, part, mine, theirs, y, z, z_send, z_recv, z_full, g_part, g_near, g_mine, g_far, g_all,
     near_sem, far_sem, y_sem, rs_sem, ag_sem, g_sem, round_a, round_b) = refs
    me, core, xl = lax.axis_index("rows"), lax.axis_index("core"), lax.axis_index("xl")
    near, far = {"core": 1 - core}, {"xl": 1 - xl}
    half_rows = slab.shape[0] // 2
    width = qb.shape[1]
    chunks = chunks_of(half_rows)
    count = len(chunks)
    deep, wide = z_send.shape[2:]
    group = rows // 2
    low = width // 2
    part_rows = low // 2
    beside = axis_peers(me, rows)
    barrier = greet([near, far] + beside)

    def rows_at(h, i):
        start, size = chunks[i]
        return pl.ds(pl.multiple_of(h * half_rows + start, 8), size)

    def load(own, i):
        at = rows_at(core if own else 1 - core, i)
        return pltpu.make_async_copy(source.at[at], slab.at[at], load_sem.at[own, i])

    if first:
        for i in range(count):
            load(0, i).start()
            load(1, i).start()
        begin = pltpu.make_async_copy(basis, q, load_sem.at[0, count])
        begin.start()
        begin.wait()

    def held(own, i):
        return slab[rows_at(core if own else 1 - core, i), :]

    def scores(own, i):
        if first:
            load(own, i).wait()
        return nn(held(own, i), qb[...])

    def at(ref, i):
        start, size = chunks[i]
        return ref.at[pl.ds(start, size)]

    def to_near(i):
        return remote(at(away, i), at(home, i), near_sem.at[0, i], near_sem.at[1, i], near)

    def to_far(i):
        return remote(at(mine, i), at(theirs, i), far_sem.at[0, i], far_sem.at[1, i], far)

    def y_at(own, i):
        return at(y.at[core if own else 1 - core], i)

    def share(i):
        return remote(y_at(1, i), y_at(1, i), y_sem.at[0, i], y_sem.at[1, i], near)

    def shared(i):
        return remote(y_at(0, i), y_at(0, i), y_sem.at[0, i], y_sem.at[1, i], near)

    def chip_sum(i):
        to_near(i).wait_recv()
        at(mine, i)[...] = (at(part, i)[...] + at(home, i)[...].astype(F32)).astype(BF16)
        to_far(i).start()

    def pass_on(sem):
        for peer in beside:
            pl.semaphore_signal(sem, inc=1, device_id=peer, device_id_type=MESH)

    def gram_terms(e, pieces, s):
        for f in range(2):
            block = pieces[s, f * group:(f + 1) * group].reshape(width, wide)
            terms_of = (nt(block[:low], block[:low]), nt(block[low:], block[:low]), nt(block[low:], block[low:]))
            for b, term in enumerate(terms_of):
                for h in range(2):
                    line = term[h * part_rows:(h + 1) * part_rows]
                    g_part[e, h, b] = line if s + f == 0 else g_part[e, h, b] + line

    def gram_copy(e, i, src, dst, target):
        return remote(src, dst, g_sem.at[0, e, i], g_sem.at[1, e, i], target)

    def gram_near(e):
        return gram_copy(e, 0, g_part.at[e, 1 - core], g_near.at[e], near)

    def gram_far(e):
        return gram_copy(e, 1, g_mine.at[e], g_far.at[e], far)

    def gram_back(e, c):
        return gram_copy(e, 2, g_all.at[e, c], g_all.at[e, c], near)

    def gram_to_far(e):
        gram_near(e).wait_recv()
        g_mine[e] = g_part[e, core] + g_near[e]
        gram_far(e).start()

    def gram_finish(e, out):
        gram_far(e).wait_recv()
        g_all[e, core] = g_mine[e] + g_far[e]
        gram_back(e, core).start()
        gram_back(e, 1 - core).wait_recv()
        for h in range(2):
            for b in range(3):
                out[b, h * part_rows:(h + 1) * part_rows, :] = g_all[e, h, b]
        gram_near(e).wait_send()
        gram_far(e).wait_send()
        gram_back(e, core).wait_send()

    if joint:
        for s in range(NS):
            gram_terms(1, z_in, s)
            for f in range(2):
                left = (f * NS + s) * wide
                qb[left:left + wide, :] = z_in[s, f * group:(f + 1) * group].reshape(width, wide).T
    else:
        qb[...] = q[...].astype(BF16)
    for i in range(count):
        at(away, i)[...] = scores(0, i).astype(BF16)
        if i == 0:
            at(part, i)[...] = scores(1, i)
            continue
        if i == 1:
            pl.semaphore_wait(barrier, len(beside) + 2)
            if joint:
                gram_near(1).start()
            to_near(0).start()
        to_near(i).start()
        at(part, i)[...] = scores(1, i)
        if joint and i == 1:
            gram_to_far(1)
        chip_sum(i - 1)
        if i == 2:
            pass_on(round_a)
    chip_sum(count - 1)
    pl.semaphore_wait(round_a, len(beside))
    pass_on(round_b)
    pl.semaphore_wait(round_b, len(beside))
    if joint:
        gram_finish(1, gram_in)
        inverse, last_size = steps_for(gram_in, unit)
        top, rest = split(inverse)
        size_out[0, 0] = last_size

    def add(own, i, start=False):
        term = tn(y_at(own, i)[...], held(own, i))
        z[...] = term if start else z[...] + term

    for i in range(count):
        to_far(i).wait_recv()
        both = (at(mine, i)[...].astype(F32) + at(theirs, i)[...].astype(F32)).astype(BF16)
        y_at(1, i)[...] = (nt(both, top) + nt(both, rest)).astype(BF16) if joint else both
        share(i).start()
        add(1, i, i == 0)
        if i > 0:
            shared(i - 1).wait_recv()
            add(0, i - 1)
    shared(count - 1).wait_recv()
    add(0, count - 1)

    peers = peers_of(me, rows)

    def scatter(s, slot, there):
        return remote(z_send.at[s, there], z_recv.at[s, slot], rs_sem.at[0, s, slot], rs_sem.at[1, s, slot],
                      {"rows": there})

    def gather(s, slot, owner, there):
        return remote(z_full.at[s, owner], z_full.at[s, owner], ag_sem.at[0, s, slot], ag_sem.at[1, s, slot],
                      {"rows": there})

    for s in range(NS):
        for p in range(rows):
            f, k = divmod(p, group)
            left = (f * NS + s) * wide
            z_send[s, p] = z[k * deep:(k + 1) * deep, left:left + wide].astype(BF16)
        for slot, there, _ in peers:
            scatter(s, slot, there).start()
    for s in range(NS):
        total = z_send[s, me].astype(F32)
        for slot, there, _ in reversed(peers):
            scatter(s, slot, there).wait_recv()
            total = total + z_recv[s, slot].astype(F32)
        z_full[s, me] = total.astype(BF16)
        for slot, there, _ in peers:
            gather(s, slot, me, there).start()

    for s in range(NS):
        for slot, there, back in reversed(peers):
            gather(s, slot, back, there).wait_recv()
        if not first:
            gram_terms(0, z_full, s)
    if not first:
        gram_near(0).start()
    z_out[...] = z_full[...]
    if not first:
        gram_to_far(0)
    for i in range(count):
        to_near(i).wait_send()
        to_far(i).wait_send()
        share(i).wait_send()
    for s in range(NS):
        for slot, there, _ in peers:
            scatter(s, slot, there).wait_send()
            gather(s, slot, me, there).wait_send()
    if not first:
        gram_finish(0, gram_out)


def covariance(slab, q, rows, ident, first=False):
    joint = q.ndim == 4
    length, feats = slab.shape
    width = q.shape[1] * q.shape[2] // 2 if joint else q.shape[1]
    half = length // 2
    count = len(SHARES)
    piece = (2 * width // rows, feats // (2 * NS))
    low = width // 2
    parts = (3, low // 2, low)
    dma = pltpu.SemaphoreType.DMA
    lower = jax.ShapeDtypeStruct((3, low, low), F32)
    out = [jax.ShapeDtypeStruct((NS, rows, *piece), BF16)] + [lower] * (not first)
    args, extra, specs = [slab, q], [], [VMEM, VMEM]
    if first:
        out.append(jax.ShapeDtypeStruct(slab.shape, BF16))
        extra = [pltpu.VMEM(q.shape, F32), dma((2, count + 1))]
        specs = [HBM, HBM]
    if joint:
        out += [lower, jax.ShapeDtypeStruct((1, 1), F32)]
        extra = [pltpu.VMEM((width, width), F32)]
    kind = "first" if first else "joint" if joint else "plain"
    grams = 1 + joint
    return pl.pallas_call(
        functools.partial(covariance_kernel, rows, kind),
        out_shape=out,
        in_specs=specs,
        out_specs=[SMEM if shape.shape == (1, 1) else VMEM for shape in out],
        scratch_shapes=extra + [
            pltpu.VMEM((feats, width), BF16),
            pltpu.VMEM((half, width), BF16),
            pltpu.VMEM((half, width), BF16),
            pltpu.VMEM((half, width), F32),
            pltpu.VMEM((half, width), BF16),
            pltpu.VMEM((half, width), BF16),
            pltpu.VMEM((2, half, width), BF16),
            pltpu.VMEM((width, feats), F32),
            pltpu.VMEM((NS, rows, *piece), BF16),
            pltpu.VMEM((NS, rows, *piece), BF16),
            pltpu.VMEM((NS, rows, *piece), BF16),
            pltpu.VMEM((grams, 2, *parts), F32),
            pltpu.VMEM((grams, *parts), F32),
            pltpu.VMEM((grams, *parts), F32),
            pltpu.VMEM((grams, *parts), F32),
            pltpu.VMEM((grams, 2, *parts), F32),
            dma((2, count)),
            dma((2, count)),
            dma((2, count)),
            dma((2, NS, rows)),
            dma((2, NS, rows)),
            dma((2, grams, 3)),
            pltpu.SemaphoreType.REGULAR,
            pltpu.SemaphoreType.REGULAR,
        ],
        compiler_params=pltpu.CompilerParams(
            collective_id=ident, has_side_effects=True, vmem_limit_bytes=(GRANT if first else 32) << 20
        ),
        name="covariance",
    )(*args)


def split(a):
    top = a.astype(BF16)
    return top, (a - top.astype(F32)).astype(BF16)


def fine(dot, a, b):
    (a0, a1), (b0, b1) = split(a), split(b)
    return dot(a0, b0) + (dot(a0, b1) + dot(a1, b0))


def masks(n):
    row = lax.broadcasted_iota(jnp.int32, (n, n), 0)
    col = lax.broadcasted_iota(jnp.int32, (n, n), 1)
    eye = jnp.where(row == col, F32(1), F32(0))
    return row, col, eye, jnp.where(row > col, F32(1), F32(0.5) * eye)


def whole_gram(gram, out):
    low = gram.shape[1]
    out[:low, :low] = gram[0]
    out[low:, :low] = gram[1]
    out[low:, low:] = gram[2]
    out[:low, low:] = gram[1].T
    return out[...]


def unit_diagonal(g, eye):
    diag = g * eye
    across = lax.rsqrt(jnp.sum(diag, axis=0, keepdims=True))
    down = lax.rsqrt(jnp.sum(diag, axis=1, keepdims=True))
    return g * across * down, across


def coarse_residual(x, unit, eye):
    near = x.astype(BF16)
    return nt(nn(near, unit.astype(BF16)).astype(BF16), near) - eye


def fine_residual(x, unit, eye):
    return fine(nt, fine(nn, x, unit), x) - eye


def improved(x, e, lower):
    return x - nn((e * lower).astype(BF16), x.astype(BF16))


def steps_for(gram, unit):
    n = unit.shape[0]
    _, _, eye, lower = masks(n)
    scaled, across = unit_diagonal(whole_gram(gram, unit), eye)
    unit[...] = scaled
    x = eye - (scaled - eye) * lower
    for step in range(5):
        e = (coarse_residual if step < 2 else fine_residual)(x, unit[...], eye)
        x = improved(x, e, lower)
    return x * across, jnp.sum(e * e)


def basis_kernel(last, kept, gram, z, q_out, unit, x, e, a, state):
    n = unit.shape[0]
    row, col, eye, lower = masks(n)
    scaled, across = unit_diagonal(whole_gram(gram, x), eye)
    unit[...] = scaled
    begin = scaled - eye
    e[...] = begin
    x[...] = eye
    state[0] = 0

    @pl.loop(0, STEPS)
    def _(step):
        @pl.when(state[0] == 0)
        def _():
            now = e[...]
            size = jnp.sum(now * now)
            better = improved(x[...], now, lower)
            x[...] = better
            done = size < TOL * TOL
            state[0] = done.astype(jnp.int32)

            @pl.when(size > COARSE * COARSE)
            def _():
                e[...] = coarse_residual(better, unit[...], eye)

            @pl.when(jnp.logical_not(done) & jnp.logical_not(size > COARSE * COARSE))
            def _():
                e[...] = fine_residual(better, unit[...], eye)

    @pl.when(state[0] == 0)
    def _():
        a[...] = unit[...]
        x[...] = eye

        @pl.loop(0, n)
        def _(j):
            pick_row = row == j
            pick_col = col == j
            now = a[...]
            inv = x[...]
            a_row = jnp.sum(jnp.where(pick_row, now, 0.0), axis=0, keepdims=True)
            a_col = jnp.sum(jnp.where(pick_col, now, 0.0), axis=1, keepdims=True)
            x_row = jnp.sum(jnp.where(pick_row, inv, 0.0), axis=0, keepdims=True)
            pivot = jnp.sum(jnp.where(pick_row & pick_col, now, 0.0))
            root = jnp.sqrt(jnp.full((1, n), pivot))
            line = x_row / root
            factor = jnp.where(row[:, :1] > j, a_col / root[:, :1], 0.0)
            x[...] = jnp.where(pick_row, line, inv - factor * line)
            a[...] = now - factor * (a_row / root)

    top, rest = split(x[...] * across)
    ns, rows, _, wide = z.shape
    group = rows // 2
    for f in range(2):
        for s in range(ns):
            block = z[s, f * group:(f + 1) * group].reshape(n, wide)
            qt = nn(top, block) + nn(rest, block)
            if last:
                index = lax.broadcasted_iota(jnp.int32, (n, wide), 0)
                qt = jnp.where(index < kept[0], qt, 0.0)
            left = (f * ns + s) * wide
            q_out[left:left + wide, :] = qt.T.astype(BF16)


def new_basis(kept, gram, z, last):
    n = 2 * gram.shape[1]
    return pl.pallas_call(
        functools.partial(basis_kernel, last),
        out_shape=jax.ShapeDtypeStruct((2 * z.shape[0] * z.shape[3], n), BF16),
        in_specs=[SMEM, VMEM, VMEM],
        out_specs=VMEM,
        scratch_shapes=[pltpu.VMEM((n, n), F32)] * 4 + [pltpu.SMEM((2,), jnp.int32)],
        compiler_params=pltpu.CompilerParams(vmem_limit_bytes=24 << 20),
        name="new_basis",
    )(kept, gram, z)


def project_kernel(clusters, source, q, ids, p_out, place, slab, away, home, keep, send, recv, p, near_sem, far_sem, p_sem, load_sem):
    core, xl = lax.axis_index("core"), lax.axis_index("xl")
    near, far = {"core": 1 - core}, {"xl": 1 - xl}
    half_rows = slab.shape[0] // 2
    half = q.shape[1] // 2
    chunks = chunks_of(half_rows)
    count = len(chunks)
    barrier = greet((near, far))

    def rows_at(own, i):
        start, size = chunks[i]
        h = core if own else 1 - core
        return pl.ds(pl.multiple_of(h * half_rows + start, 8), size)

    def load(own, i):
        at = rows_at(own, i)
        return pltpu.make_async_copy(source.at[at], slab.at[at], load_sem.at[own, i])

    for i in range(count):
        load(0, i).start()
        load(1, i).start()

    def scores(own, i):
        load(own, i).wait()
        return nn(slab[rows_at(own, i), :], q[...])

    def at(ref, i):
        start, size = chunks[i]
        return ref.at[pl.ds(start, size)]

    def p_at(own, i):
        return at(p.at[core if own else 1 - core], i)

    def to_near(i):
        return remote(at(away, i), at(home, i), near_sem.at[0, i], near_sem.at[1, i], near)

    def to_far(i):
        return remote(at(send, i), at(recv, i), far_sem.at[0, i], far_sem.at[1, i], far)

    def share(i):
        return remote(p_at(1, i), p_at(1, i), p_sem.at[0, i], p_sem.at[1, i], near)

    def shared(i):
        return remote(p_at(0, i), p_at(0, i), p_sem.at[0, i], p_sem.at[1, i], near)

    def chip_sum(i, part):
        to_near(i).wait_recv()
        both = part + at(home, i)[...].astype(F32)
        low, high = both[:, :half], both[:, half:]
        at(send, i)[...] = jnp.where(xl == 0, high, low).astype(BF16)
        to_far(i).start()
        at(keep, i)[...] = jnp.where(xl == 0, low, high)

    for i in range(2):
        at(away, i)[...] = scores(0, i).astype(BF16)
    own = [scores(1, 0)]
    pl.semaphore_wait(barrier, 2)
    to_near(0).start()
    to_near(1).start()
    for i in range(count):
        if i + 2 < count:
            at(away, i + 2)[...] = scores(0, i + 2).astype(BF16)
            to_near(i + 2).start()
        if i + 1 < count:
            own.append(scores(1, i + 1))
        chip_sum(i, own[i])
    find_places(clusters, ids, place)
    for i in range(count):
        to_far(i).wait_recv()
        p_at(1, i)[...] = (at(keep, i)[...] + at(recv, i)[...].astype(F32)).astype(BF16)
        share(i).start()
    for i in range(count):
        to_near(i).wait_send()
        to_far(i).wait_send()
    for i in range(count):
        shared(i).wait_recv()
    p_out[...] = p[...].reshape(p_out.shape)
    for i in range(count):
        share(i).wait_send()


def project(slab, q, ids, clusters, ident):
    length = slab.shape[0]
    width = q.shape[1]
    half = width // 2
    dma = pltpu.SemaphoreType.DMA((2, len(SHARES)))
    return pl.pallas_call(
        functools.partial(project_kernel, clusters),
        out_shape=[jax.ShapeDtypeStruct((length, half), BF16), jax.ShapeDtypeStruct(ids.shape, jnp.int32)],
        in_specs=[HBM, VMEM, VMEM],
        out_specs=[VMEM, VMEM],
        scratch_shapes=[
            pltpu.VMEM(slab.shape, BF16),
            pltpu.VMEM((length // 2, width), BF16),
            pltpu.VMEM((length // 2, width), BF16),
            pltpu.VMEM((length // 2, half), F32),
            pltpu.VMEM((length // 2, half), BF16),
            pltpu.VMEM((length // 2, half), BF16),
            pltpu.VMEM((2, length // 2, half), BF16),
            dma,
            dma,
            dma,
            dma,
        ],
        compiler_params=pltpu.CompilerParams(
            collective_id=ident, has_side_effects=True, vmem_limit_bytes=32 << 20
        ),
        name="project",
    )(slab, q, ids)


def pack_kernel(place, side, p, spread, doubled):
    length, lanes = p.shape
    cols = lanes // 2
    unroll = 16
    low = lax.broadcasted_iota(jnp.int32, (length, lanes), 1) < cols
    wide = p[...].astype(F32)
    turned = pltpu.roll(wide, cols, 1)
    doubled[...] = jnp.where(low == (side[0] == 0), wide, turned)
    spread[...] = jnp.zeros_like(spread)

    @pl.loop(0, length // unroll)
    def _(step):
        for u in range(unroll):
            i = step * unroll + u
            spread[pl.ds(place[i], 1), :] = doubled[pl.ds(i, 1), :]


def spread_rows(place, side, p, rows):
    length, lanes = p.shape
    return pl.pallas_call(
        pack_kernel,
        out_shape=jax.ShapeDtypeStruct((2 * rows * CAP, lanes), F32),
        in_specs=[SMEM, SMEM, VMEM],
        out_specs=VMEM,
        scratch_shapes=[pltpu.VMEM((length, lanes), F32)],
        compiler_params=pltpu.CompilerParams(vmem_limit_bytes=16 << 20),
        name="spread_rows",
    )(place, side, p)


def exchange_kernel(rows, spread, out, buf, arrived, sem):
    me = lax.axis_index("rows")
    lanes = spread.shape[1]
    peers = peers_of(me, rows)
    barrier = greet([{"rows": there} for _, there, _ in peers])
    even = lax.broadcasted_iota(jnp.int32, (CAP, lanes), 1) < lanes // 2

    def block(r):
        start = pl.multiple_of(r * CAP, CAP)
        low = spread[pl.ds(start, CAP), :]
        high = spread[pl.ds(pl.multiple_of(start + rows * CAP, CAP), CAP), :]
        return jnp.where(even, low, high).T.astype(BF16)

    def send(slot, there, at):
        return remote(buf.at[slot], arrived.at[at], sem.at[0, slot], sem.at[1, slot], {"rows": there})

    for slot, there, _ in peers:
        buf[slot] = block(there)
    pl.semaphore_wait(barrier, rows - 1)
    for slot, there, _ in peers:
        send(slot, there, me).start()
    out[me] = block(me)
    for slot, there, back in reversed(peers):
        send(slot, there, back).wait_recv()
        out[back] = arrived[back]
    for slot, there, _ in peers:
        send(slot, there, me).wait_send()


def exchange(spread, rows, ident):
    lanes = spread.shape[1]
    whole = (rows, lanes, CAP)
    return pl.pallas_call(
        functools.partial(exchange_kernel, rows),
        out_shape=jax.ShapeDtypeStruct(whole, BF16),
        in_specs=[VMEM],
        out_specs=VMEM,
        scratch_shapes=[
            pltpu.VMEM((rows - 1, lanes, CAP), BF16),
            pltpu.VMEM(whole, BF16),
            pltpu.SemaphoreType.DMA((2, rows - 1)),
        ],
        compiler_params=pltpu.CompilerParams(
            collective_id=ident, has_side_effects=True, vmem_limit_bytes=16 << 20
        ),
        name="exchange",
    )(spread)


def arrange_kernel(arrived, out):
    cols = out.shape[1]
    for r in range(arrived.shape[0]):
        for h in range(2):
            out[h, :, r * CAP:(r + 1) * CAP] = arrived[r, h * cols:(h + 1) * cols, :]


def arrange(arrived):
    rows, lanes, _ = arrived.shape
    return pl.pallas_call(
        arrange_kernel,
        out_shape=jax.ShapeDtypeStruct((2, lanes // 2, rows * CAP), BF16),
        in_specs=[VMEM],
        out_specs=VMEM,
        compiler_params=pltpu.CompilerParams(vmem_limit_bytes=16 << 20),
        name="arrange",
    )(arrived)


def shards(rows, slab, basis, cluster_ids, kept):
    side = jnp.broadcast_to(lax.axis_index("core"), (1,)).astype(jnp.int32)
    z, near_slab = covariance(slab, basis, rows, 0, True)
    for step in range(1, ITERS):
        after, gram, before, size = covariance(near_slab, z, rows, step)

        def again(before, z, after, gram):
            return tuple(covariance(slab, new_basis(kept, before, z, False), rows, ITERS + 1 + step))

        def kept_on(before, z, after, gram):
            return after, gram

        z, gram = lax.cond(size[0, 0] < TOL * TOL, kept_on, again, before, z, after, gram)
    q = new_basis(kept, gram, z, True)
    p, place = project(slab, q, cluster_ids.reshape(-1, CAP), 2 * rows, ITERS)
    spread = spread_rows(place.reshape(-1), side, p, rows)
    return jnp.swapaxes(arrange(exchange(spread, rows, ITERS + 1)), 1, 2)


def solution(mesh):
    rows = mesh.shape["rows"]
    torus = Mesh(mesh.devices.reshape(rows, 2, 2), ("rows", "xl", "core"))
    placed = (P("rows", FEAT), P(FEAT, None), P("rows", None), P())
    return jax.shard_map(
        functools.partial(shards, rows), mesh=torus, in_specs=placed,
        out_specs=P("rows", None, FEAT), check_vma=False,
    )
```

```python
import functools

import jax
import jax.numpy as jnp
from jax import lax
from jax.experimental import pallas as pl
from jax.experimental.pallas import tpu as pltpu
from jax.sharding import Mesh
from jax.sharding import PartitionSpec as P

ITERS = 2
CAP = 128
SHARES = (1, 2, 2, 2, 2, 2, 1)
NS = 1
GRANT = 44
TOL = 2e-3
COARSE = 1.0
STEPS = 14
F32 = jnp.float32
BF16 = jnp.bfloat16
MESH = pl.DeviceIdType.MESH
VMEM = pl.BlockSpec(memory_space=pltpu.VMEM)
SMEM = pl.BlockSpec(memory_space=pltpu.SMEM)
HBM = pl.BlockSpec(memory_space=pltpu.HBM)
FEAT = ("xl", "core")


def nn(a, b):
    return lax.dot_general(a, b, (((1,), (0,)), ((), ())), preferred_element_type=F32)


def nt(a, b):
    return lax.dot_general(a, b, (((1,), (1,)), ((), ())), preferred_element_type=F32)


def tn(a, b):
    return lax.dot_general(a, b, (((0,), (0,)), ((), ())), preferred_element_type=F32)


def greet(targets):
    barrier = pltpu.get_barrier_semaphore()
    for target in targets:
        pl.semaphore_signal(barrier, inc=1, device_id=target, device_id_type=MESH)
    return barrier


def grid_of(rows):
    return (4, 4, 2) if rows == 32 else (2, rows // 4, 2)


def terms(me, rows):
    nz, ny, nx = grid_of(rows)
    z, y, x = me // (ny * nx), (me // nx) % ny, me % nx
    along_z = [((z + d) % nz) * (ny * nx) for d in range(nz)]
    along_y = [((y + d) % ny) * nx for d in range(ny)]
    return along_z, along_y, [(x + d) % nx for d in range(nx)]


def axis_peers(me, rows):
    az, ay, ax = terms(me, rows)
    return ([{"rows": a + ay[0] + ax[0]} for a in az[1:]] + [{"rows": az[0] + a + ax[0]} for a in ay[1:]]
            + [{"rows": az[0] + ay[0] + a} for a in ax[1:]])


def peers_of(me, rows):
    lists = terms(me, rows)

    def order(n):
        return sorted(range(n), key=lambda d: -min(d, n - d))

    found = []
    for dx in order(len(lists[2])):
        for dz in order(len(lists[0])):
            for dy in order(len(lists[1])):
                if dz or dy or dx:
                    there = lists[0][dz] + lists[1][dy] + lists[2][dx]
                    back = lists[0][-dz] + lists[1][-dy] + lists[2][-dx]
                    found.append((len(found), there, back))
    return found


def chunks_of(half):
    unit = half // sum(SHARES)
    found, start = [], 0
    for share in SHARES:
        found.append((start, share * unit))
        start += share * unit
    return found


def remote(src, dst, send, recv, target):
    return pltpu.make_async_remote_copy(
        src_ref=src, dst_ref=dst, send_sem=send, recv_sem=recv, device_id=target, device_id_type=MESH
    )


def find_places(clusters, ids, place):
    blocks = ids.shape[0]
    lane = lax.broadcasted_iota(jnp.int32, (CAP, CAP), 1)
    sub = lax.broadcasted_iota(jnp.int32, (CAP, CAP), 0)
    before = jnp.where(sub < lane, F32(1), F32(0)).astype(BF16)
    names = lax.broadcasted_iota(jnp.int32, (clusters, CAP), 0)
    seen = jnp.zeros((clusters, 1), F32)
    for b in range(blocks):
        block = ids[b:b + 1, :]
        hot = jnp.where(names == block, F32(1), F32(0))
        earlier = nn(hot.astype(BF16), before) + seen
        slot = jnp.sum(hot * earlier, axis=0, keepdims=True).astype(jnp.int32)
        pair = block // 2
        odd = block - 2 * pair
        place[b:b + 1, :] = odd * (clusters // 2 * CAP) + pair * CAP + slot
        seen = seen + jnp.sum(hot, axis=1, keepdims=True)


def covariance_kernel(rows, kind, *refs):
    first, joint = kind == "first", kind == "joint"
    if first:
        source, basis, z_out, slab, q, load_sem, *refs = refs
    elif joint:
        slab, z_in, z_out, gram_out, gram_in, size_out, unit, *refs = refs
    else:
        slab, q, z_out, gram_out, *refs = refs
    (qb, away, home, part, mine, theirs, y, z, z_send, z_recv, z_full, g_part, g_near, g_mine, g_far, g_all,
     near_sem, far_sem, y_sem, rs_sem, ag_sem, g_sem, round_a, round_b) = refs
    me, core, xl = lax.axis_index("rows"), lax.axis_index("core"), lax.axis_index("xl")
    near, far = {"core": 1 - core}, {"xl": 1 - xl}
    half_rows = slab.shape[0] // 2
    width = qb.shape[1]
    chunks = chunks_of(half_rows)
    count = len(chunks)
    deep, wide = z_send.shape[2:]
    group = rows // 2
    low = width // 2
    part_rows = low // 2
    beside = axis_peers(me, rows)
    barrier = greet([near, far] + beside)

    def rows_at(h, i):
        start, size = chunks[i]
        return pl.ds(pl.multiple_of(h * half_rows + start, 8), size)

    def load(own, i):
        at = rows_at(core if own else 1 - core, i)
        return pltpu.make_async_copy(source.at[at], slab.at[at], load_sem.at[own, i])

    if first:
        for i in range(count):
            load(0, i).start()
            load(1, i).start()
        begin = pltpu.make_async_copy(basis, q, load_sem.at[0, count])
        begin.start()
        begin.wait()

    def held(own, i):
        return slab[rows_at(core if own else 1 - core, i), :]

    def scores(own, i):
        if first:
            load(own, i).wait()
        return nn(held(own, i), qb[...])

    def at(ref, i):
        start, size = chunks[i]
        return ref.at[pl.ds(start, size)]

    def to_near(i):
        return remote(at(away, i), at(home, i), near_sem.at[0, i], near_sem.at[1, i], near)

    def to_far(i):
        return remote(at(mine, i), at(theirs, i), far_sem.at[0, i], far_sem.at[1, i], far)

    def y_at(own, i):
        return at(y.at[core if own else 1 - core], i)

    def share(i):
        return remote(y_at(1, i), y_at(1, i), y_sem.at[0, i], y_sem.at[1, i], near)

    def shared(i):
        return remote(y_at(0, i), y_at(0, i), y_sem.at[0, i], y_sem.at[1, i], near)

    def chip_sum(i):
        to_near(i).wait_recv()
        at(mine, i)[...] = (at(part, i)[...] + at(home, i)[...].astype(F32)).astype(BF16)
        to_far(i).start()

    def pass_on(sem):
        for peer in beside:
            pl.semaphore_signal(sem, inc=1, device_id=peer, device_id_type=MESH)

    def gram_terms(e, pieces, s):
        for f in range(2):
            block = pieces[s, f * group:(f + 1) * group].reshape(width, wide)
            terms_of = (nt(block[:low], block[:low]), nt(block[low:], block[:low]), nt(block[low:], block[low:]))
            for b, term in enumerate(terms_of):
                for h in range(2):
                    line = term[h * part_rows:(h + 1) * part_rows]
                    g_part[e, h, b] = line if s + f == 0 else g_part[e, h, b] + line

    def gram_copy(e, i, src, dst, target):
        return remote(src, dst, g_sem.at[0, e, i], g_sem.at[1, e, i], target)

    def gram_near(e):
        return gram_copy(e, 0, g_part.at[e, 1 - core], g_near.at[e], near)

    def gram_far(e):
        return gram_copy(e, 1, g_mine.at[e], g_far.at[e], far)

    def gram_back(e, c):
        return gram_copy(e, 2, g_all.at[e, c], g_all.at[e, c], near)

    def gram_to_far(e):
        gram_near(e).wait_recv()
        g_mine[e] = g_part[e, core] + g_near[e]
        gram_far(e).start()

    def gram_finish(e, out):
        gram_far(e).wait_recv()
        g_all[e, core] = g_mine[e] + g_far[e]
        gram_back(e, core).start()
        gram_back(e, 1 - core).wait_recv()
        for h in range(2):
            for b in range(3):
                out[b, h * part_rows:(h + 1) * part_rows, :] = g_all[e, h, b]
        gram_near(e).wait_send()
        gram_far(e).wait_send()
        gram_back(e, core).wait_send()

    if joint:
        for s in range(NS):
            gram_terms(1, z_in, s)
            for f in range(2):
                left = (f * NS + s) * wide
                qb[left:left + wide, :] = z_in[s, f * group:(f + 1) * group].reshape(width, wide).T
    else:
        qb[...] = q[...].astype(BF16)
    for i in range(count):
        at(away, i)[...] = scores(0, i).astype(BF16)
        if i == 0:
            at(part, i)[...] = scores(1, i)
            continue
        if i == 1:
            pl.semaphore_wait(barrier, len(beside) + 2)
            if joint:
                gram_near(1).start()
            to_near(0).start()
        to_near(i).start()
        at(part, i)[...] = scores(1, i)
        if joint and i == 1:
            gram_to_far(1)
        chip_sum(i - 1)
        if i == 2:
            pass_on(round_a)
    chip_sum(count - 1)
    pl.semaphore_wait(round_a, len(beside))
    pass_on(round_b)
    pl.semaphore_wait(round_b, len(beside))
    if joint:
        gram_finish(1, gram_in)
        inverse, last_size = steps_for(gram_in, unit)
        top, rest = split(inverse)
        size_out[0, 0] = last_size

    def add(own, i, start=False):
        term = tn(y_at(own, i)[...], held(own, i))
        z[...] = term if start else z[...] + term

    for i in range(count):
        to_far(i).wait_recv()
        both = (at(mine, i)[...].astype(F32) + at(theirs, i)[...].astype(F32)).astype(BF16)
        y_at(1, i)[...] = (nt(both, top) + nt(both, rest)).astype(BF16) if joint else both
        share(i).start()
        add(1, i, i == 0)
        if i > 0:
            shared(i - 1).wait_recv()
            add(0, i - 1)
    shared(count - 1).wait_recv()
    add(0, count - 1)

    peers = peers_of(me, rows)

    def scatter(s, slot, there):
        return remote(z_send.at[s, there], z_recv.at[s, slot], rs_sem.at[0, s, slot], rs_sem.at[1, s, slot],
                      {"rows": there})

    def gather(s, slot, owner, there):
        return remote(z_full.at[s, owner], z_full.at[s, owner], ag_sem.at[0, s, slot], ag_sem.at[1, s, slot],
                      {"rows": there})

    for s in range(NS):
        for p in range(rows):
            f, k = divmod(p, group)
            left = (f * NS + s) * wide
            z_send[s, p] = z[k * deep:(k + 1) * deep, left:left + wide].astype(BF16)
        for slot, there, _ in peers:
            scatter(s, slot, there).start()
    for s in range(NS):
        total = z_send[s, me].astype(F32)
        for slot, there, _ in reversed(peers):
            scatter(s, slot, there).wait_recv()
            total = total + z_recv[s, slot].astype(F32)
        z_full[s, me] = total.astype(BF16)
        for slot, there, _ in peers:
            gather(s, slot, me, there).start()

    for s in range(NS):
        for slot, there, back in reversed(peers):
            gather(s, slot, back, there).wait_recv()
        if not first:
            gram_terms(0, z_full, s)
    if not first:
        gram_near(0).start()
    z_out[...] = z_full[...]
    if not first:
        gram_to_far(0)
    for i in range(count):
        to_near(i).wait_send()
        to_far(i).wait_send()
        share(i).wait_send()
    for s in range(NS):
        for slot, there, _ in peers:
            scatter(s, slot, there).wait_send()
            gather(s, slot, me, there).wait_send()
    if not first:
        gram_finish(0, gram_out)


def covariance(slab, q, rows, ident, first=False):
    joint = q.ndim == 4
    length, feats = slab.shape
    width = q.shape[1] * q.shape[2] // 2 if joint else q.shape[1]
    half = length // 2
    count = len(SHARES)
    piece = (2 * width // rows, feats // (2 * NS))
    low = width // 2
    parts = (3, low // 2, low)
    dma = pltpu.SemaphoreType.DMA
    lower = jax.ShapeDtypeStruct((3, low, low), F32)
    out = [jax.ShapeDtypeStruct((NS, rows, *piece), BF16)] + [lower] * (not first)
    args, extra, specs = [slab, q], [], [VMEM, VMEM]
    if first:
        out.append(jax.ShapeDtypeStruct(slab.shape, BF16))
        extra = [pltpu.VMEM(q.shape, F32), dma((2, count + 1))]
        specs = [HBM, HBM]
    if joint:
        out += [lower, jax.ShapeDtypeStruct((1, 1), F32)]
        extra = [pltpu.VMEM((width, width), F32)]
    kind = "first" if first else "joint" if joint else "plain"
    grams = 1 + joint
    return pl.pallas_call(
        functools.partial(covariance_kernel, rows, kind),
        out_shape=out,
        in_specs=specs,
        out_specs=[SMEM if shape.shape == (1, 1) else VMEM for shape in out],
        scratch_shapes=extra + [
            pltpu.VMEM((feats, width), BF16),
            pltpu.VMEM((half, width), BF16),
            pltpu.VMEM((half, width), BF16),
            pltpu.VMEM((half, width), F32),
            pltpu.VMEM((half, width), BF16),
            pltpu.VMEM((half, width), BF16),
            pltpu.VMEM((2, half, width), BF16),
            pltpu.VMEM((width, feats), F32),
            pltpu.VMEM((NS, rows, *piece), BF16),
            pltpu.VMEM((NS, rows, *piece), BF16),
            pltpu.VMEM((NS, rows, *piece), BF16),
            pltpu.VMEM((grams, 2, *parts), F32),
            pltpu.VMEM((grams, *parts), F32),
            pltpu.VMEM((grams, *parts), F32),
            pltpu.VMEM((grams, *parts), F32),
            pltpu.VMEM((grams, 2, *parts), F32),
            dma((2, count)),
            dma((2, count)),
            dma((2, count)),
            dma((2, NS, rows)),
            dma((2, NS, rows)),
            dma((2, grams, 3)),
            pltpu.SemaphoreType.REGULAR,
            pltpu.SemaphoreType.REGULAR,
        ],
        compiler_params=pltpu.CompilerParams(
            collective_id=ident, has_side_effects=True, vmem_limit_bytes=(GRANT if first else 32) << 20
        ),
        name="covariance",
    )(*args)


def split(a):
    top = a.astype(BF16)
    return top, (a - top.astype(F32)).astype(BF16)


def fine(dot, a, b):
    (a0, a1), (b0, b1) = split(a), split(b)
    return dot(a0, b0) + (dot(a0, b1) + dot(a1, b0))


def masks(n):
    row = lax.broadcasted_iota(jnp.int32, (n, n), 0)
    col = lax.broadcasted_iota(jnp.int32, (n, n), 1)
    eye = jnp.where(row == col, F32(1), F32(0))
    return row, col, eye, jnp.where(row > col, F32(1), F32(0.5) * eye)


def whole_gram(gram, out):
    low = gram.shape[1]
    out[:low, :low] = gram[0]
    out[low:, :low] = gram[1]
    out[low:, low:] = gram[2]
    out[:low, low:] = gram[1].T
    return out[...]


def unit_diagonal(g, eye):
    diag = g * eye
    across = lax.rsqrt(jnp.sum(diag, axis=0, keepdims=True))
    down = lax.rsqrt(jnp.sum(diag, axis=1, keepdims=True))
    return g * across * down, across


def coarse_residual(x, unit, eye):
    near = x.astype(BF16)
    return nt(nn(near, unit.astype(BF16)).astype(BF16), near) - eye


def fine_residual(x, unit, eye):
    return fine(nt, fine(nn, x, unit), x) - eye


def improved(x, e, lower):
    return x - nn((e * lower).astype(BF16), x.astype(BF16))


def steps_for(gram, unit):
    n = unit.shape[0]
    _, _, eye, lower = masks(n)
    scaled, across = unit_diagonal(whole_gram(gram, unit), eye)
    unit[...] = scaled
    x = eye - (scaled - eye) * lower
    for step in range(5):
        e = (coarse_residual if step < 2 else fine_residual)(x, unit[...], eye)
        x = improved(x, e, lower)
    return x * across, jnp.sum(e * e)


def basis_kernel(last, kept, gram, z, q_out, unit, x, e, a, state):
    n = unit.shape[0]
    row, col, eye, lower = masks(n)
    scaled, across = unit_diagonal(whole_gram(gram, x), eye)
    unit[...] = scaled
    begin = scaled - eye
    e[...] = begin
    x[...] = eye
    state[0] = 0

    @pl.loop(0, STEPS)
    def _(step):
        @pl.when(state[0] == 0)
        def _():
            now = e[...]
            size = jnp.sum(now * now)
            better = improved(x[...], now, lower)
            x[...] = better
            done = size < TOL * TOL
            state[0] = done.astype(jnp.int32)

            @pl.when(size > COARSE * COARSE)
            def _():
                e[...] = coarse_residual(better, unit[...], eye)

            @pl.when(jnp.logical_not(done) & jnp.logical_not(size > COARSE * COARSE))
            def _():
                e[...] = fine_residual(better, unit[...], eye)

    @pl.when(state[0] == 0)
    def _():
        a[...] = unit[...]
        x[...] = eye

        @pl.loop(0, n)
        def _(j):
            pick_row = row == j
            pick_col = col == j
            now = a[...]
            inv = x[...]
            a_row = jnp.sum(jnp.where(pick_row, now, 0.0), axis=0, keepdims=True)
            a_col = jnp.sum(jnp.where(pick_col, now, 0.0), axis=1, keepdims=True)
            x_row = jnp.sum(jnp.where(pick_row, inv, 0.0), axis=0, keepdims=True)
            pivot = jnp.sum(jnp.where(pick_row & pick_col, now, 0.0))
            root = jnp.sqrt(jnp.full((1, n), pivot))
            line = x_row / root
            factor = jnp.where(row[:, :1] > j, a_col / root[:, :1], 0.0)
            x[...] = jnp.where(pick_row, line, inv - factor * line)
            a[...] = now - factor * (a_row / root)

    top, rest = split(x[...] * across)
    ns, rows, _, wide = z.shape
    group = rows // 2
    for f in range(2):
        for s in range(ns):
            block = z[s, f * group:(f + 1) * group].reshape(n, wide)
            qt = nn(top, block) + nn(rest, block)
            if last:
                index = lax.broadcasted_iota(jnp.int32, (n, wide), 0)
                qt = jnp.where(index < kept[0], qt, 0.0)
            left = (f * ns + s) * wide
            q_out[left:left + wide, :] = qt.T.astype(BF16)


def new_basis(kept, gram, z, last):
    n = 2 * gram.shape[1]
    return pl.pallas_call(
        functools.partial(basis_kernel, last),
        out_shape=jax.ShapeDtypeStruct((2 * z.shape[0] * z.shape[3], n), BF16),
        in_specs=[SMEM, VMEM, VMEM],
        out_specs=VMEM,
        scratch_shapes=[pltpu.VMEM((n, n), F32)] * 4 + [pltpu.SMEM((2,), jnp.int32)],
        compiler_params=pltpu.CompilerParams(vmem_limit_bytes=24 << 20),
        name="new_basis",
    )(kept, gram, z)


def project_kernel(clusters, source, q, ids, doubled, place, slab, away, home, keep, send, recv, p, near_sem, far_sem, p_sem, load_sem):
    core, xl = lax.axis_index("core"), lax.axis_index("xl")
    near, far = {"core": 1 - core}, {"xl": 1 - xl}
    half_rows = slab.shape[0] // 2
    half = q.shape[1] // 2
    chunks = chunks_of(half_rows)
    count = len(chunks)
    barrier = greet((near, far))

    def rows_at(own, i):
        start, size = chunks[i]
        h = core if own else 1 - core
        return pl.ds(pl.multiple_of(h * half_rows + start, 8), size)

    def load(own, i):
        at = rows_at(own, i)
        return pltpu.make_async_copy(source.at[at], slab.at[at], load_sem.at[own, i])

    for i in range(count):
        load(0, i).start()
        load(1, i).start()

    def scores(own, i):
        load(own, i).wait()
        return nn(slab[rows_at(own, i), :], q[...])

    def at(ref, i):
        start, size = chunks[i]
        return ref.at[pl.ds(start, size)]

    def p_at(own, i):
        return at(p.at[core if own else 1 - core], i)

    def to_near(i):
        return remote(at(away, i), at(home, i), near_sem.at[0, i], near_sem.at[1, i], near)

    def to_far(i):
        return remote(at(send, i), at(recv, i), far_sem.at[0, i], far_sem.at[1, i], far)

    def share(i):
        return remote(p_at(1, i), p_at(1, i), p_sem.at[0, i], p_sem.at[1, i], near)

    def shared(i):
        return remote(p_at(0, i), p_at(0, i), p_sem.at[0, i], p_sem.at[1, i], near)

    def chip_sum(i, part):
        to_near(i).wait_recv()
        both = part + at(home, i)[...].astype(F32)
        low, high = both[:, :half], both[:, half:]
        at(send, i)[...] = jnp.where(xl == 0, high, low).astype(BF16)
        to_far(i).start()
        at(keep, i)[...] = jnp.where(xl == 0, low, high)

    for i in range(2):
        at(away, i)[...] = scores(0, i).astype(BF16)
    own = [scores(1, 0)]
    pl.semaphore_wait(barrier, 2)
    to_near(0).start()
    to_near(1).start()
    for i in range(count):
        if i + 2 < count:
            at(away, i + 2)[...] = scores(0, i + 2).astype(BF16)
            to_near(i + 2).start()
        if i + 1 < count:
            own.append(scores(1, i + 1))
        chip_sum(i, own[i])
    find_places(clusters, ids, place)

    def double(own, i):
        wide = p_at(own, i)[...].astype(F32)
        low = lax.broadcasted_iota(jnp.int32, wide.shape, 1) < half // 2
        turned = pltpu.roll(wide, half // 2, 1)
        doubled[rows_at(own, i), :] = jnp.where(low == (core == 0), wide, turned)

    for i in range(count):
        to_far(i).wait_recv()
        p_at(1, i)[...] = (at(keep, i)[...] + at(recv, i)[...].astype(F32)).astype(BF16)
        share(i).start()
        double(1, i)
    for i in range(count):
        to_near(i).wait_send()
        to_far(i).wait_send()
    for i in range(count):
        shared(i).wait_recv()
        double(0, i)
    for i in range(count):
        share(i).wait_send()


def project(slab, q, ids, clusters, ident):
    length = slab.shape[0]
    width = q.shape[1]
    half = width // 2
    dma = pltpu.SemaphoreType.DMA((2, len(SHARES)))
    return pl.pallas_call(
        functools.partial(project_kernel, clusters),
        out_shape=[
            jax.ShapeDtypeStruct((length, half), F32),
            jax.ShapeDtypeStruct(ids.shape, jnp.int32),
        ],
        in_specs=[HBM, VMEM, VMEM],
        out_specs=[VMEM] * 2,
        scratch_shapes=[
            pltpu.VMEM(slab.shape, BF16),
            pltpu.VMEM((length // 2, width), BF16),
            pltpu.VMEM((length // 2, width), BF16),
            pltpu.VMEM((length // 2, half), F32),
            pltpu.VMEM((length // 2, half), BF16),
            pltpu.VMEM((length // 2, half), BF16),
            pltpu.VMEM((2, length // 2, half), BF16),
            dma,
            dma,
            dma,
            dma,
        ],
        compiler_params=pltpu.CompilerParams(
            collective_id=ident, has_side_effects=True, vmem_limit_bytes=32 << 20
        ),
        name="project",
    )(slab, q, ids)


def pack_kernel(place, doubled, spread):
    unroll = 16
    spread[...] = jnp.zeros_like(spread)

    @pl.loop(0, doubled.shape[0] // unroll)
    def _(step):
        for u in range(unroll):
            i = step * unroll + u
            spread[pl.ds(place[i], 1), :] = doubled[pl.ds(i, 1), :]


def spread_rows(place, doubled, slots):
    return pl.pallas_call(
        pack_kernel,
        out_shape=jax.ShapeDtypeStruct((slots, doubled.shape[1]), F32),
        in_specs=[SMEM, VMEM],
        out_specs=VMEM,
        compiler_params=pltpu.CompilerParams(vmem_limit_bytes=16 << 20),
        name="spread_rows",
    )(place, doubled)


def exchange_kernel(rows, spread, out, buf, arrived, sem):
    me = lax.axis_index("rows")
    lanes = spread.shape[1]
    peers = peers_of(me, rows)
    barrier = greet([{"rows": there} for _, there, _ in peers])
    even = lax.broadcasted_iota(jnp.int32, (CAP, lanes), 1) < lanes // 2

    def block(r):
        start = pl.multiple_of(r * CAP, CAP)
        low = spread[pl.ds(start, CAP), :]
        high = spread[pl.ds(pl.multiple_of(start + rows * CAP, CAP), CAP), :]
        return jnp.where(even, low, high).T.astype(BF16)

    def send(slot, there, at):
        return remote(buf.at[slot], arrived.at[at], sem.at[0, slot], sem.at[1, slot], {"rows": there})

    for slot, there, _ in peers:
        buf[slot] = block(there)
    pl.semaphore_wait(barrier, rows - 1)
    for slot, there, _ in peers:
        send(slot, there, me).start()
    out[me] = block(me)
    for slot, there, back in reversed(peers):
        send(slot, there, back).wait_recv()
        out[back] = arrived[back]
    for slot, there, _ in peers:
        send(slot, there, me).wait_send()


def exchange(spread, rows, ident):
    lanes = spread.shape[1]
    whole = (rows, lanes, CAP)
    return pl.pallas_call(
        functools.partial(exchange_kernel, rows),
        out_shape=jax.ShapeDtypeStruct(whole, BF16),
        in_specs=[VMEM],
        out_specs=VMEM,
        scratch_shapes=[
            pltpu.VMEM((rows - 1, lanes, CAP), BF16),
            pltpu.VMEM(whole, BF16),
            pltpu.SemaphoreType.DMA((2, rows - 1)),
        ],
        compiler_params=pltpu.CompilerParams(
            collective_id=ident, has_side_effects=True, vmem_limit_bytes=16 << 20
        ),
        name="exchange",
    )(spread)


def arrange_kernel(arrived, out):
    cols = out.shape[1]
    for r in range(arrived.shape[0]):
        for h in range(2):
            out[h, :, r * CAP:(r + 1) * CAP] = arrived[r, h * cols:(h + 1) * cols, :]


def arrange(arrived):
    rows, lanes, _ = arrived.shape
    return pl.pallas_call(
        arrange_kernel,
        out_shape=jax.ShapeDtypeStruct((2, lanes // 2, rows * CAP), BF16),
        in_specs=[VMEM],
        out_specs=VMEM,
        compiler_params=pltpu.CompilerParams(vmem_limit_bytes=16 << 20),
        name="arrange",
    )(arrived)


def shards(rows, slab, basis, cluster_ids, kept):
    z, near_slab = covariance(slab, basis, rows, 0, True)
    for step in range(1, ITERS):
        after, gram, before, size = covariance(near_slab, z, rows, step)

        def again(before, z, after, gram):
            return tuple(covariance(slab, new_basis(kept, before, z, False), rows, ITERS + 1 + step))

        def kept_on(before, z, after, gram):
            return after, gram

        z, gram = lax.cond(size[0, 0] < TOL * TOL, kept_on, again, before, z, after, gram)
    q = new_basis(kept, gram, z, True)
    doubled, place = project(slab, q, cluster_ids.reshape(-1, CAP), 2 * rows, ITERS)
    spread = spread_rows(place.reshape(-1), doubled, 2 * rows * CAP)
    return jnp.swapaxes(arrange(exchange(spread, rows, ITERS + 1)), 1, 2)


def solution(mesh):
    rows = mesh.shape["rows"]
    torus = Mesh(mesh.devices.reshape(rows, 2, 2), ("rows", "xl", "core"))
    placed = (P("rows", FEAT), P(FEAT, None), P("rows", None), P())
    return jax.shard_map(
        functools.partial(shards, rows), mesh=torus, in_specs=placed,
        out_specs=P("rows", None, FEAT), check_vma=False,
    )
```

```python
import functools

import jax
import jax.numpy as jnp
from jax import lax
from jax.experimental import pallas as pl
from jax.experimental.pallas import tpu as pltpu
from jax.sharding import Mesh
from jax.sharding import PartitionSpec as P

ITERS = 2
CAP = 128
SHARES = (1, 2, 2, 2, 2, 2, 1)
NS = 1
GRANT = 44
TOL = 2e-3
COARSE = 1.0
STEPS = 14
F32 = jnp.float32
BF16 = jnp.bfloat16
MESH = pl.DeviceIdType.MESH
VMEM = pl.BlockSpec(memory_space=pltpu.VMEM)
SMEM = pl.BlockSpec(memory_space=pltpu.SMEM)
HBM = pl.BlockSpec(memory_space=pltpu.HBM)
FEAT = ("xl", "core")


def nn(a, b):
    return lax.dot_general(a, b, (((1,), (0,)), ((), ())), preferred_element_type=F32)


def nt(a, b):
    return lax.dot_general(a, b, (((1,), (1,)), ((), ())), preferred_element_type=F32)


def tn(a, b):
    return lax.dot_general(a, b, (((0,), (0,)), ((), ())), preferred_element_type=F32)


def greet(targets):
    barrier = pltpu.get_barrier_semaphore()
    for target in targets:
        pl.semaphore_signal(barrier, inc=1, device_id=target, device_id_type=MESH)
    return barrier


def grid_of(rows):
    return (4, 4, 2) if rows == 32 else (2, rows // 4, 2)


def terms(me, rows):
    nz, ny, nx = grid_of(rows)
    z, y, x = me // (ny * nx), (me // nx) % ny, me % nx
    along_z = [((z + d) % nz) * (ny * nx) for d in range(nz)]
    along_y = [((y + d) % ny) * nx for d in range(ny)]
    return along_z, along_y, [(x + d) % nx for d in range(nx)]


def axis_peers(me, rows):
    az, ay, ax = terms(me, rows)
    return ([{"rows": a + ay[0] + ax[0]} for a in az[1:]] + [{"rows": az[0] + a + ax[0]} for a in ay[1:]]
            + [{"rows": az[0] + ay[0] + a} for a in ax[1:]])


def peers_of(me, rows):
    lists = terms(me, rows)

    def order(n):
        return sorted(range(n), key=lambda d: -min(d, n - d))

    found = []
    for dx in order(len(lists[2])):
        for dz in order(len(lists[0])):
            for dy in order(len(lists[1])):
                if dz or dy or dx:
                    there = lists[0][dz] + lists[1][dy] + lists[2][dx]
                    back = lists[0][-dz] + lists[1][-dy] + lists[2][-dx]
                    found.append((len(found), there, back))
    return found


def chunks_of(half):
    unit = half // sum(SHARES)
    found, start = [], 0
    for share in SHARES:
        found.append((start, share * unit))
        start += share * unit
    return found


def remote(src, dst, send, recv, target):
    return pltpu.make_async_remote_copy(
        src_ref=src, dst_ref=dst, send_sem=send, recv_sem=recv, device_id=target, device_id_type=MESH
    )


def find_places(clusters, ids, place):
    blocks = ids.shape[0]
    lane = lax.broadcasted_iota(jnp.int32, (CAP, CAP), 1)
    sub = lax.broadcasted_iota(jnp.int32, (CAP, CAP), 0)
    before = jnp.where(sub < lane, F32(1), F32(0)).astype(BF16)
    names = lax.broadcasted_iota(jnp.int32, (clusters, CAP), 0)
    seen = jnp.zeros((clusters, 1), F32)
    for b in range(blocks):
        block = ids[b:b + 1, :]
        hot = jnp.where(names == block, F32(1), F32(0))
        earlier = nn(hot.astype(BF16), before) + seen
        slot = jnp.sum(hot * earlier, axis=0, keepdims=True).astype(jnp.int32)
        pair = block // 2
        odd = block - 2 * pair
        place[b:b + 1, :] = odd * (clusters // 2 * CAP) + pair * CAP + slot
        seen = seen + jnp.sum(hot, axis=1, keepdims=True)


def covariance_kernel(rows, kind, *refs):
    first, joint = kind == "first", kind == "joint"
    if first:
        source, basis, z_out, slab, q, load_sem, *refs = refs
    elif joint:
        slab, z_in, z_out, gram_out, gram_in, size_out, unit, *refs = refs
    else:
        slab, q, z_out, gram_out, *refs = refs
    (qb, away, home, part, mine, theirs, y, z, z_send, z_recv, z_full, g_part, g_near, g_mine, g_far, g_all,
     near_sem, far_sem, y_sem, rs_sem, ag_sem, g_sem, round_a, round_b) = refs
    me, core, xl = lax.axis_index("rows"), lax.axis_index("core"), lax.axis_index("xl")
    near, far = {"core": 1 - core}, {"xl": 1 - xl}
    half_rows = slab.shape[0] // 2
    width = qb.shape[1]
    chunks = chunks_of(half_rows)
    count = len(chunks)
    deep, wide = z_send.shape[2:]
    group = rows // 2
    low = width // 2
    part_rows = low // 2
    beside = axis_peers(me, rows)
    barrier = greet([near, far] + beside)

    def rows_at(h, i):
        start, size = chunks[i]
        return pl.ds(pl.multiple_of(h * half_rows + start, 8), size)

    def load(own, i):
        at = rows_at(core if own else 1 - core, i)
        return pltpu.make_async_copy(source.at[at], slab.at[at], load_sem.at[own, i])

    if first:
        for i in range(count):
            load(0, i).start()
            load(1, i).start()
        begin = pltpu.make_async_copy(basis, q, load_sem.at[0, count])
        begin.start()
        begin.wait()

    def held(own, i):
        return slab[rows_at(core if own else 1 - core, i), :]

    def scores(own, i):
        if first:
            load(own, i).wait()
        return nn(held(own, i), qb[...])

    def at(ref, i):
        start, size = chunks[i]
        return ref.at[pl.ds(start, size)]

    def to_near(i):
        return remote(at(away, i), at(home, i), near_sem.at[0, i], near_sem.at[1, i], near)

    def to_far(i):
        return remote(at(mine, i), at(theirs, i), far_sem.at[0, i], far_sem.at[1, i], far)

    def y_at(own, i):
        return at(y.at[core if own else 1 - core], i)

    def share(i):
        return remote(y_at(1, i), y_at(1, i), y_sem.at[0, i], y_sem.at[1, i], near)

    def shared(i):
        return remote(y_at(0, i), y_at(0, i), y_sem.at[0, i], y_sem.at[1, i], near)

    def chip_sum(i):
        to_near(i).wait_recv()
        at(mine, i)[...] = (at(part, i)[...] + at(home, i)[...].astype(F32)).astype(BF16)
        to_far(i).start()

    def pass_on(sem):
        for peer in beside:
            pl.semaphore_signal(sem, inc=1, device_id=peer, device_id_type=MESH)

    def gram_terms(e, pieces, s):
        for f in range(2):
            block = pieces[s, f * group:(f + 1) * group].reshape(width, wide)
            terms_of = (nt(block[:low], block[:low]), nt(block[low:], block[:low]), nt(block[low:], block[low:]))
            for b, term in enumerate(terms_of):
                for h in range(2):
                    line = term[h * part_rows:(h + 1) * part_rows]
                    g_part[e, h, b] = line if s + f == 0 else g_part[e, h, b] + line

    def gram_copy(e, i, src, dst, target):
        return remote(src, dst, g_sem.at[0, e, i], g_sem.at[1, e, i], target)

    def gram_near(e):
        return gram_copy(e, 0, g_part.at[e, 1 - core], g_near.at[e], near)

    def gram_far(e):
        return gram_copy(e, 1, g_mine.at[e], g_far.at[e], far)

    def gram_back(e, c):
        return gram_copy(e, 2, g_all.at[e, c], g_all.at[e, c], near)

    def gram_to_far(e):
        gram_near(e).wait_recv()
        g_mine[e] = g_part[e, core] + g_near[e]
        gram_far(e).start()

    def gram_finish(e, out):
        gram_far(e).wait_recv()
        g_all[e, core] = g_mine[e] + g_far[e]
        gram_back(e, core).start()
        gram_back(e, 1 - core).wait_recv()
        for h in range(2):
            for b in range(3):
                out[b, h * part_rows:(h + 1) * part_rows, :] = g_all[e, h, b]
        gram_near(e).wait_send()
        gram_far(e).wait_send()
        gram_back(e, core).wait_send()

    if joint:
        for s in range(NS):
            gram_terms(1, z_in, s)
            for f in range(2):
                left = (f * NS + s) * wide
                qb[left:left + wide, :] = z_in[s, f * group:(f + 1) * group].reshape(width, wide).T
    else:
        qb[...] = q[...].astype(BF16)
    for i in range(count):
        at(away, i)[...] = scores(0, i).astype(BF16)
        if i == 0:
            at(part, i)[...] = scores(1, i)
            continue
        if i == 1:
            pl.semaphore_wait(barrier, len(beside) + 2)
            if joint:
                gram_near(1).start()
            to_near(0).start()
        to_near(i).start()
        at(part, i)[...] = scores(1, i)
        if joint and i == 1:
            gram_to_far(1)
        chip_sum(i - 1)
        if i == 2:
            pass_on(round_a)
    chip_sum(count - 1)
    pl.semaphore_wait(round_a, len(beside))
    pass_on(round_b)
    pl.semaphore_wait(round_b, len(beside))
    if joint:
        gram_finish(1, gram_in)
        inverse, last_size = steps_for(gram_in, unit)
        top, rest = split(inverse)
        size_out[0, 0] = last_size

    def add(own, i, start=False):
        term = tn(y_at(own, i)[...], held(own, i))
        z[...] = term if start else z[...] + term

    for i in range(count):
        to_far(i).wait_recv()
        both = (at(mine, i)[...].astype(F32) + at(theirs, i)[...].astype(F32)).astype(BF16)
        y_at(1, i)[...] = (nt(both, top) + nt(both, rest)).astype(BF16) if joint else both
        share(i).start()
        add(1, i, i == 0)
        if i > 0:
            shared(i - 1).wait_recv()
            add(0, i - 1)
    shared(count - 1).wait_recv()
    add(0, count - 1)

    peers = peers_of(me, rows)

    def scatter(s, slot, there):
        return remote(z_send.at[s, there], z_recv.at[s, slot], rs_sem.at[0, s, slot], rs_sem.at[1, s, slot],
                      {"rows": there})

    def gather(s, slot, owner, there):
        return remote(z_full.at[s, owner], z_full.at[s, owner], ag_sem.at[0, s, slot], ag_sem.at[1, s, slot],
                      {"rows": there})

    for s in range(NS):
        for p in range(rows):
            f, k = divmod(p, group)
            left = (f * NS + s) * wide
            z_send[s, p] = z[k * deep:(k + 1) * deep, left:left + wide].astype(BF16)
        for slot, there, _ in peers:
            scatter(s, slot, there).start()
    for s in range(NS):
        total = z_send[s, me].astype(F32)
        for slot, there, _ in reversed(peers):
            scatter(s, slot, there).wait_recv()
            total = total + z_recv[s, slot].astype(F32)
        z_full[s, me] = total.astype(BF16)
        for slot, there, _ in peers:
            gather(s, slot, me, there).start()

    for s in range(NS):
        for slot, there, back in reversed(peers):
            gather(s, slot, back, there).wait_recv()
        if not first:
            gram_terms(0, z_full, s)
    if not first:
        gram_near(0).start()
    z_out[...] = z_full[...]
    if not first:
        gram_to_far(0)
    for i in range(count):
        to_near(i).wait_send()
        to_far(i).wait_send()
        share(i).wait_send()
    for s in range(NS):
        for slot, there, _ in peers:
            scatter(s, slot, there).wait_send()
            gather(s, slot, me, there).wait_send()
    if not first:
        gram_finish(0, gram_out)


def covariance(slab, q, rows, ident, first=False):
    joint = q.ndim == 4
    length, feats = slab.shape
    width = q.shape[1] * q.shape[2] // 2 if joint else q.shape[1]
    half = length // 2
    count = len(SHARES)
    piece = (2 * width // rows, feats // (2 * NS))
    low = width // 2
    parts = (3, low // 2, low)
    dma = pltpu.SemaphoreType.DMA
    lower = jax.ShapeDtypeStruct((3, low, low), F32)
    out = [jax.ShapeDtypeStruct((NS, rows, *piece), BF16)] + [lower] * (not first)
    args, extra, specs = [slab, q], [], [VMEM, VMEM]
    if first:
        out.append(jax.ShapeDtypeStruct(slab.shape, BF16))
        extra = [pltpu.VMEM(q.shape, F32), dma((2, count + 1))]
        specs = [HBM, HBM]
    if joint:
        out += [lower, jax.ShapeDtypeStruct((1, 1), F32)]
        extra = [pltpu.VMEM((width, width), F32)]
    kind = "first" if first else "joint" if joint else "plain"
    grams = 1 + joint
    return pl.pallas_call(
        functools.partial(covariance_kernel, rows, kind),
        out_shape=out,
        in_specs=specs,
        out_specs=[SMEM if shape.shape == (1, 1) else VMEM for shape in out],
        scratch_shapes=extra + [
            pltpu.VMEM((feats, width), BF16),
            pltpu.VMEM((half, width), BF16),
            pltpu.VMEM((half, width), BF16),
            pltpu.VMEM((half, width), F32),
            pltpu.VMEM((half, width), BF16),
            pltpu.VMEM((half, width), BF16),
            pltpu.VMEM((2, half, width), BF16),
            pltpu.VMEM((width, feats), F32),
            pltpu.VMEM((NS, rows, *piece), BF16),
            pltpu.VMEM((NS, rows, *piece), BF16),
            pltpu.VMEM((NS, rows, *piece), BF16),
            pltpu.VMEM((grams, 2, *parts), F32),
            pltpu.VMEM((grams, *parts), F32),
            pltpu.VMEM((grams, *parts), F32),
            pltpu.VMEM((grams, *parts), F32),
            pltpu.VMEM((grams, 2, *parts), F32),
            dma((2, count)),
            dma((2, count)),
            dma((2, count)),
            dma((2, NS, rows)),
            dma((2, NS, rows)),
            dma((2, grams, 3)),
            pltpu.SemaphoreType.REGULAR,
            pltpu.SemaphoreType.REGULAR,
        ],
        compiler_params=pltpu.CompilerParams(
            collective_id=ident, has_side_effects=True, vmem_limit_bytes=(GRANT if first else 32) << 20
        ),
        name="covariance",
    )(*args)


def split(a):
    top = a.astype(BF16)
    return top, (a - top.astype(F32)).astype(BF16)


def fine(dot, a, b):
    (a0, a1), (b0, b1) = split(a), split(b)
    return dot(a0, b0) + (dot(a0, b1) + dot(a1, b0))


def masks(n):
    row = lax.broadcasted_iota(jnp.int32, (n, n), 0)
    col = lax.broadcasted_iota(jnp.int32, (n, n), 1)
    eye = jnp.where(row == col, F32(1), F32(0))
    return row, col, eye, jnp.where(row > col, F32(1), F32(0.5) * eye)


def whole_gram(gram, out):
    low = gram.shape[1]
    out[:low, :low] = gram[0]
    out[low:, :low] = gram[1]
    out[low:, low:] = gram[2]
    out[:low, low:] = gram[1].T
    return out[...]


def unit_diagonal(g, eye):
    diag = g * eye
    across = lax.rsqrt(jnp.sum(diag, axis=0, keepdims=True))
    down = lax.rsqrt(jnp.sum(diag, axis=1, keepdims=True))
    return g * across * down, across


def coarse_residual(x, unit, eye):
    near = x.astype(BF16)
    return nt(nn(near, unit.astype(BF16)).astype(BF16), near) - eye


def fine_residual(x, unit, eye):
    return fine(nt, fine(nn, x, unit), x) - eye


def improved(x, e, lower):
    return x - nn((e * lower).astype(BF16), x.astype(BF16))


def steps_for(gram, unit):
    n = unit.shape[0]
    _, _, eye, lower = masks(n)
    scaled, across = unit_diagonal(whole_gram(gram, unit), eye)
    unit[...] = scaled
    x = eye - (scaled - eye) * lower
    for step in range(5):
        e = (coarse_residual if step < 2 else fine_residual)(x, unit[...], eye)
        x = improved(x, e, lower)
    return x * across, jnp.sum(e * e)


def basis_kernel(last, kept, gram, z, q_out, unit, x, e, a, state):
    n = unit.shape[0]
    row, col, eye, lower = masks(n)
    scaled, across = unit_diagonal(whole_gram(gram, x), eye)
    unit[...] = scaled
    begin = scaled - eye
    e[...] = begin
    x[...] = eye
    state[0] = 0

    @pl.loop(0, STEPS)
    def _(step):
        @pl.when(state[0] == 0)
        def _():
            now = e[...]
            size = jnp.sum(now * now)
            better = improved(x[...], now, lower)
            x[...] = better
            done = size < TOL * TOL
            state[0] = done.astype(jnp.int32)

            @pl.when(size > COARSE * COARSE)
            def _():
                e[...] = coarse_residual(better, unit[...], eye)

            @pl.when(jnp.logical_not(done) & jnp.logical_not(size > COARSE * COARSE))
            def _():
                e[...] = fine_residual(better, unit[...], eye)

    @pl.when(state[0] == 0)
    def _():
        a[...] = unit[...]
        x[...] = eye

        @pl.loop(0, n)
        def _(j):
            pick_row = row == j
            pick_col = col == j
            now = a[...]
            inv = x[...]
            a_row = jnp.sum(jnp.where(pick_row, now, 0.0), axis=0, keepdims=True)
            a_col = jnp.sum(jnp.where(pick_col, now, 0.0), axis=1, keepdims=True)
            x_row = jnp.sum(jnp.where(pick_row, inv, 0.0), axis=0, keepdims=True)
            pivot = jnp.sum(jnp.where(pick_row & pick_col, now, 0.0))
            root = jnp.sqrt(jnp.full((1, n), pivot))
            line = x_row / root
            factor = jnp.where(row[:, :1] > j, a_col / root[:, :1], 0.0)
            x[...] = jnp.where(pick_row, line, inv - factor * line)
            a[...] = now - factor * (a_row / root)

    top, rest = split(x[...] * across)
    ns, rows, _, wide = z.shape
    group = rows // 2
    for f in range(2):
        for s in range(ns):
            block = z[s, f * group:(f + 1) * group].reshape(n, wide)
            qt = nn(top, block) + nn(rest, block)
            if last:
                index = lax.broadcasted_iota(jnp.int32, (n, wide), 0)
                qt = jnp.where(index < kept[0], qt, 0.0)
            left = (f * ns + s) * wide
            q_out[left:left + wide, :] = qt.astype(BF16).T


def new_basis(kept, gram, z, last):
    n = 2 * gram.shape[1]
    return pl.pallas_call(
        functools.partial(basis_kernel, last),
        out_shape=jax.ShapeDtypeStruct((2 * z.shape[0] * z.shape[3], n), BF16),
        in_specs=[SMEM, VMEM, VMEM],
        out_specs=VMEM,
        scratch_shapes=[pltpu.VMEM((n, n), F32)] * 4 + [pltpu.SMEM((2,), jnp.int32)],
        compiler_params=pltpu.CompilerParams(vmem_limit_bytes=24 << 20),
        name="new_basis",
    )(kept, gram, z)


def project_kernel(clusters, source, q, ids, doubled, place, slab, away, home, keep, send, recv, p, near_sem, far_sem, p_sem, load_sem):
    core, xl = lax.axis_index("core"), lax.axis_index("xl")
    near, far = {"core": 1 - core}, {"xl": 1 - xl}
    half_rows = slab.shape[0] // 2
    half = q.shape[1] // 2
    chunks = chunks_of(half_rows)
    count = len(chunks)
    barrier = greet((near, far))

    def rows_at(own, i):
        start, size = chunks[i]
        h = core if own else 1 - core
        return pl.ds(pl.multiple_of(h * half_rows + start, 8), size)

    def load(own, i):
        at = rows_at(own, i)
        return pltpu.make_async_copy(source.at[at], slab.at[at], load_sem.at[own, i])

    for i in range(count):
        load(0, i).start()
        load(1, i).start()

    def scores(own, i):
        load(own, i).wait()
        return nn(slab[rows_at(own, i), :], q[...])

    def at(ref, i):
        start, size = chunks[i]
        return ref.at[pl.ds(start, size)]

    def p_at(own, i):
        return at(p.at[core if own else 1 - core], i)

    def to_near(i):
        return remote(at(away, i), at(home, i), near_sem.at[0, i], near_sem.at[1, i], near)

    def to_far(i):
        return remote(at(send, i), at(recv, i), far_sem.at[0, i], far_sem.at[1, i], far)

    def share(i):
        return remote(p_at(1, i), p_at(1, i), p_sem.at[0, i], p_sem.at[1, i], near)

    def shared(i):
        return remote(p_at(0, i), p_at(0, i), p_sem.at[0, i], p_sem.at[1, i], near)

    def chip_sum(i, part):
        to_near(i).wait_recv()
        both = part + at(home, i)[...].astype(F32)
        low, high = both[:, :half], both[:, half:]
        at(send, i)[...] = jnp.where(xl == 0, high, low).astype(BF16)
        to_far(i).start()
        at(keep, i)[...] = jnp.where(xl == 0, low, high)

    for i in range(2):
        at(away, i)[...] = scores(0, i).astype(BF16)
    own = [scores(1, 0)]
    pl.semaphore_wait(barrier, 2)
    to_near(0).start()
    to_near(1).start()
    for i in range(count):
        if i + 2 < count:
            at(away, i + 2)[...] = scores(0, i + 2).astype(BF16)
            to_near(i + 2).start()
        if i + 1 < count:
            own.append(scores(1, i + 1))
        chip_sum(i, own[i])
    find_places(clusters, ids, place)

    def double(own, i):
        wide = p_at(own, i)[...].astype(F32)
        low = lax.broadcasted_iota(jnp.int32, wide.shape, 1) < half // 2
        turned = pltpu.roll(wide, half // 2, 1)
        doubled[rows_at(own, i), :] = jnp.where(low == (core == 0), wide, turned)

    for i in range(count):
        to_far(i).wait_recv()
        p_at(1, i)[...] = (at(keep, i)[...] + at(recv, i)[...].astype(F32)).astype(BF16)
        share(i).start()
        double(1, i)
    for i in range(count):
        to_near(i).wait_send()
        to_far(i).wait_send()
    for i in range(count):
        shared(i).wait_recv()
        double(0, i)
    for i in range(count):
        share(i).wait_send()


def project(slab, q, ids, clusters, ident):
    length = slab.shape[0]
    width = q.shape[1]
    half = width // 2
    dma = pltpu.SemaphoreType.DMA((2, len(SHARES)))
    return pl.pallas_call(
        functools.partial(project_kernel, clusters),
        out_shape=[
            jax.ShapeDtypeStruct((length, half), F32),
            jax.ShapeDtypeStruct(ids.shape, jnp.int32),
        ],
        in_specs=[HBM, VMEM, VMEM],
        out_specs=[VMEM] * 2,
        scratch_shapes=[
            pltpu.VMEM(slab.shape, BF16),
            pltpu.VMEM((length // 2, width), BF16),
            pltpu.VMEM((length // 2, width), BF16),
            pltpu.VMEM((length // 2, half), F32),
            pltpu.VMEM((length // 2, half), BF16),
            pltpu.VMEM((length // 2, half), BF16),
            pltpu.VMEM((2, length // 2, half), BF16),
            dma,
            dma,
            dma,
            dma,
        ],
        compiler_params=pltpu.CompilerParams(
            collective_id=ident, has_side_effects=True, vmem_limit_bytes=32 << 20
        ),
        name="project",
    )(slab, q, ids)


def pack_kernel(place, doubled, spread):
    unroll = 16
    spread[...] = jnp.zeros_like(spread)

    @pl.loop(0, doubled.shape[0] // unroll)
    def _(step):
        for u in range(unroll):
            i = step * unroll + u
            spread[pl.ds(place[i], 1), :] = doubled[pl.ds(i, 1), :]


def spread_rows(place, doubled, slots):
    return pl.pallas_call(
        pack_kernel,
        out_shape=jax.ShapeDtypeStruct((slots, doubled.shape[1]), F32),
        in_specs=[SMEM, VMEM],
        out_specs=VMEM,
        compiler_params=pltpu.CompilerParams(vmem_limit_bytes=16 << 20),
        name="spread_rows",
    )(place, doubled)


def exchange_kernel(rows, spread, out, buf, arrived, sem):
    me = lax.axis_index("rows")
    lanes = spread.shape[1]
    peers = peers_of(me, rows)
    barrier = greet([{"rows": there} for _, there, _ in peers])
    even = lax.broadcasted_iota(jnp.int32, (CAP, lanes), 1) < lanes // 2

    def block(r):
        start = pl.multiple_of(r * CAP, CAP)
        low = spread[pl.ds(start, CAP), :]
        high = spread[pl.ds(pl.multiple_of(start + rows * CAP, CAP), CAP), :]
        return jnp.where(even, low, high).astype(BF16).T

    def send(slot, there, at):
        return remote(buf.at[slot], arrived.at[at], sem.at[0, slot], sem.at[1, slot], {"rows": there})

    for slot, there, _ in peers:
        buf[slot] = block(there)
    pl.semaphore_wait(barrier, rows - 1)
    for slot, there, _ in peers:
        send(slot, there, me).start()
    out[me] = block(me)
    for slot, there, back in reversed(peers):
        send(slot, there, back).wait_recv()
        out[back] = arrived[back]
    for slot, there, _ in peers:
        send(slot, there, me).wait_send()


def exchange(spread, rows, ident):
    lanes = spread.shape[1]
    whole = (rows, lanes, CAP)
    return pl.pallas_call(
        functools.partial(exchange_kernel, rows),
        out_shape=jax.ShapeDtypeStruct(whole, BF16),
        in_specs=[VMEM],
        out_specs=VMEM,
        scratch_shapes=[
            pltpu.VMEM((rows - 1, lanes, CAP), BF16),
            pltpu.VMEM(whole, BF16),
            pltpu.SemaphoreType.DMA((2, rows - 1)),
        ],
        compiler_params=pltpu.CompilerParams(
            collective_id=ident, has_side_effects=True, vmem_limit_bytes=16 << 20
        ),
        name="exchange",
    )(spread)


def arrange_kernel(arrived, out):
    cols = out.shape[1]
    for r in range(arrived.shape[0]):
        for h in range(2):
            out[h, :, r * CAP:(r + 1) * CAP] = arrived[r, h * cols:(h + 1) * cols, :]


def arrange(arrived):
    rows, lanes, _ = arrived.shape
    return pl.pallas_call(
        arrange_kernel,
        out_shape=jax.ShapeDtypeStruct((2, lanes // 2, rows * CAP), BF16),
        in_specs=[VMEM],
        out_specs=VMEM,
        compiler_params=pltpu.CompilerParams(vmem_limit_bytes=16 << 20),
        name="arrange",
    )(arrived)


def shards(rows, slab, basis, cluster_ids, kept):
    z, near_slab = covariance(slab, basis, rows, 0, True)
    for step in range(1, ITERS):
        after, gram, before, size = covariance(near_slab, z, rows, step)

        def again(before, z, after, gram):
            return tuple(covariance(slab, new_basis(kept, before, z, False), rows, ITERS + 1 + step))

        def kept_on(before, z, after, gram):
            return after, gram

        z, gram = lax.cond(size[0, 0] < TOL * TOL, kept_on, again, before, z, after, gram)
    q = new_basis(kept, gram, z, True)
    doubled, place = project(slab, q, cluster_ids.reshape(-1, CAP), 2 * rows, ITERS)
    spread = spread_rows(place.reshape(-1), doubled, 2 * rows * CAP)
    return jnp.swapaxes(arrange(exchange(spread, rows, ITERS + 1)), 1, 2)


def solution(mesh):
    rows = mesh.shape["rows"]
    torus = Mesh(mesh.devices.reshape(rows, 2, 2), ("rows", "xl", "core"))
    placed = (P("rows", FEAT), P(FEAT, None), P("rows", None), P())
    return jax.shard_map(
        functools.partial(shards, rows), mesh=torus, in_specs=placed,
        out_specs=P("rows", None, FEAT), check_vma=False,
    )
```

```python
import functools

import jax
import jax.numpy as jnp
from jax import lax
from jax.experimental import pallas as pl
from jax.experimental.pallas import tpu as pltpu
from jax.sharding import Mesh
from jax.sharding import PartitionSpec as P

ITERS = 2
CAP = 128
SHARES = (1, 2, 2, 2, 2, 2, 1)
NS = 1
GRANT = 44
TOL = 4e-3
COARSE = 0.5
STEPS = 14
F32 = jnp.float32
BF16 = jnp.bfloat16
MESH = pl.DeviceIdType.MESH
VMEM = pl.BlockSpec(memory_space=pltpu.VMEM)
SMEM = pl.BlockSpec(memory_space=pltpu.SMEM)
HBM = pl.BlockSpec(memory_space=pltpu.HBM)
FEAT = ("xl", "core")


def nn(a, b):
    return lax.dot_general(a, b, (((1,), (0,)), ((), ())), preferred_element_type=F32)


def nt(a, b):
    return lax.dot_general(a, b, (((1,), (1,)), ((), ())), preferred_element_type=F32)


def tn(a, b):
    return lax.dot_general(a, b, (((0,), (0,)), ((), ())), preferred_element_type=F32)


def greet(targets):
    barrier = pltpu.get_barrier_semaphore()
    for target in targets:
        pl.semaphore_signal(barrier, inc=1, device_id=target, device_id_type=MESH)
    return barrier


def grid_of(rows):
    return (4, 4, 2) if rows == 32 else (2, rows // 4, 2)


def terms(me, rows):
    nz, ny, nx = grid_of(rows)
    z, y, x = me // (ny * nx), (me // nx) % ny, me % nx
    along_z = [((z + d) % nz) * (ny * nx) for d in range(nz)]
    along_y = [((y + d) % ny) * nx for d in range(ny)]
    return along_z, along_y, [(x + d) % nx for d in range(nx)]


def axis_peers(me, rows):
    az, ay, ax = terms(me, rows)
    return ([{"rows": a + ay[0] + ax[0]} for a in az[1:]] + [{"rows": az[0] + a + ax[0]} for a in ay[1:]]
            + [{"rows": az[0] + ay[0] + a} for a in ax[1:]])


def peers_of(me, rows):
    lists = terms(me, rows)

    def order(n):
        return sorted(range(n), key=lambda d: -min(d, n - d))

    found = []
    for dx in order(len(lists[2])):
        for dz in order(len(lists[0])):
            for dy in order(len(lists[1])):
                if dz or dy or dx:
                    there = lists[0][dz] + lists[1][dy] + lists[2][dx]
                    back = lists[0][-dz] + lists[1][-dy] + lists[2][-dx]
                    found.append((len(found), there, back))
    return found


def chunks_of(half):
    unit = half // sum(SHARES)
    found, start = [], 0
    for share in SHARES:
        found.append((start, share * unit))
        start += share * unit
    return found


def remote(src, dst, send, recv, target):
    return pltpu.make_async_remote_copy(
        src_ref=src, dst_ref=dst, send_sem=send, recv_sem=recv, device_id=target, device_id_type=MESH
    )


def find_places(clusters, ids, place):
    blocks = ids.shape[0]
    lane = lax.broadcasted_iota(jnp.int32, (CAP, CAP), 1)
    sub = lax.broadcasted_iota(jnp.int32, (CAP, CAP), 0)
    before = jnp.where(sub < lane, F32(1), F32(0)).astype(BF16)
    names = lax.broadcasted_iota(jnp.int32, (clusters, CAP), 0)
    seen = jnp.zeros((clusters, 1), F32)
    for b in range(blocks):
        block = ids[b:b + 1, :]
        hot = jnp.where(names == block, F32(1), F32(0))
        earlier = nn(hot.astype(BF16), before) + seen
        slot = jnp.sum(hot * earlier, axis=0, keepdims=True).astype(jnp.int32)
        pair = block // 2
        odd = block - 2 * pair
        place[b:b + 1, :] = odd * (clusters // 2 * CAP) + pair * CAP + slot
        seen = seen + jnp.sum(hot, axis=1, keepdims=True)


def covariance_kernel(rows, kind, *refs):
    first, joint = kind == "first", kind == "joint"
    if first:
        source, basis, z_out, slab, q, load_sem, *refs = refs
    elif joint:
        slab, z_in, z_out, gram_out, gram_in, size_out, unit, *refs = refs
    else:
        slab, q, z_out, gram_out, *refs = refs
    (qb, away, home, part, mine, theirs, y, z, z_send, z_recv, z_full, g_part, g_near, g_mine, g_far, g_all,
     near_sem, far_sem, y_sem, rs_sem, ag_sem, g_sem, round_a, round_b) = refs
    me, core, xl = lax.axis_index("rows"), lax.axis_index("core"), lax.axis_index("xl")
    near, far = {"core": 1 - core}, {"xl": 1 - xl}
    half_rows = slab.shape[0] // 2
    width = qb.shape[1]
    chunks = chunks_of(half_rows)
    count = len(chunks)
    deep, wide = z_send.shape[2:]
    group = rows // 2
    low = width // 2
    part_rows = low // 2
    beside = axis_peers(me, rows)
    barrier = greet([near, far] + beside)

    def rows_at(h, i):
        start, size = chunks[i]
        return pl.ds(pl.multiple_of(h * half_rows + start, 8), size)

    def load(own, i):
        at = rows_at(core if own else 1 - core, i)
        return pltpu.make_async_copy(source.at[at], slab.at[at], load_sem.at[own, i])

    if first:
        for i in range(count):
            load(0, i).start()
            load(1, i).start()
        begin = pltpu.make_async_copy(basis, q, load_sem.at[0, count])
        begin.start()
        begin.wait()

    def held(own, i):
        return slab[rows_at(core if own else 1 - core, i), :]

    def scores(own, i):
        if first:
            load(own, i).wait()
        return nn(held(own, i), qb[...])

    def at(ref, i):
        start, size = chunks[i]
        return ref.at[pl.ds(start, size)]

    def to_near(i):
        return remote(at(away, i), at(home, i), near_sem.at[0, i], near_sem.at[1, i], near)

    def to_far(i):
        return remote(at(mine, i), at(theirs, i), far_sem.at[0, i], far_sem.at[1, i], far)

    def y_at(own, i):
        return at(y.at[core if own else 1 - core], i)

    def share(i):
        return remote(y_at(1, i), y_at(1, i), y_sem.at[0, i], y_sem.at[1, i], near)

    def shared(i):
        return remote(y_at(0, i), y_at(0, i), y_sem.at[0, i], y_sem.at[1, i], near)

    def chip_sum(i):
        to_near(i).wait_recv()
        at(mine, i)[...] = (at(part, i)[...] + at(home, i)[...].astype(F32)).astype(BF16)
        to_far(i).start()

    def pass_on(sem):
        for peer in beside:
            pl.semaphore_signal(sem, inc=1, device_id=peer, device_id_type=MESH)

    def gram_terms(e, pieces, s):
        for f in range(2):
            block = pieces[s, f * group:(f + 1) * group].reshape(width, wide)
            terms_of = (nt(block[:low], block[:low]), nt(block[low:], block[:low]), nt(block[low:], block[low:]))
            for b, term in enumerate(terms_of):
                for h in range(2):
                    line = term[h * part_rows:(h + 1) * part_rows]
                    g_part[e, h, b] = line if s + f == 0 else g_part[e, h, b] + line

    def gram_copy(e, i, src, dst, target):
        return remote(src, dst, g_sem.at[0, e, i], g_sem.at[1, e, i], target)

    def gram_near(e):
        return gram_copy(e, 0, g_part.at[e, 1 - core], g_near.at[e], near)

    def gram_far(e):
        return gram_copy(e, 1, g_mine.at[e], g_far.at[e], far)

    def gram_back(e, c):
        return gram_copy(e, 2, g_all.at[e, c], g_all.at[e, c], near)

    def gram_to_far(e):
        gram_near(e).wait_recv()
        g_mine[e] = g_part[e, core] + g_near[e]
        gram_far(e).start()

    def gram_finish(e, out):
        gram_far(e).wait_recv()
        g_all[e, core] = g_mine[e] + g_far[e]
        gram_back(e, core).start()
        gram_back(e, 1 - core).wait_recv()
        for h in range(2):
            for b in range(3):
                out[b, h * part_rows:(h + 1) * part_rows, :] = g_all[e, h, b]
        gram_near(e).wait_send()
        gram_far(e).wait_send()
        gram_back(e, core).wait_send()

    if joint:
        for s in range(NS):
            gram_terms(1, z_in, s)
            for f in range(2):
                left = (f * NS + s) * wide
                qb[left:left + wide, :] = z_in[s, f * group:(f + 1) * group].reshape(width, wide).T
    else:
        qb[...] = q[...].astype(BF16)
    for i in range(count):
        at(away, i)[...] = scores(0, i).astype(BF16)
        if i == 0:
            at(part, i)[...] = scores(1, i)
            continue
        if i == 1:
            pl.semaphore_wait(barrier, len(beside) + 2)
            if joint:
                gram_near(1).start()
            to_near(0).start()
        to_near(i).start()
        at(part, i)[...] = scores(1, i)
        if joint and i == 1:
            gram_to_far(1)
        chip_sum(i - 1)
        if i == 2:
            pass_on(round_a)
    chip_sum(count - 1)
    pl.semaphore_wait(round_a, len(beside))
    pass_on(round_b)
    pl.semaphore_wait(round_b, len(beside))
    if joint:
        gram_finish(1, gram_in)
        inverse, last_size = steps_for(gram_in, unit)
        top, rest = split(inverse)
        size_out[0, 0] = last_size

    def add(own, i, start=False):
        term = tn(y_at(own, i)[...], held(own, i))
        z[...] = term if start else z[...] + term

    for i in range(count):
        to_far(i).wait_recv()
        both = (at(mine, i)[...].astype(F32) + at(theirs, i)[...].astype(F32)).astype(BF16)
        y_at(1, i)[...] = (nt(both, top) + nt(both, rest)).astype(BF16) if joint else both
        share(i).start()
        add(1, i, i == 0)
        if i > 0:
            shared(i - 1).wait_recv()
            add(0, i - 1)
    shared(count - 1).wait_recv()
    add(0, count - 1)

    peers = peers_of(me, rows)

    def scatter(s, slot, there):
        return remote(z_send.at[s, there], z_recv.at[s, slot], rs_sem.at[0, s, slot], rs_sem.at[1, s, slot],
                      {"rows": there})

    def gather(s, slot, owner, there):
        return remote(z_full.at[s, owner], z_full.at[s, owner], ag_sem.at[0, s, slot], ag_sem.at[1, s, slot],
                      {"rows": there})

    for s in range(NS):
        for p in range(rows):
            f, k = divmod(p, group)
            left = (f * NS + s) * wide
            z_send[s, p] = z[k * deep:(k + 1) * deep, left:left + wide].astype(BF16)
        for slot, there, _ in peers:
            scatter(s, slot, there).start()
    for s in range(NS):
        total = z_send[s, me].astype(F32)
        for slot, there, _ in reversed(peers):
            scatter(s, slot, there).wait_recv()
            total = total + z_recv[s, slot].astype(F32)
        z_full[s, me] = total.astype(BF16)
        for slot, there, _ in peers:
            gather(s, slot, me, there).start()

    for s in range(NS):
        for slot, there, back in reversed(peers):
            gather(s, slot, back, there).wait_recv()
        if not first:
            gram_terms(0, z_full, s)
    if not first:
        gram_near(0).start()
    z_out[...] = z_full[...]
    if not first:
        gram_to_far(0)
    for i in range(count):
        to_near(i).wait_send()
        to_far(i).wait_send()
        share(i).wait_send()
    for s in range(NS):
        for slot, there, _ in peers:
            scatter(s, slot, there).wait_send()
            gather(s, slot, me, there).wait_send()
    if not first:
        gram_finish(0, gram_out)


def covariance(slab, q, rows, ident, first=False):
    joint = q.ndim == 4
    length, feats = slab.shape
    width = q.shape[1] * q.shape[2] // 2 if joint else q.shape[1]
    half = length // 2
    count = len(SHARES)
    piece = (2 * width // rows, feats // (2 * NS))
    low = width // 2
    parts = (3, low // 2, low)
    dma = pltpu.SemaphoreType.DMA
    lower = jax.ShapeDtypeStruct((3, low, low), F32)
    out = [jax.ShapeDtypeStruct((NS, rows, *piece), BF16)] + [lower] * (not first)
    args, extra, specs = [slab, q], [], [VMEM, VMEM]
    if first:
        out.append(jax.ShapeDtypeStruct(slab.shape, BF16))
        extra = [pltpu.VMEM(q.shape, F32), dma((2, count + 1))]
        specs = [HBM, HBM]
    if joint:
        out += [lower, jax.ShapeDtypeStruct((1, 1), F32)]
        extra = [pltpu.VMEM((width, width), F32)]
    kind = "first" if first else "joint" if joint else "plain"
    grams = 1 + joint
    return pl.pallas_call(
        functools.partial(covariance_kernel, rows, kind),
        out_shape=out,
        in_specs=specs,
        out_specs=[SMEM if shape.shape == (1, 1) else VMEM for shape in out],
        scratch_shapes=extra + [
            pltpu.VMEM((feats, width), BF16),
            pltpu.VMEM((half, width), BF16),
            pltpu.VMEM((half, width), BF16),
            pltpu.VMEM((half, width), F32),
            pltpu.VMEM((half, width), BF16),
            pltpu.VMEM((half, width), BF16),
            pltpu.VMEM((2, half, width), BF16),
            pltpu.VMEM((width, feats), F32),
            pltpu.VMEM((NS, rows, *piece), BF16),
            pltpu.VMEM((NS, rows, *piece), BF16),
            pltpu.VMEM((NS, rows, *piece), BF16),
            pltpu.VMEM((grams, 2, *parts), F32),
            pltpu.VMEM((grams, *parts), F32),
            pltpu.VMEM((grams, *parts), F32),
            pltpu.VMEM((grams, *parts), F32),
            pltpu.VMEM((grams, 2, *parts), F32),
            dma((2, count)),
            dma((2, count)),
            dma((2, count)),
            dma((2, NS, rows)),
            dma((2, NS, rows)),
            dma((2, grams, 3)),
            pltpu.SemaphoreType.REGULAR,
            pltpu.SemaphoreType.REGULAR,
        ],
        compiler_params=pltpu.CompilerParams(
            collective_id=ident, has_side_effects=True, vmem_limit_bytes=(GRANT if first else 32) << 20
        ),
        name="covariance",
    )(*args)


def split(a):
    top = a.astype(BF16)
    return top, (a - top.astype(F32)).astype(BF16)


def fine(dot, a, b):
    (a0, a1), (b0, b1) = split(a), split(b)
    return dot(a0, b0) + (dot(a0, b1) + dot(a1, b0))


def masks(n):
    row = lax.broadcasted_iota(jnp.int32, (n, n), 0)
    col = lax.broadcasted_iota(jnp.int32, (n, n), 1)
    eye = jnp.where(row == col, F32(1), F32(0))
    return row, col, eye, jnp.where(row > col, F32(1), F32(0.5) * eye)


def whole_gram(gram, out):
    low = gram.shape[1]
    out[:low, :low] = gram[0]
    out[low:, :low] = gram[1]
    out[low:, low:] = gram[2]
    out[:low, low:] = gram[1].T
    return out[...]


def unit_diagonal(g, eye):
    diag = g * eye
    across = lax.rsqrt(jnp.sum(diag, axis=0, keepdims=True))
    down = lax.rsqrt(jnp.sum(diag, axis=1, keepdims=True))
    return g * across * down, across


def coarse_residual(x, unit, eye):
    near = x.astype(BF16)
    return nt(nn(near, unit.astype(BF16)).astype(BF16), near) - eye


def fine_residual(x, unit, eye):
    return fine(nt, fine(nn, x, unit), x) - eye


def improved(x, e, lower):
    return x - nn((e * lower).astype(BF16), x.astype(BF16))


def steps_for(gram, unit):
    n = unit.shape[0]
    _, _, eye, lower = masks(n)
    scaled, across = unit_diagonal(whole_gram(gram, unit), eye)
    unit[...] = scaled
    x = eye - (scaled - eye) * lower
    for step in range(5):
        e = (coarse_residual if step < 2 else fine_residual)(x, unit[...], eye)
        x = improved(x, e, lower)
    return x * across, jnp.sum(e * e)


def basis_kernel(last, kept, gram, z, q_out, unit, x, e, a, state):
    n = unit.shape[0]
    row, col, eye, lower = masks(n)
    scaled, across = unit_diagonal(whole_gram(gram, x), eye)
    unit[...] = scaled
    begin = scaled - eye
    e[...] = begin
    x[...] = eye
    state[0] = 0

    @pl.loop(0, STEPS)
    def _(step):
        @pl.when(state[0] == 0)
        def _():
            now = e[...]
            size = jnp.sum(now * now)
            better = improved(x[...], now, lower)
            x[...] = better
            done = size < TOL * TOL
            state[0] = done.astype(jnp.int32)

            @pl.when(size > COARSE * COARSE)
            def _():
                e[...] = coarse_residual(better, unit[...], eye)

            @pl.when(jnp.logical_not(done) & jnp.logical_not(size > COARSE * COARSE))
            def _():
                e[...] = fine_residual(better, unit[...], eye)

    @pl.when(state[0] == 0)
    def _():
        a[...] = unit[...]
        x[...] = eye

        @pl.loop(0, n)
        def _(j):
            pick_row = row == j
            pick_col = col == j
            now = a[...]
            inv = x[...]
            a_row = jnp.sum(jnp.where(pick_row, now, 0.0), axis=0, keepdims=True)
            a_col = jnp.sum(jnp.where(pick_col, now, 0.0), axis=1, keepdims=True)
            x_row = jnp.sum(jnp.where(pick_row, inv, 0.0), axis=0, keepdims=True)
            pivot = jnp.sum(jnp.where(pick_row & pick_col, now, 0.0))
            root = jnp.sqrt(jnp.full((1, n), pivot))
            line = x_row / root
            factor = jnp.where(row[:, :1] > j, a_col / root[:, :1], 0.0)
            x[...] = jnp.where(pick_row, line, inv - factor * line)
            a[...] = now - factor * (a_row / root)

    top, rest = split(x[...] * across)
    ns, rows, _, wide = z.shape
    group = rows // 2
    for f in range(2):
        for s in range(ns):
            block = z[s, f * group:(f + 1) * group].reshape(n, wide)
            qt = nn(top, block) + nn(rest, block)
            if last:
                index = lax.broadcasted_iota(jnp.int32, (n, wide), 0)
                qt = jnp.where(index < kept[0], qt, 0.0)
            left = (f * ns + s) * wide
            q_out[left:left + wide, :] = qt.astype(BF16).T


def new_basis(kept, gram, z, last):
    n = 2 * gram.shape[1]
    return pl.pallas_call(
        functools.partial(basis_kernel, last),
        out_shape=jax.ShapeDtypeStruct((2 * z.shape[0] * z.shape[3], n), BF16),
        in_specs=[SMEM, VMEM, VMEM],
        out_specs=VMEM,
        scratch_shapes=[pltpu.VMEM((n, n), F32)] * 4 + [pltpu.SMEM((2,), jnp.int32)],
        compiler_params=pltpu.CompilerParams(vmem_limit_bytes=24 << 20),
        name="new_basis",
    )(kept, gram, z)


def project_kernel(clusters, source, q, ids, doubled, place, slab, away, home, keep, send, recv, p, near_sem, far_sem, p_sem, load_sem):
    core, xl = lax.axis_index("core"), lax.axis_index("xl")
    near, far = {"core": 1 - core}, {"xl": 1 - xl}
    half_rows = slab.shape[0] // 2
    half = q.shape[1] // 2
    chunks = chunks_of(half_rows)
    count = len(chunks)
    barrier = greet((near, far))

    def rows_at(own, i):
        start, size = chunks[i]
        h = core if own else 1 - core
        return pl.ds(pl.multiple_of(h * half_rows + start, 8), size)

    def load(own, i):
        at = rows_at(own, i)
        return pltpu.make_async_copy(source.at[at], slab.at[at], load_sem.at[own, i])

    for i in range(count):
        load(0, i).start()
        load(1, i).start()

    def scores(own, i):
        load(own, i).wait()
        return nn(slab[rows_at(own, i), :], q[...])

    def at(ref, i):
        start, size = chunks[i]
        return ref.at[pl.ds(start, size)]

    def p_at(own, i):
        return at(p.at[core if own else 1 - core], i)

    def to_near(i):
        return remote(at(away, i), at(home, i), near_sem.at[0, i], near_sem.at[1, i], near)

    def to_far(i):
        return remote(at(send, i), at(recv, i), far_sem.at[0, i], far_sem.at[1, i], far)

    def share(i):
        return remote(p_at(1, i), p_at(1, i), p_sem.at[0, i], p_sem.at[1, i], near)

    def shared(i):
        return remote(p_at(0, i), p_at(0, i), p_sem.at[0, i], p_sem.at[1, i], near)

    def chip_sum(i, part):
        to_near(i).wait_recv()
        both = part + at(home, i)[...].astype(F32)
        low, high = both[:, :half], both[:, half:]
        at(send, i)[...] = jnp.where(xl == 0, high, low).astype(BF16)
        to_far(i).start()
        at(keep, i)[...] = jnp.where(xl == 0, low, high)

    for i in range(2):
        at(away, i)[...] = scores(0, i).astype(BF16)
    own = [scores(1, 0)]
    pl.semaphore_wait(barrier, 2)
    to_near(0).start()
    to_near(1).start()
    for i in range(count):
        if i + 2 < count:
            at(away, i + 2)[...] = scores(0, i + 2).astype(BF16)
            to_near(i + 2).start()
        if i + 1 < count:
            own.append(scores(1, i + 1))
        chip_sum(i, own[i])
    find_places(clusters, ids, place)

    def double(own, i):
        wide = p_at(own, i)[...].astype(F32)
        low = lax.broadcasted_iota(jnp.int32, wide.shape, 1) < half // 2
        turned = pltpu.roll(wide, half // 2, 1)
        doubled[rows_at(own, i), :] = jnp.where(low == (core == 0), wide, turned)

    for i in range(count):
        to_far(i).wait_recv()
        p_at(1, i)[...] = (at(keep, i)[...] + at(recv, i)[...].astype(F32)).astype(BF16)
        share(i).start()
        double(1, i)
    for i in range(count):
        to_near(i).wait_send()
        to_far(i).wait_send()
    for i in range(count):
        shared(i).wait_recv()
        double(0, i)
    for i in range(count):
        share(i).wait_send()


def project(slab, q, ids, clusters, ident):
    length = slab.shape[0]
    width = q.shape[1]
    half = width // 2
    dma = pltpu.SemaphoreType.DMA((2, len(SHARES)))
    return pl.pallas_call(
        functools.partial(project_kernel, clusters),
        out_shape=[
            jax.ShapeDtypeStruct((length, half), F32),
            jax.ShapeDtypeStruct(ids.shape, jnp.int32),
        ],
        in_specs=[HBM, VMEM, VMEM],
        out_specs=[VMEM] * 2,
        scratch_shapes=[
            pltpu.VMEM(slab.shape, BF16),
            pltpu.VMEM((length // 2, width), BF16),
            pltpu.VMEM((length // 2, width), BF16),
            pltpu.VMEM((length // 2, half), F32),
            pltpu.VMEM((length // 2, half), BF16),
            pltpu.VMEM((length // 2, half), BF16),
            pltpu.VMEM((2, length // 2, half), BF16),
            dma,
            dma,
            dma,
            dma,
        ],
        compiler_params=pltpu.CompilerParams(
            collective_id=ident, has_side_effects=True, vmem_limit_bytes=32 << 20
        ),
        name="project",
    )(slab, q, ids)


def pack_kernel(place, doubled, spread):
    unroll = 16
    spread[...] = jnp.zeros_like(spread)

    @pl.loop(0, doubled.shape[0] // unroll)
    def _(step):
        for u in range(unroll):
            i = step * unroll + u
            spread[pl.ds(place[i], 1), :] = doubled[pl.ds(i, 1), :]


def spread_rows(place, doubled, slots):
    return pl.pallas_call(
        pack_kernel,
        out_shape=jax.ShapeDtypeStruct((slots, doubled.shape[1]), F32),
        in_specs=[SMEM, VMEM],
        out_specs=VMEM,
        compiler_params=pltpu.CompilerParams(vmem_limit_bytes=16 << 20),
        name="spread_rows",
    )(place, doubled)


def exchange_kernel(rows, spread, out, buf, arrived, sem):
    me = lax.axis_index("rows")
    lanes = spread.shape[1]
    peers = peers_of(me, rows)
    barrier = greet([{"rows": there} for _, there, _ in peers])
    even = lax.broadcasted_iota(jnp.int32, (CAP, lanes), 1) < lanes // 2

    def block(r):
        start = pl.multiple_of(r * CAP, CAP)
        low = spread[pl.ds(start, CAP), :]
        high = spread[pl.ds(pl.multiple_of(start + rows * CAP, CAP), CAP), :]
        return jnp.where(even, low, high).astype(BF16).T

    def send(slot, there, at):
        return remote(buf.at[slot], arrived.at[at], sem.at[0, slot], sem.at[1, slot], {"rows": there})

    for slot, there, _ in peers:
        buf[slot] = block(there)
    pl.semaphore_wait(barrier, rows - 1)
    for slot, there, _ in peers:
        send(slot, there, me).start()
    out[me] = block(me)
    for slot, there, back in reversed(peers):
        send(slot, there, back).wait_recv()
        out[back] = arrived[back]
    for slot, there, _ in peers:
        send(slot, there, me).wait_send()


def exchange(spread, rows, ident):
    lanes = spread.shape[1]
    whole = (rows, lanes, CAP)
    return pl.pallas_call(
        functools.partial(exchange_kernel, rows),
        out_shape=jax.ShapeDtypeStruct(whole, BF16),
        in_specs=[VMEM],
        out_specs=VMEM,
        scratch_shapes=[
            pltpu.VMEM((rows - 1, lanes, CAP), BF16),
            pltpu.VMEM(whole, BF16),
            pltpu.SemaphoreType.DMA((2, rows - 1)),
        ],
        compiler_params=pltpu.CompilerParams(
            collective_id=ident, has_side_effects=True, vmem_limit_bytes=16 << 20
        ),
        name="exchange",
    )(spread)


def arrange_kernel(arrived, out):
    cols = out.shape[1]
    for r in range(arrived.shape[0]):
        for h in range(2):
            out[h, :, r * CAP:(r + 1) * CAP] = arrived[r, h * cols:(h + 1) * cols, :]


def arrange(arrived):
    rows, lanes, _ = arrived.shape
    return pl.pallas_call(
        arrange_kernel,
        out_shape=jax.ShapeDtypeStruct((2, lanes // 2, rows * CAP), BF16),
        in_specs=[VMEM],
        out_specs=VMEM,
        compiler_params=pltpu.CompilerParams(vmem_limit_bytes=16 << 20),
        name="arrange",
    )(arrived)


def shards(rows, slab, basis, cluster_ids, kept):
    z, near_slab = covariance(slab, basis, rows, 0, True)
    for step in range(1, ITERS):
        after, gram, before, size = covariance(near_slab, z, rows, step)

        def again(before, z, after, gram):
            return tuple(covariance(slab, new_basis(kept, before, z, False), rows, ITERS + 1 + step))

        def kept_on(before, z, after, gram):
            return after, gram

        z, gram = lax.cond(size[0, 0] < TOL * TOL, kept_on, again, before, z, after, gram)
    q = new_basis(kept, gram, z, True)
    doubled, place = project(slab, q, cluster_ids.reshape(-1, CAP), 2 * rows, ITERS)
    spread = spread_rows(place.reshape(-1), doubled, 2 * rows * CAP)
    return jnp.swapaxes(arrange(exchange(spread, rows, ITERS + 1)), 1, 2)


def solution(mesh):
    rows = mesh.shape["rows"]
    torus = Mesh(mesh.devices.reshape(rows, 2, 2), ("rows", "xl", "core"))
    placed = (P("rows", FEAT), P(FEAT, None), P("rows", None), P())
    return jax.shard_map(
        functools.partial(shards, rows), mesh=torus, in_specs=placed,
        out_specs=P("rows", None, FEAT), check_vma=False,
    )
```
